32 devices in a mesh: frames: 16 (over z, y, core), text: 2 (over x).
Axes of the slice: x: 2, y: 2, z: 4, core: 2. Of those that a mesh axis runs over, the one named last changes fastest.
Arguments:
- frames_in: bfloat16 [32768, 768], P(('frames', 'text')), may hold values from -6 to 6
- frame_item: int32 [32, 1024], P('frames'), may hold values from 0 to 3, never falling along the last dimension, each value on 1 to 512 neighbouring positions
- text_in: bfloat16 [128, 256, 768], P('frames', 'text'), may hold values from -6 to 6
- text_len: int32 [128], P('frames'), may hold values from 77 to 256
- time_embed: bfloat16 [128, 768], P(('frames', 'text')), may hold values from -6 to 6
- cotangent: bfloat16 [32768, 768], P(('frames', 'text')), may hold values from -6 to 6
- w_mod: bfloat16 [768, 6144], replicated, may hold values from -0.21875 to 0.21875
- b_mod: bfloat16 [6144], replicated, may hold values from -1.75 to 1.75
- w_qkv: bfloat16 [768, 2304], replicated, may hold values from -0.21875 to 0.21875
- w_out: bfloat16 [768, 768], replicated, may hold values from -0.625 to 0.625
- b_out: bfloat16 [768], replicated, may hold values from -1.75 to 1.75
- w_q_cross: bfloat16 [768, 768], replicated, may hold values from -0.21875 to 0.21875
- w_kv_cross: bfloat16 [768, 1536], replicated, may hold values from -0.21875 to 0.21875
- w_out_cross: bfloat16 [768, 768], replicated, may hold values from -0.625 to 0.625
- b_out_cross: bfloat16 [768], replicated, may hold values from -1.75 to 1.75
- w_up: bfloat16 [768, 3072], replicated, may hold values from -0.21875 to 0.21875
- b_up: bfloat16 [3072], replicated, may hold values from -1.75 to 1.75
- w_down: bfloat16 [3072, 768], replicated, may hold values from -0.109375 to 0.109375
- b_down: bfloat16 [768], replicated, may hold values from -1.75 to 1.75
Outputs:
- frames_out: float32 [32768, 768], P(('frames', 'text'))
- frames_grad: float32 [32768, 768], P(('frames', 'text'))
- text_grad: float32 [128, 256, 768], P('frames', 'text')
- time_grad: float32 [128, 768], P(('frames', 'text'))
- grad_w_mod: float32 [768, 6144], P('frames')
- grad_b_mod: float32 [6144], P('frames')
- grad_w_qkv: float32 [768, 2304], P('frames')
- grad_w_out: float32 [768, 768], P('frames')
- grad_b_out: float32 [768], P('frames')
- grad_w_q_cross: float32 [768, 768], P('frames')
- grad_w_kv_cross: float32 [768, 1536], P('frames')
- grad_w_out_cross: float32 [768, 768], P('frames')
- grad_b_out_cross: float32 [768], P('frames')
- grad_w_up: float32 [768, 3072], P('frames')
- grad_b_up: float32 [3072], P('frames')
- grad_w_down: float32 [3072, 768], P('frames')
- grad_b_down: float32 [768], P('frames')
The draws below stay inside these ranges and needn't reach their ends.
Inputs may be any that keep to these rules, and one draw needn't show every extreme that they name: `frame_item`: in each row of 1024 frames the item numbers never fall; each of the 4 items holds 1 to 512 frames, one exactly 512.
All inputs are finite; a program needn't handle non-finite values.
Results may differ from the reference program's by a relative error of at most 0.03.
Values may be sent and summed in bfloat16 or wider, within the bound.
A program may use at most 384 MiB of HBM per device.

```python
import math
import jax
import jax.numpy as jnp
import numpy as np
from jax import lax

D = 768
HEADS = 12
HEAD_DIM = 64
FF = 3072
TD = 768
TXT = 256
TOK_DEV = 1024
ITEMS_DEV = 4
BLOCKS = 32
FRAMES = 32768
ITEMS = 128
N_TEXT = 2


def set_ends(values, key, least, largest):
    longest = values.shape.index(max(values.shape))
    spots = []
    for shift in (0, 1):
        where = [jax.random.randint(jax.random.fold_in(key, axis), (), 0, length) for axis, length in enumerate(values.shape)]
        where[longest] = (where[longest] + shift) % values.shape[longest]
        spots.append(tuple(where))
    return values.at[spots[0]].set(least).at[spots[1]].set(largest)


def levels(stream_key, dims, cuts, low, top_value):
    def one(dim, blocks):
        steps = jax.random.uniform(jax.random.fold_in(jax.random.fold_in(stream_key, 6), dim), (blocks,), jnp.float32, low / len(cuts), top_value / len(cuts))
        return jnp.repeat(jnp.exp(steps), dims[dim] // blocks).reshape((-1,) + (1,) * (len(dims) - dim - 1))

    gain = one(*cuts[0])
    for cut in cuts[1:]:
        gain = gain * one(*cut)
    return gain


def split_up(count, total, most, skew):
    weights = [(1 << 20) // math.isqrt(standing ** skew) + 1 for standing in range(2, count + 1)]
    rest, holding = total - most - (count - 1), [1] * (count - 1)
    while rest > 0:
        free = [i for i in range(count - 1) if holding[i] < most]
        whole, budget = sum([weights[i] for i in free]), rest
        for i in free:
            addition = min(most - holding[i], max(1, budget * weights[i] // whole), rest)
            holding[i] = holding[i] + addition
            rest = rest - addition
    return np.array([most] + holding)


def ragged_sizes(own_key, amount, total, limit, slope):
    if amount == 2:
        one = jax.random.randint(own_key, (), max(1, total - limit), min(limit, total - 1) + 1)
        return jnp.stack([one, total - one])
    tallies = jnp.asarray(split_up(amount, total, limit, slope), jnp.int32)
    twos = (amount - 1) // 2
    giver, taker = tallies[1:1 + 2 * twos:2], tallies[2:2 + 2 * twos:2]
    room = jnp.minimum(giver - 1, limit - taker)
    moved = jax.random.randint(jax.random.fold_in(own_key, 1), (twos,), 0, 1 << 20) % (room + 1)
    tallies = tallies.at[1:1 + 2 * twos:2].set(giver - moved).at[2:2 + 2 * twos:2].set(taker + moved)
    return tallies[jax.random.permutation(jax.random.fold_in(own_key, 2), amount)]


def normal_values(own_key, shape, deviation, most, cuts=(), kind=jnp.bfloat16):
    entries = jax.random.normal(own_key, shape, jnp.float32) * deviation
    if len(cuts) > 0:
        entries = levels(own_key, shape, cuts, -0.22, 0.18) * entries
    return jnp.clip(entries, min=-most, max=most).astype(kind)


def setup_inputs(seed: int = 0) -> dict:
    keys = jax.random.split(jax.random.key(seed), 20)
    frames_in = normal_values(keys[0], (FRAMES, D), 1.0, 6.0, ((0, 32),))
    frame_item = jax.vmap(lambda own: jnp.searchsorted(jnp.cumsum(ragged_sizes(own, ITEMS_DEV, TOK_DEV, TOK_DEV // 2, 2)), jnp.arange(TOK_DEV), side="right"))(jax.random.split(keys[1], BLOCKS)).reshape((BLOCKS, TOK_DEV)).astype(jnp.int32)
    text_in = normal_values(keys[2], (ITEMS, TXT, TD), 1.0, 6.0, ((0, 16), (1, 2)))
    text_len = set_ends(jax.random.randint(keys[3], (ITEMS,), TXT * 77 // 256, TXT + 1), jax.random.fold_in(keys[3], 1), TXT * 77 // 256, TXT).astype(jnp.int32)
    time_embed = normal_values(keys[4], (ITEMS, D), 1.0, 6.0, ((0, 32),))
    cotangent = normal_values(keys[5], (FRAMES, D), 1.0, 6.0, ((0, 32),))
    w_mod = normal_values(keys[6], (D, 8 * D), D ** -0.5, 0.21875)
    b_mod = normal_values(keys[7], (8 * D,), 0.3, 1.75)
    w_qkv = normal_values(keys[8], (D, 3 * D), D ** -0.5, 0.21875)
    w_out = normal_values(keys[9], (D, D), (D // 8) ** -0.5, 0.625)
    b_out = normal_values(keys[10], (D,), 0.3, 1.75)
    w_q_cross = normal_values(keys[11], (D, D), D ** -0.5, 0.21875)
    w_kv_cross = normal_values(keys[12], (TD, 2 * D), TD ** -0.5, 0.21875)
    w_out_cross = normal_values(keys[13], (D, D), (D // 8) ** -0.5, 0.625)
    b_out_cross = normal_values(keys[14], (D,), 0.3, 1.75)
    w_up = normal_values(keys[15], (D, FF), D ** -0.5, 0.21875)
    b_up = normal_values(keys[16], (FF,), 0.3, 1.75)
    w_down = normal_values(keys[17], (FF, D), FF ** -0.5, 0.109375)
    b_down = normal_values(keys[18], (D,), 0.3, 1.75)
    return dict(frames_in=frames_in, frame_item=frame_item, text_in=text_in, text_len=text_len, time_embed=time_embed, cotangent=cotangent, w_mod=w_mod, b_mod=b_mod, w_qkv=w_qkv, w_out=w_out, b_out=b_out, w_q_cross=w_q_cross, w_kv_cross=w_kv_cross, w_out_cross=w_out_cross, b_out_cross=b_out_cross, w_up=w_up, b_up=b_up, w_down=w_down, b_down=b_down)


@jax.custom_vjp
def low(v):
    return lax.optimization_barrier(v.astype(jnp.bfloat16)).astype(jnp.float32)

@jax.custom_vjp
def low_back(v):
    return v

def low_keep(v):
    return (low(v), None)

def low_pass(kept, grad):
    return (grad,)

def back_keep(v):
    return (v, None)

def back_low(kept, grad):
    return (low(grad),)
low.defvjp(low_keep, low_pass)
low_back.defvjp(back_keep, back_low)
epsilon = 1e-06
masked_add = -1000000000.0
highest = lax.Precision.HIGHEST

def matmul(left_side, right_side):
    return jnp.dot(left_side, right_side, precision=highest)

def layer_norm(values):
    center = values - lax.optimization_barrier(jnp.mean(values, axis=-1, keepdims=True))
    spread = lax.optimization_barrier(jnp.mean(center * center, axis=-1, keepdims=True))
    return center * lax.rsqrt(spread + epsilon)

def gelu_tanh(inputs):
    return 0.5 * inputs * (1.0 + jnp.tanh(0.7978845608028654 * (inputs + 0.044715 * inputs * inputs * inputs)))

def block_forward(frames, embedding, context, params, segment, lengths):
    w_mod, b_mod, w_qkv, w_out, b_out, w_q_cross, w_kv_cross, w_out_cross, b_out_cross, w_up, b_up, w_down, b_down = params
    row_count = frames.shape[0]
    item_count = embedding.shape[0]
    score_scale = HEAD_DIM ** (-0.5)
    condition = low(jax.nn.silu(embedding))
    mod_items = low_back(matmul(condition, w_mod)) + b_mod
    mod_rows = jnp.take(mod_items, segment, axis=0)
    shift_a, scale_a, gate_a, shift_b, scale_b, shift_c, scale_c, gate_c = jnp.split(mod_rows, 8, axis=1)
    normed_a = low(layer_norm(frames) * (1.0 + scale_a) + shift_a)
    packed = low(low_back(matmul(normed_a, w_qkv)))
    queries = packed[:, :D].reshape(row_count, HEADS, HEAD_DIM)
    key_rows = packed[:, D:2 * D].reshape(row_count, HEADS, HEAD_DIM)
    value_rows = packed[:, 2 * D:].reshape(row_count, HEADS, HEAD_DIM)
    same_item = segment[:, None] == segment[None, :]
    scores = jnp.einsum('qhd,khd->hqk', queries, key_rows, precision=highest) * score_scale
    scores = low_back(scores + jnp.where(same_item, 0.0, masked_add)[None])
    maximum = lax.optimization_barrier(jnp.max(scores, axis=-1, keepdims=True))
    exponent = jnp.exp(scores - maximum)
    prob_full = exponent / lax.optimization_barrier(jnp.sum(exponent, axis=-1, keepdims=True))
    attended = jnp.einsum('hqk,khd->qhd', low(prob_full), value_rows, precision=highest).reshape(row_count, D)
    attended = low(low_back(attended))
    branch_a = low_back(matmul(attended, w_out)) + b_out
    after_a = frames + gate_a * branch_a
    normed_b = low(layer_norm(after_a) * (1.0 + scale_b) + shift_b)
    cross_q = low(low_back(matmul(normed_b, w_q_cross))).reshape(row_count, HEADS, HEAD_DIM)
    text_kv = low(low_back(jnp.einsum('itc,cf->itf', context, w_kv_cross, precision=highest)))
    halves = N_TEXT
    token_span = TXT // halves
    cross_k = text_kv[..., :D].reshape(item_count, halves, token_span, HEADS, HEAD_DIM)
    cross_v = text_kv[..., D:].reshape(item_count, halves, token_span, HEADS, HEAD_DIM)
    position = jnp.arange(TXT, dtype=jnp.int32).reshape(halves, token_span)
    item_ids = jnp.arange(item_count, dtype=jnp.int32)
    valid_key = (segment[:, None, None, None] == item_ids[None, :, None, None]) & (position[None, None] < lengths[None, :, None, None])
    cross_s = jnp.einsum('qhd,itjhd->hqitj', cross_q, cross_k, precision=highest) * score_scale
    cross_s = low_back(cross_s + jnp.where(valid_key, 0.0, masked_add)[None])
    peak = lax.optimization_barrier(jnp.max(cross_s, axis=(2, 4), keepdims=True))
    cross_e = jnp.exp(cross_s - peak)
    totals = lax.optimization_barrier(jnp.sum(cross_e, axis=(2, 4)))
    partial_value = jnp.einsum('hqitj,itjhd->hqtd', low(cross_e), cross_v, precision=highest)
    peak_half = peak[:, :, 0, :, 0]
    overall = lax.optimization_barrier(jnp.max(peak_half, axis=2, keepdims=True))
    factor = jnp.exp(peak_half - overall)
    mixed_out = lax.optimization_barrier(jnp.sum(partial_value * factor[..., None], axis=2)) / lax.optimization_barrier(jnp.sum(totals * factor, axis=2))[..., None]
    cross_out = low(low_back(jnp.transpose(mixed_out, (1, 0, 2)).reshape(row_count, D)))
    branch_b = low_back(matmul(cross_out, w_out_cross)) + b_out_cross
    after_b = after_a + branch_b
    normed_c = low(layer_norm(after_b) * (1.0 + scale_c) + shift_c)
    hidden = low_back(matmul(normed_c, w_up)) + b_up
    active = low(gelu_tanh(hidden))
    branch_c = low_back(matmul(active, w_down)) + b_down
    return after_b + gate_c * branch_c

def reference(frames_in, frame_item, text_in, text_len, time_embed, cotangent, w_mod, b_mod, w_qkv, w_out, b_out, w_q_cross, w_kv_cross, w_out_cross, b_out_cross, w_up, b_up, w_down, b_down):
    params = tuple((weight.astype(jnp.float32) for weight in (w_mod, b_mod, w_qkv, w_out, b_out, w_q_cross, w_kv_cross, w_out_cross, b_out_cross, w_up, b_up, w_down, b_down)))
    block_count = frame_item.shape[0]
    frames = frames_in.astype(jnp.float32).reshape(block_count, TOK_DEV, D)
    context = text_in.astype(jnp.float32).reshape(block_count, ITEMS_DEV, TXT, TD)
    lengths = text_len.reshape(block_count, ITEMS_DEV)
    embedding = time_embed.astype(jnp.float32).reshape(block_count, ITEMS_DEV, D)
    upstream = cotangent.astype(jnp.float32).reshape(block_count, TOK_DEV, D)

    def one_block(summed, inputs):
        frame_rows, segment, context_rows, length_rows, embed_rows, upstream_rows = inputs

        def forward(frame_arg, embed_arg, context_arg, param_arg):
            return block_forward(frame_arg, embed_arg, context_arg, param_arg, segment, length_rows)
        result, pullback = jax.vjp(forward, frame_rows, embed_rows, context_rows, params)
        grad_frames, grad_embed, grad_context, grad_params = pullback(upstream_rows)
        summed = tuple((total + piece for total, piece in zip(summed, grad_params)))
        return (summed, (result, grad_frames, grad_context, grad_embed))
    zeros_start = tuple((jnp.zeros(weight.shape, jnp.float32) for weight in params))
    summed, (result, grad_frames, grad_context, grad_embed) = lax.scan(one_block, zeros_start, (frames, frame_item, context, lengths, embedding, upstream))
    return (result.reshape(FRAMES, D), grad_frames.reshape(FRAMES, D), grad_context.reshape(ITEMS, TXT, TD), grad_embed.reshape(ITEMS, D), summed[0], summed[1], summed[2], summed[3], summed[4], summed[5], summed[6], summed[7], summed[8], summed[9], summed[10], summed[11], summed[12])
```

```python
import functools

import jax
import jax.numpy as jnp
from jax import lax
from jax.experimental import pallas as pl
from jax.experimental.pallas import tpu as pltpu
from jax.sharding import PartitionSpec as P

HEAD_DIM = 64
LANES = 128
VMEM_LIMIT = 56 << 20

epsilon = 1e-06
masked_add = -1000000000.0
highest = lax.Precision.HIGHEST
low_type = jnp.bfloat16


def rows_dot(left_side, right_side):
    return jnp.dot(left_side, right_side, preferred_element_type=jnp.float32)


def left_dot(left_side, right_side):
    return lax.dot_general(
        left_side, right_side, (((0,), (0,)), ((), ())), preferred_element_type=jnp.float32
    )


def right_dot(left_side, right_side):
    return lax.dot_general(
        left_side, right_side, (((1,), (1,)), ((), ())), preferred_element_type=jnp.float32
    )


def layer_norm(values):
    center = values - jnp.mean(values, axis=-1, keepdims=True)
    spread = jnp.mean(center * center, axis=-1, keepdims=True)
    return center * lax.rsqrt(spread + epsilon)


def modulate(values, shift_by, scale_by):
    return layer_norm(values) * (1.0 + scale_by) + shift_by


def gelu_tanh(inputs):
    return (
        0.5
        * inputs
        * (1.0 + jnp.tanh(0.7978845608028654 * (inputs + 0.044715 * inputs * inputs * inputs)))
    )


def head_lanes(value, head, scale=None):
    lane = lax.broadcasted_iota(jnp.int32, value.shape, 1)
    scaled = value if scale is None else value * jnp.asarray(scale, value.dtype)
    return jnp.where(lane // HEAD_DIM == head, scaled, jnp.zeros_like(scaled))


def fill_bias(code_column_ref, code_row_ref, bias_refs, key_split):
    half = code_row_ref.shape[1] // 2
    spans = ((0, key_split), (key_split, code_column_ref.shape[0]))
    for part, bias_ref in enumerate(bias_refs):
        if bias_ref is None:
            continue
        low, top = spans[part]
        bias_ref[...] = jnp.where(
            code_column_ref[low:top, :] == code_row_ref[:, part * half : (part + 1) * half],
            0.0,
            masked_add,
        )


def attend_kernel(
    q_ref, k_ref, v_ref, code_column_ref, code_row_ref, out_ref, log_ref, *bias_refs, key_split
):
    half = q_ref.shape[0] // 2
    scale = HEAD_DIM ** (-0.5)
    if len(bias_refs) == 1:
        bias_refs = (None,) + bias_refs

    @pl.when(pl.program_id(0) == 0)
    def _():
        fill_bias(code_column_ref, code_row_ref, bias_refs, key_split)

    value_t = v_ref[...].T
    key_spans = (slice(0, key_split), slice(key_split, k_ref.shape[0]))
    for part in range(2):
        rows = slice(part * half, (part + 1) * half)
        queries = q_ref[rows, :]
        keys = k_ref[key_spans[part], :]
        outs = []
        for head in range(2):
            scores = right_dot(keys, head_lanes(queries, head, scale))
            if bias_refs[part] is not None:
                scores = scores + bias_refs[part][...]
            peak = jnp.max(scores, axis=0, keepdims=True)
            exponent = jnp.exp(scores - peak)
            total = jnp.sum(exponent, axis=0, keepdims=True)
            outs.append(
                rows_dot(
                    value_t[HEAD_DIM * head : HEAD_DIM * (head + 1), key_spans[part]],
                    exponent.astype(low_type),
                )
                / total
            )
            log_ref[0, head : head + 1, rows] = peak + jnp.log(total)
        out_ref[rows, :] = jnp.concatenate(outs, axis=0).T.astype(low_type)


def attend_back_kernel(
    q_ref,
    k_ref,
    v_ref,
    grad_ref,
    log_ref,
    code_column_ref,
    code_row_ref,
    grad_q_ref,
    grad_k_ref,
    grad_v_ref,
    *bias_refs,
    key_split,
):
    half = q_ref.shape[0] // 2
    scale = HEAD_DIM ** (-0.5)
    if len(bias_refs) == 1:
        bias_refs = (None,) + bias_refs

    @pl.when(pl.program_id(0) == 0)
    def _():
        fill_bias(code_column_ref, code_row_ref, bias_refs, key_split)

    key_t = k_ref[...].T
    key_spans = (slice(0, key_split), slice(key_split, k_ref.shape[0]))
    for part in range(2):
        rows = slice(part * half, (part + 1) * half)
        queries = q_ref[rows, :]
        grads = grad_ref[rows, :]
        keys = k_ref[key_spans[part], :]
        values = v_ref[key_spans[part], :]
        grad_q, grad_k, grad_v = [], [], []
        for head in range(2):
            query_head = head_lanes(queries, head, scale)
            grad_head = head_lanes(grads, head)
            scores = right_dot(keys, query_head)
            if bias_refs[part] is not None:
                scores = scores + bias_refs[part][...]
            prob = jnp.exp(scores - log_ref[0, head : head + 1, rows])
            grad_prob = right_dot(values, grad_head)
            weighted = prob * grad_prob
            delta = jnp.sum(weighted, axis=0, keepdims=True)
            grad_scores = (weighted - prob * delta).astype(low_type)
            grad_k.append(rows_dot(grad_scores, query_head))
            grad_v.append(rows_dot(prob.astype(low_type), grad_head))
            grad_q.append(
                rows_dot(
                    key_t[HEAD_DIM * head : HEAD_DIM * (head + 1), key_spans[part]], grad_scores
                )
                * scale
            )
        grad_q_ref[rows, :] = jnp.concatenate(grad_q, axis=0).T.astype(low_type)
        grad_k_ref[key_spans[part], :] = (grad_k[0] + grad_k[1]).astype(low_type)
        grad_v_ref[key_spans[part], :] = (grad_v[0] + grad_v[1]).astype(low_type)


def attention_call(kernel, name, operands, columns, codes, log_total, outs, key_split, key_rows):
    rows = codes[1].shape[1]
    half = rows // 2
    pairs = operands[0].shape[1] // LANES if columns is None else columns[0]
    offsets = columns[1]
    in_specs = [
        pl.BlockSpec((array.shape[0], LANES), lambda step, offset=offset: (0, offset + step))
        for array, offset in zip(operands, offsets)
    ]
    extra = []
    log_spec = pl.BlockSpec((1, 8, rows), lambda step: (step, 0, 0))
    if log_total is not None:
        in_specs.append(log_spec)
        extra.append(log_total)
    in_specs += [
        pl.BlockSpec(codes[0].shape, lambda step: (0, 0)),
        pl.BlockSpec(codes[1].shape, lambda step: (0, 0)),
    ]
    out_shape, out_specs = [], []
    for count in outs:
        if count == "log":
            out_shape.append(jax.ShapeDtypeStruct((pairs, 8, rows), jnp.float32))
            out_specs.append(log_spec)
        else:
            out_shape.append(jax.ShapeDtypeStruct((count, pairs * LANES), low_type))
            out_specs.append(pl.BlockSpec((count, LANES), lambda step: (0, step)))
    scratch = [pltpu.VMEM((key_rows - key_split, half), jnp.float32)]
    if key_split != half:
        scratch = [pltpu.VMEM((key_split, half), jnp.float32)] + scratch
    products = 2 if log_total is None else 5
    cells = half * key_rows
    return pl.pallas_call(
        functools.partial(kernel, key_split=key_split),
        out_shape=out_shape,
        grid=(pairs,),
        in_specs=in_specs,
        out_specs=out_specs,
        scratch_shapes=scratch,
        compiler_params=pltpu.CompilerParams(vmem_limit_bytes=VMEM_LIMIT),
        cost_estimate=pl.CostEstimate(
            flops=products * pairs * 2 * cells * 256 * 2,
            transcendentals=pairs * 2 * cells,
            bytes_accessed=rows * pairs * LANES * 2 * 8,
        ),
        name=name,
    )(*operands, *extra, *codes)


def swapped(value, axis, stride):
    pairs = [(source, source ^ stride) for source in range(lax.axis_size(axis))]
    return lax.ppermute(value, axis, pairs)


def summed_low(kept, received):
    return (kept.astype(jnp.float32) + received.astype(jnp.float32)).astype(low_type)


def share_sum(grad, text_first):
    count = lax.axis_size("frames")
    bits = count.bit_length() - 1
    rows, columns = grad.shape
    spot = lax.axis_index("frames")
    value = grad.reshape((2,) * bits + (rows // count, columns))
    side = lax.axis_index("text")
    dims = list(range(bits))[::-1]
    split = columns // 2

    def along(value, bit):
        dim = dims.index(bit)
        mine = (spot >> bit) & 1
        kept = lax.dynamic_index_in_dim(value, mine, dim, keepdims=False)
        sent = lax.dynamic_index_in_dim(value, 1 - mine, dim, keepdims=False)
        dims.pop(dim)
        return summed_low(kept, swapped(sent, "frames", 1 << bit))

    value = along(value, 0)
    if text_first:
        kept = lax.dynamic_slice_in_dim(value, side * split, split, value.ndim - 1)
        sent = lax.dynamic_slice_in_dim(value, (1 - side) * split, split, value.ndim - 1)
        value = summed_low(kept, swapped(sent, "text", 1))
    for bit in range(1, bits):
        value = along(value, bit)
    if text_first:
        other = swapped(value, "text", 1)
        pair = jnp.where(
            side == 0,
            jnp.concatenate([value, other], axis=1),
            jnp.concatenate([other, value], axis=1),
        )
        return pair.astype(jnp.float32)
    return value.astype(jnp.float32) + swapped(value, "text", 1).astype(jnp.float32)


def gathered(value, order):
    count = lax.axis_size("frames")
    bits = count.bit_length() - 1
    spot = lax.axis_index("frames")
    side = lax.axis_index("text")
    shape = [1] * (bits + 1)
    value = value.reshape(tuple(shape) + value.shape)
    for step in order:
        if step == "text":
            dim, mine = bits, side
            other = swapped(value, "text", 1)
        else:
            dim, mine = bits - 1 - step, (spot >> step) & 1
            other = swapped(value, "frames", 1 << step)
        value = jnp.where(
            mine == 0,
            jnp.concatenate([value, other], axis=dim),
            jnp.concatenate([other, value], axis=dim),
        )
    return value.reshape((-1,) + value.shape[bits + 1 :][1:])


def on_device(
    frames_in,
    frame_item,
    text_in,
    text_len,
    time_embed,
    cotangent,
    w_mod,
    b_mod,
    w_qkv,
    w_out,
    b_out,
    w_q_cross,
    w_kv_cross,
    w_out_cross,
    b_out_cross,
    w_up,
    b_up,
    w_down,
    b_down,
):
    text_side = lax.axis_index("text")
    partner_side = 1 - text_side
    row_count, width = frames_in.shape
    half = row_count // 2
    item_count = time_embed.shape[0]
    token_span = text_in.shape[1]
    token_rows = item_count * 2 * token_span
    frame_bits = lax.axis_size("frames").bit_length() - 1
    segment = lax.dynamic_index_in_dim(frame_item, text_side, 0, keepdims=False)
    own_lengths = lax.dynamic_slice_in_dim(text_len, text_side * item_count, item_count)
    item_ids = jnp.arange(item_count, dtype=jnp.int32)

    own_text = lax.dynamic_slice_in_dim(text_in, text_side * item_count, item_count, 0)
    partner_text = lax.dynamic_slice_in_dim(text_in, partner_side * item_count, item_count, 0)
    fetched_text = swapped(partner_text, "text", 1)

    counts = jnp.sum((segment[None, :] == item_ids[:, None]).astype(jnp.int32), axis=1)
    big = jnp.argmax((counts == half).astype(jnp.int32)).astype(jnp.int32)
    start = jnp.sum((segment < big).astype(jnp.int32))
    segment = jnp.roll(jnp.mod(segment - big, item_count), -start)
    frames = jnp.roll(frames_in, -start, axis=0).astype(jnp.float32)
    upstream = jnp.roll(cotangent, -start, axis=0).astype(jnp.float32)
    lengths = jnp.roll(own_lengths, -big)
    embedding = jnp.roll(time_embed, -big, axis=0).astype(jnp.float32)
    text = jnp.roll(jnp.concatenate([own_text, fetched_text], axis=1), -big, axis=0)
    text = text.reshape(token_rows, text.shape[2])

    self_codes = (segment[:, None], segment[None, :])
    slot = jnp.arange(2 * token_span, dtype=jnp.int32)
    position = jnp.where(
        slot < token_span,
        text_side * token_span + slot,
        partner_side * token_span + slot - token_span,
    )
    token_code = jnp.where(position[None, :] < lengths[:, None], item_ids[:, None], -1)
    cross_codes = (token_code.reshape(token_rows, 1), segment[None, :])
    pairs = width // LANES

    condition = jax.nn.silu(embedding).astype(low_type)
    mod_items = rows_dot(condition, w_mod) + b_mod.astype(jnp.float32)
    onehot = (segment[:, None] == item_ids[None, :]).astype(jnp.float32)
    mod_rows = jnp.dot(onehot, mod_items, precision=highest)
    shift_a, scale_a, gate_a, shift_b, scale_b, shift_c, scale_c, gate_c = jnp.split(
        mod_rows, 8, axis=1
    )
    normed_a = modulate(frames, shift_a, scale_a).astype(low_type)
    packed = rows_dot(normed_a, w_qkv).astype(low_type)
    packed_columns = (pairs, (0, pairs, 2 * pairs, 0))
    attended, self_log = attention_call(
        attend_kernel,
        "self_forward",
        (packed, packed, packed),
        packed_columns,
        self_codes,
        None,
        (row_count, "log"),
        half,
        row_count,
    )
    branch_a = rows_dot(attended, w_out) + b_out.astype(jnp.float32)
    after_a = frames + gate_a * branch_a
    normed_b = modulate(after_a, shift_b, scale_b).astype(low_type)
    cross_q = rows_dot(normed_b, w_q_cross).astype(low_type)
    text_kv = rows_dot(text, w_kv_cross).astype(low_type)
    cross_columns = (pairs, (0, 0, pairs, 0))
    cross_out, cross_log = attention_call(
        attend_kernel,
        "cross_forward",
        (cross_q, text_kv, text_kv),
        cross_columns,
        cross_codes,
        None,
        (row_count, "log"),
        2 * token_span,
        token_rows,
    )
    branch_b = rows_dot(cross_out, w_out_cross) + b_out_cross.astype(jnp.float32)
    after_b = after_a + branch_b
    normed_c = modulate(after_b, shift_c, scale_c).astype(low_type)
    hidden = rows_dot(normed_c, w_up) + b_up.astype(jnp.float32)
    active = gelu_tanh(hidden).astype(low_type)
    branch_c = rows_dot(active, w_down) + b_down.astype(jnp.float32)
    frames_out = jnp.roll(after_b + gate_c * branch_c, start, axis=0)
    grad_branch_c = gate_c * upstream
    grad_gate_c = upstream * branch_c
    low_branch_c = grad_branch_c.astype(low_type)
    grad_w_down = left_dot(active, low_branch_c).astype(low_type)
    grad_b_down = jnp.sum(grad_branch_c, axis=0)
    grad_active = right_dot(low_branch_c, w_down)
    grad_hidden = jax.vjp(gelu_tanh, hidden)[1](grad_active)[0]
    low_hidden = grad_hidden.astype(low_type)
    grad_w_up = left_dot(normed_c, low_hidden).astype(low_type)
    grad_b_up = jnp.sum(grad_hidden, axis=0)
    sum_w_down = share_sum(grad_w_down, False)
    sum_w_up = share_sum(grad_w_up, True)
    grad_after_b, grad_shift_c, grad_scale_c = jax.vjp(modulate, after_b, shift_c, scale_c)[1](
        right_dot(low_hidden, w_up)
    )
    grad_after_b = grad_after_b + upstream
    low_after_b = grad_after_b.astype(low_type)
    grad_w_out_cross = left_dot(cross_out, low_after_b).astype(low_type)
    grad_b_out_cross = jnp.sum(grad_after_b, axis=0)
    grad_cross = right_dot(low_after_b, w_out_cross).astype(low_type)
    low_cross_q, grad_text_k, grad_text_v = attention_call(
        attend_back_kernel,
        "cross_backward",
        (cross_q, text_kv, text_kv, grad_cross),
        cross_columns,
        cross_codes,
        cross_log,
        (row_count, token_rows, token_rows),
        2 * token_span,
        token_rows,
    )
    text_sum = right_dot(grad_text_k, w_kv_cross[:, :width]) + right_dot(
        grad_text_v, w_kv_cross[:, width:]
    )
    text_sum = jnp.roll(text_sum.reshape(item_count, 2 * token_span, -1), big, axis=0)
    own_text_grad = text_sum[:, :token_span]
    sent_text_grad = text_sum[:, token_span:].astype(low_type)
    partner_text_grad = swapped(sent_text_grad, "text", 1).astype(jnp.float32)
    text_grad = jnp.where(
        text_side == 0,
        jnp.concatenate([own_text_grad, partner_text_grad], axis=0),
        jnp.concatenate([partner_text_grad, own_text_grad], axis=0),
    )
    grad_w_kv_cross = jnp.concatenate(
        [left_dot(text, grad_text_k).astype(low_type), left_dot(text, grad_text_v).astype(low_type)],
        axis=1,
    )
    grad_w_q_cross = left_dot(normed_b, low_cross_q).astype(low_type)
    cross_sum = share_sum(
        jnp.concatenate([grad_w_kv_cross, grad_w_q_cross, grad_w_out_cross], axis=1), True
    )
    grad_after_a, grad_shift_b, grad_scale_b = jax.vjp(modulate, after_a, shift_b, scale_b)[1](
        right_dot(low_cross_q, w_q_cross)
    )
    grad_after_a = grad_after_a + grad_after_b
    grad_branch_a = gate_a * grad_after_a
    grad_gate_a = grad_after_a * branch_a
    low_branch_a = grad_branch_a.astype(low_type)
    grad_w_out = left_dot(attended, low_branch_a).astype(low_type)
    grad_b_out = jnp.sum(grad_branch_a, axis=0)
    grad_attended = right_dot(low_branch_a, w_out).astype(low_type)
    grad_packed = attention_call(
        attend_back_kernel,
        "self_backward",
        (packed, packed, packed, grad_attended),
        packed_columns,
        self_codes,
        self_log,
        (row_count, row_count, row_count),
        half,
        row_count,
    )
    grad_w_qkv = [left_dot(normed_a, piece).astype(low_type) for piece in grad_packed]
    self_sum = share_sum(jnp.concatenate(grad_w_qkv + [grad_w_out], axis=1), False)
    grad_normed_a = sum(
        right_dot(piece, w_qkv[:, index * width : (index + 1) * width])
        for index, piece in enumerate(grad_packed)
    )
    grad_frames, grad_shift_a, grad_scale_a = jax.vjp(modulate, frames, shift_a, scale_a)[1](
        grad_normed_a
    )
    frames_grad = jnp.roll(grad_frames + grad_after_a, start, axis=0)
    grad_mod_rows = jnp.concatenate(
        [
            grad_shift_a,
            grad_scale_a,
            grad_gate_a,
            grad_shift_b,
            grad_scale_b,
            grad_shift_c,
            grad_scale_c,
            grad_gate_c,
        ],
        axis=1,
    )
    grad_mod = lax.dot_general(onehot, grad_mod_rows, (((0,), (0,)), ((), ())), precision=highest)
    low_mod = grad_mod.astype(low_type)
    time_grad = jax.vjp(jax.nn.silu, embedding)[1](right_dot(low_mod, w_mod))[0]
    time_grad = jnp.roll(time_grad, big, axis=0)

    order = tuple(range(frame_bits - 1, 0, -1)) + ("text", 0)
    all_mod = gathered(jnp.roll(low_mod, big, axis=0), order)
    all_conditions = gathered(jnp.roll(condition, big, axis=0), order)
    share = lax.axis_size("frames")
    spot = lax.axis_index("frames")
    own_conditions = lax.dynamic_slice_in_dim(
        all_conditions, spot * (width // share), width // share, 1
    )
    grad_w_mod = left_dot(own_conditions, all_mod)
    mod_columns = all_mod.shape[1] // share
    grad_b_mod = jnp.sum(
        lax.dynamic_slice_in_dim(all_mod, spot * mod_columns, mod_columns, 1).astype(jnp.float32),
        axis=0,
    )
    biases = [grad_b_out, grad_b_out_cross, grad_b_up, grad_b_down]
    bias_sum = lax.psum(
        lax.psum_scatter(
            jnp.concatenate([bias.reshape(share, -1) for bias in biases], axis=1),
            "frames",
            scatter_dimension=0,
            tiled=True,
        ),
        "text",
    )[0]
    bias_cuts, done = [], 0
    for bias in biases:
        bias_cuts.append(bias_sum[done : done + bias.shape[0] // share])
        done += bias.shape[0] // share
    sum_kv_cross = cross_sum[:, : 2 * width]
    sum_q_cross = cross_sum[:, 2 * width : 3 * width]
    sum_out_cross = cross_sum[:, 3 * width :]
    return (
        frames_out,
        frames_grad,
        text_grad,
        time_grad,
        grad_w_mod,
        grad_b_mod,
        self_sum[:, : 3 * width],
        self_sum[:, 3 * width :],
        bias_cuts[0],
        sum_q_cross,
        sum_kv_cross,
        sum_out_cross,
        bias_cuts[1],
        sum_w_up,
        bias_cuts[2],
        sum_w_down,
        bias_cuts[3],
    )


def solution(mesh):
    in_specs = (
        P(("frames", "text"), None),
        P("frames", None),
        P("frames", "text", None),
        P("frames"),
        P(("frames", "text"), None),
        P(("frames", "text"), None),
    ) + (P(),) * 13
    out_specs = (
        P(("frames", "text"), None),
        P(("frames", "text"), None),
        P("frames", "text", None),
        P(("frames", "text"), None),
        P("frames", None),
        P("frames"),
        P("frames", None),
        P("frames", None),
        P("frames"),
        P("frames", None),
        P("frames", None),
        P("frames", None),
        P("frames"),
        P("frames", None),
        P("frames"),
        P("frames", None),
        P("frames"),
    )
    return jax.shard_map(
        on_device, mesh=mesh, in_specs=in_specs, out_specs=out_specs, check_vma=False
    )
```

```python
import functools

import jax
import jax.numpy as jnp
from jax import lax
from jax.experimental import pallas as pl
from jax.experimental.pallas import tpu as pltpu
from jax.sharding import PartitionSpec as P

HEAD_DIM = 64
LANES = 128
VMEM_LIMIT = 60 << 20

epsilon = 1e-06
masked_add = -1000000000.0
highest = lax.Precision.HIGHEST
low_type = jnp.bfloat16


def rows_dot(left_side, right_side):
    return jnp.dot(left_side, right_side, preferred_element_type=jnp.float32)


def left_dot(left_side, right_side):
    return lax.dot_general(
        left_side, right_side, (((0,), (0,)), ((), ())), preferred_element_type=jnp.float32
    )


def right_dot(left_side, right_side):
    return lax.dot_general(
        left_side, right_side, (((1,), (1,)), ((), ())), preferred_element_type=jnp.float32
    )


def layer_norm(values):
    center = values - jnp.mean(values, axis=-1, keepdims=True)
    spread = jnp.mean(center * center, axis=-1, keepdims=True)
    return center * lax.rsqrt(spread + epsilon)


def modulate(values, shift_by, scale_by):
    return layer_norm(values) * (1.0 + scale_by) + shift_by


def gelu_tanh(inputs):
    return (
        0.5
        * inputs
        * (1.0 + jnp.tanh(0.7978845608028654 * (inputs + 0.044715 * inputs * inputs * inputs)))
    )


def head_lanes(value, head, scale=None):
    lane = lax.broadcasted_iota(jnp.int32, value.shape, 1)
    scaled = value if scale is None else value * jnp.asarray(scale, value.dtype)
    return jnp.where(lane // HEAD_DIM == head, scaled, jnp.zeros_like(scaled))


def fill_bias(code_column_ref, code_row_ref, bias_refs, key_split):
    half = code_row_ref.shape[1] // 2
    spans = ((0, key_split), (key_split, code_column_ref.shape[0]))
    for part, bias_ref in enumerate(bias_refs):
        if bias_ref is None:
            continue
        low, top = spans[part]
        bias_ref[...] = jnp.where(
            code_column_ref[low:top, :] == code_row_ref[:, part * half : (part + 1) * half],
            0.0,
            masked_add,
        )


def attend_kernel(
    q_ref, k_ref, v_ref, code_column_ref, code_row_ref, out_ref, log_ref, *bias_refs, key_split
):
    half = q_ref.shape[0] // 2
    scale = HEAD_DIM ** (-0.5)
    if len(bias_refs) == 1:
        bias_refs = (None,) + bias_refs

    @pl.when(pl.program_id(0) == 0)
    def _():
        fill_bias(code_column_ref, code_row_ref, bias_refs, key_split)

    value_t = v_ref[...].T
    key_spans = (slice(0, key_split), slice(key_split, k_ref.shape[0]))
    for part in range(2):
        rows = slice(part * half, (part + 1) * half)
        queries = q_ref[rows, :]
        keys = k_ref[key_spans[part], :]
        outs = []
        for head in range(2):
            scores = right_dot(keys, head_lanes(queries, head, scale))
            if bias_refs[part] is not None:
                scores = scores + bias_refs[part][...]
            peak = jnp.max(scores, axis=0, keepdims=True)
            exponent = jnp.exp(scores - peak)
            total = jnp.sum(exponent, axis=0, keepdims=True)
            outs.append(
                rows_dot(
                    value_t[HEAD_DIM * head : HEAD_DIM * (head + 1), key_spans[part]],
                    exponent.astype(low_type),
                )
                / total
            )
            log_ref[0, head : head + 1, rows] = peak + jnp.log(total)
        out_ref[rows, :] = jnp.concatenate(outs, axis=0).T.astype(low_type)


def attend_back_kernel(
    q_ref,
    k_ref,
    v_ref,
    grad_ref,
    log_ref,
    code_column_ref,
    code_row_ref,
    grad_q_ref,
    grad_k_ref,
    grad_v_ref,
    *bias_refs,
    key_split,
):
    half = q_ref.shape[0] // 2
    scale = HEAD_DIM ** (-0.5)
    if len(bias_refs) == 1:
        bias_refs = (None,) + bias_refs

    @pl.when(pl.program_id(0) == 0)
    def _():
        fill_bias(code_column_ref, code_row_ref, bias_refs, key_split)

    key_t = k_ref[...].T
    key_spans = (slice(0, key_split), slice(key_split, k_ref.shape[0]))
    for part in range(2):
        rows = slice(part * half, (part + 1) * half)
        queries = q_ref[rows, :]
        grads = grad_ref[rows, :]
        keys = k_ref[key_spans[part], :]
        values = v_ref[key_spans[part], :]
        grad_q, grad_k, grad_v = [], [], []
        for head in range(2):
            query_head = head_lanes(queries, head, scale)
            grad_head = head_lanes(grads, head)
            scores = right_dot(keys, query_head)
            if bias_refs[part] is not None:
                scores = scores + bias_refs[part][...]
            prob = jnp.exp(scores - log_ref[0, head : head + 1, rows])
            grad_prob = right_dot(values, grad_head)
            weighted = prob * grad_prob
            delta = jnp.sum(weighted, axis=0, keepdims=True)
            grad_scores = (weighted - prob * delta).astype(low_type)
            grad_k.append(rows_dot(grad_scores, query_head))
            grad_v.append(rows_dot(prob.astype(low_type), grad_head))
            grad_q.append(
                rows_dot(
                    key_t[HEAD_DIM * head : HEAD_DIM * (head + 1), key_spans[part]], grad_scores
                )
                * scale
            )
        grad_q_ref[rows, :] = jnp.concatenate(grad_q, axis=0).T.astype(low_type)
        grad_k_ref[key_spans[part], :] = (grad_k[0] + grad_k[1]).astype(low_type)
        grad_v_ref[key_spans[part], :] = (grad_v[0] + grad_v[1]).astype(low_type)


def attention_call(
    kernel, name, operands, columns, codes, log_total, outs, key_split, key_rows, exchange=None
):
    rows = codes[1].shape[1]
    half = rows // 2
    pairs, offsets = columns
    specs = [
        pl.BlockSpec((array.shape[0], LANES), lambda step, offset=offset: (0, offset + step))
        for array, offset in zip(operands, offsets)
    ]
    extra = []
    log_spec = pl.BlockSpec((1, 8, rows), lambda step: (step, 0, 0))
    if log_total is not None:
        specs.append(log_spec)
        extra.append(log_total)
    specs += [whole(code) for code in codes]
    out_shape, out_specs = [], []
    for count in outs:
        if count == "log":
            out_shape.append(jax.ShapeDtypeStruct((pairs, 8, rows), jnp.float32))
            out_specs.append(log_spec)
        else:
            out_shape.append(jax.ShapeDtypeStruct((count, pairs * LANES), low_type))
            out_specs.append(pl.BlockSpec((count, LANES), lambda step: (0, step)))
    scratch = [pltpu.VMEM((key_rows - key_split, half), jnp.float32)]
    if key_split != half:
        scratch = [pltpu.VMEM((key_split, half), jnp.float32)] + scratch
    products = 2 if log_total is None else 5
    cells = half * key_rows
    return run(
        functools.partial(kernel, key_split=key_split),
        name,
        pairs,
        (),
        list(operands) + extra + list(codes),
        specs,
        out_shape,
        out_specs,
        scratch,
        products * pairs * 2 * cells * 256 * 2,
        exchange,
        pairs * 2 * cells,
    )


ROW_BLOCK = 256
SHIFT_A, SCALE_A, GATE_A, SHIFT_B, SCALE_B, SHIFT_C, SCALE_C, GATE_C = range(8)


def item_rows(mod_ref, part, code):
    out = mod_ref[0, part : part + 1, :]
    for item in range(1, mod_ref.shape[0]):
        out = jnp.where(code == item, mod_ref[item, part : part + 1, :], out)
    return out


def item_mask(code_row):
    ids = lax.broadcasted_iota(jnp.int32, (8, code_row.shape[1]), 0)
    return jnp.where(ids == code_row, 1.0, 0.0).astype(low_type)


def item_sums(mask, values):
    high = values.astype(low_type)
    rest = (values - high.astype(jnp.float32)).astype(low_type)
    return rows_dot(mask, high) + rows_dot(mask, rest)


def column_sum(values):
    return jnp.sum(values, axis=0, keepdims=True)


def normed_of(values):
    center = values - jnp.mean(values, axis=-1, keepdims=True)
    spread = jnp.mean(center * center, axis=-1, keepdims=True)
    inverse = lax.rsqrt(spread + epsilon)
    return center * inverse, inverse


def normed_back(grad, scale_by, normed, inverse):
    inner = grad * (1.0 + scale_by)
    return inverse * (
        inner
        - jnp.mean(inner, axis=-1, keepdims=True)
        - normed * jnp.mean(inner * normed, axis=-1, keepdims=True)
    )


def rolled_rows(source_ref, wide_ref):
    rows = source_ref.shape[0]
    wide_ref[:rows, :] = source_ref[...].astype(jnp.float32)
    wide_ref[rows : rows + rows // 2, :] = source_ref[: rows // 2, :].astype(jnp.float32)


def rows_from(wide_ref, first, offset, count):
    rest = lax.rem(first, 8)
    where = pl.ds(pl.multiple_of(first - rest + offset, 8), count + 8)
    rows = wide_ref[where, :].reshape(count // 8 + 1, 8, wide_ref.shape[1])
    turned = pltpu.roll(rows, lax.rem(8 - rest, 8), 1)
    near = lax.broadcasted_iota(jnp.int32, (1, 8, wide_ref.shape[1]), 1) < 8 - rest
    return jnp.where(near, turned[:-1], turned[1:]).reshape(count, wide_ref.shape[1])


def enter_kernel(
    start_ref,
    frames_ref,
    cotangent_ref,
    code_ref,
    mod_ref,
    w_qkv_ref,
    packed_ref,
    normed_ref,
    frames_out_ref,
    cotangent_out_ref,
    wide_frames,
    wide_cotangent,
):
    step = pl.program_id(0)
    block = packed_ref.shape[0]

    @pl.when(step == 0)
    def _():
        rolled_rows(frames_ref, wide_frames)
        rolled_rows(cotangent_ref, wide_cotangent)

    frames = rows_from(wide_frames, start_ref[0], step * block, block)
    frames_out_ref[...] = frames.astype(low_type)
    cotangent_out_ref[...] = rows_from(wide_cotangent, start_ref[0], step * block, block).astype(
        low_type
    )
    code = code_ref[...]
    normed, _ = normed_of(frames)
    modulated = normed * (1.0 + item_rows(mod_ref, SCALE_A, code)) + item_rows(
        mod_ref, SHIFT_A, code
    )
    low = modulated.astype(low_type)
    normed_ref[...] = low
    packed_ref[...] = rows_dot(low, w_qkv_ref[...]).astype(low_type)


def middle_kernel(
    attended_ref,
    frames_ref,
    code_ref,
    mod_ref,
    w_out_ref,
    b_out_ref,
    w_q_ref,
    after_ref,
    branch_ref,
    normed_ref,
    cross_q_ref,
):
    code = code_ref[...]
    branch = rows_dot(attended_ref[...], w_out_ref[...]) + b_out_ref[...]
    branch_ref[...] = branch
    after = frames_ref[...].astype(jnp.float32) + item_rows(mod_ref, GATE_A, code) * branch
    after_ref[...] = after
    normed, _ = normed_of(after)
    low = (
        normed * (1.0 + item_rows(mod_ref, SCALE_B, code)) + item_rows(mod_ref, SHIFT_B, code)
    ).astype(low_type)
    normed_ref[...] = low
    cross_q_ref[...] = rows_dot(low, w_q_ref[...]).astype(low_type)


GELU_FACTOR = 0.7978845608028654
GELU_CUBE = 0.044715


def gelu_both(inputs):
    square = inputs * inputs
    bend = jnp.tanh(inputs * (GELU_FACTOR + (GELU_FACTOR * GELU_CUBE) * square))
    half_up = 0.5 + 0.5 * bend
    slope = half_up + (0.5 * inputs) * (1.0 - bend * bend) * (
        GELU_FACTOR + (3.0 * GELU_FACTOR * GELU_CUBE) * square
    )
    return inputs * half_up, slope


def mlp_kernel(
    cross_out_ref,
    after_a_ref,
    cotangent_ref,
    code_ref,
    code_row_ref,
    mod_ref,
    w_out_cross_ref,
    b_out_cross_ref,
    b_down_ref,
    w_up_ref,
    b_up_ref,
    w_down_ref,
    wide,
    grad_after_ref,
    grad_cross_ref,
    grad_w_down_ref,
    grad_w_up_ref,
    grad_w_out_cross_ref,
    grad_b_up_ref,
    grad_b_ref,
    sums_ref,
    normed_c,
    normed_c_t,
    low_branch,
    back_sum,
    active,
    low_hidden,
    *core,
):
    after_b = grad_after_ref
    step = pl.program_id(0)
    steps = pl.num_programs(0)
    rows = cross_out_ref.shape[0]
    half = rows // 2
    block = ROW_BLOCK
    blocks = rows // block

    def span(index):
        return pl.ds(pl.multiple_of(index * block, block), block)

    def after_half(index):
        return pl.ds(pl.multiple_of(half + index * block, block), block)

    def copies(index):
        down, up, down_in, up_in, send, receive = core
        mine, peer = place(0)
        slot = lax.rem(index, 2)
        return [
            pltpu.make_async_remote_copy(
                src_ref=out.at[slot, :, 1 - mine],
                dst_ref=into.at[index],
                send_sem=send.at[index, which],
                recv_sem=receive.at[index, which],
                device_id=peer,
                device_id_type=MESH,
            )
            for which, (out, into) in enumerate(((down, down_in), (up, up_in)))
        ]

    def settle(index):
        down, up, down_in, up_in, send, receive = core
        mine = place(0)[0]
        slot = lax.rem(index, 2)
        for copy in copies(index):
            copy.wait()
        grad_w_down_ref[index] = down[slot, :, mine] + down_in[index]
        side, part = index // 2, lax.rem(index, 2)
        grad_w_up_ref[side, part] = up[slot, :, mine] + up_in[index]

    @pl.when(step == 0)
    def _():
        if core:
            greet([0])

        def body(index, _):
            where = span(index)
            code = code_ref[where, :]
            branch = rows_dot(cross_out_ref[where, :], w_out_cross_ref[...]) + b_out_cross_ref[...]
            after = after_a_ref[where, :] + branch
            after_b[where, :] = after
            normed, _ = normed_of(after)
            normed_c[where, :] = (
                normed * (1.0 + item_rows(mod_ref, SCALE_C, code))
                + item_rows(mod_ref, SHIFT_C, code)
            ).astype(low_type)
            low_branch[where, :] = (
                item_rows(mod_ref, GATE_C, code) * cotangent_ref[where, :].astype(jnp.float32)
            ).astype(low_type)
            wide[after_half(index), :] = jnp.zeros((block, wide.shape[1]), jnp.float32)
            back_sum[where, :] = jnp.zeros((block, back_sum.shape[1]), jnp.float32)
            return 0

        lax.fori_loop(0, blocks, body, 0)
        normed_c_t[...] = normed_c[...].T

    bias_total = jnp.zeros((1, w_up_ref.shape[1]), jnp.float32)
    for index in range(blocks):
        where = pl.ds(index * block, block)
        hidden = rows_dot(normed_c[where, :], w_up_ref[...]) + b_up_ref[...]
        grad_active = right_dot(low_branch[where, :], w_down_ref[...])
        value, slope = gelu_both(hidden)
        low_value = value.astype(low_type)
        active[where, :] = low_value
        wide[after_half(index), :] += rows_dot(low_value, w_down_ref[...])
        grad_hidden = slope * grad_active
        bias_total = bias_total + column_sum(grad_hidden)
        low = grad_hidden.astype(low_type)
        low_hidden[where, :] = low
        back_sum[where, :] += right_dot(low, w_up_ref[...])
    grad_b_up_ref[...] = bias_total
    down_part = left_dot(active[...], low_branch[...]).astype(low_type)
    up_part = rows_dot(normed_c_t[...], low_hidden[...]).astype(low_type)
    if core:
        slot = lax.rem(step, 2)
        core[0][slot] = down_part.reshape(core[0].shape[1:])
        core[1][slot] = up_part.reshape(core[1].shape[1:])
        for copy in copies(step):
            copy.start()

        @pl.when(step > 0)
        def _():
            settle(step - 1)
    else:
        grad_w_down_ref[0] = down_part
        grad_w_up_ref[0] = up_part

    @pl.when(step == steps - 1)
    def _():
        sums_ref[...] = jnp.zeros(sums_ref.shape, jnp.float32)
        grad_b_ref[...] = jnp.zeros(grad_b_ref.shape, jnp.float32)

        def body(index, _):
            where = span(index)
            code = code_ref[where, :]
            mask = item_mask(code_row_ref[:, where])
            upstream = cotangent_ref[where, :].astype(jnp.float32)
            branch = wide[after_half(index), :] + b_down_ref[...]
            gate = item_rows(mod_ref, GATE_C, code)
            after = after_b[where, :]
            out = after + gate * branch
            wide[after_half(index), :] = out

            @pl.when(index >= blocks // 2)
            def _():
                wide[pl.ds(pl.multiple_of(index * block - half, block), block), :] = out

            sums_ref[2] += item_sums(mask, upstream * branch)
            grad_b_ref[0:1, :] += column_sum(gate * upstream)
            normed, inverse = normed_of(after)
            grad = back_sum[where, :]
            sums_ref[0] += item_sums(mask, grad)
            sums_ref[1] += item_sums(mask, grad * normed)
            total = upstream + normed_back(
                grad, item_rows(mod_ref, SCALE_C, code), normed, inverse
            )
            grad_after_ref[where, :] = total
            grad_b_ref[1:2, :] += column_sum(total)
            low = total.astype(low_type)
            low_branch[where, :] = low
            grad_cross_ref[where, :] = right_dot(low, w_out_cross_ref[...]).astype(low_type)
            return 0

        lax.fori_loop(0, blocks, body, 0)
        grad_w_out_cross_ref[...] = left_dot(cross_out_ref[...], low_branch[...]).astype(low_type)

        if core:
            settle(step)


def text_back_kernel(
    big_ref,
    start_ref,
    grad_k_ref,
    grad_v_ref,
    text_ref,
    w_kv_ref,
    wide_ref,
    own_ref,
    sent_ref,
    grad_w_ref,
    frames_out_ref,
    all_k,
    all_v,
    all_text,
):
    step = pl.program_id(0)
    rows = frames_out_ref.shape[0]
    half = pl.num_programs(0) * rows // 2
    frames_out_ref[...] = rows_from(wide_ref, half - start_ref[0], step * rows, rows)
    block, width = grad_k_ref.shape
    span = own_ref.shape[1]
    where = pl.ds(pl.multiple_of(step * block, block), block)
    keys, values = grad_k_ref[...], grad_v_ref[...]
    all_k[where, :] = keys
    all_v[where, :] = values
    all_text[where, :] = text_ref[...]
    total = right_dot(keys, w_kv_ref[:, :width]) + right_dot(values, w_kv_ref[:, width:])
    own_ref[0] = total[:span]
    sent_ref[0] = total[span:].astype(low_type)

    @pl.when(step == pl.num_programs(0) - 1)
    def _():
        text_t = all_text[...].T
        grad_w_ref[0] = rows_dot(text_t, all_k[...]).astype(low_type)
        grad_w_ref[1] = rows_dot(text_t, all_v[...]).astype(low_type)


def back_middle_kernel(
    low_q_ref,
    normed_b_ref,
    after_a_ref,
    grad_after_b_ref,
    branch_ref,
    attended_ref,
    code_ref,
    code_row_ref,
    mod_ref,
    w_q_ref,
    w_out_ref,
    grad_after_ref,
    grad_attended_ref,
    grad_w_q_ref,
    grad_w_out_ref,
    grad_b_ref,
    sums_ref,
    all_q,
    all_normed,
    all_attended,
    all_branch,
):
    step = pl.program_id(0)
    block = low_q_ref.shape[0]

    @pl.when(step == 0)
    def _():
        sums_ref[...] = jnp.zeros(sums_ref.shape, jnp.float32)
        grad_b_ref[...] = jnp.zeros(grad_b_ref.shape, jnp.float32)

    where = pl.ds(pl.multiple_of(step * block, block), block)
    code = code_ref[...]
    mask = item_mask(code_row_ref[...])
    low_q = low_q_ref[...]
    all_q[where, :] = low_q
    all_normed[where, :] = normed_b_ref[...]
    all_attended[where, :] = attended_ref[...]
    grad = right_dot(low_q, w_q_ref[...])
    normed, inverse = normed_of(after_a_ref[...])
    sums_ref[1] += item_sums(mask, grad)
    sums_ref[2] += item_sums(mask, grad * normed)
    total = grad_after_b_ref[...] + normed_back(
        grad, item_rows(mod_ref, SCALE_B, code), normed, inverse
    )
    grad_after_ref[...] = total
    sums_ref[0] += item_sums(mask, total * branch_ref[...])
    grad_branch = item_rows(mod_ref, GATE_A, code) * total
    grad_b_ref[0:1, :] += column_sum(grad_branch)
    low = grad_branch.astype(low_type)
    all_branch[where, :] = low
    grad_attended_ref[...] = right_dot(low, w_out_ref[...]).astype(low_type)

    @pl.when(step == pl.num_programs(0) - 1)
    def _():
        grad_w_q_ref[...] = left_dot(all_normed[...], all_q[...]).astype(low_type)
        grad_w_out_ref[...] = left_dot(all_attended[...], all_branch[...]).astype(low_type)


def leave_kernel(
    grad_q_ref,
    grad_k_ref,
    grad_v_ref,
    normed_a_ref,
    frames_ref,
    grad_after_ref,
    code_ref,
    code_row_ref,
    mod_ref,
    w_qkv_ref,
    wide,
    grad_w_first_ref,
    grad_w_second_ref,
    sums_ref,
    all_pieces,
    all_normed,
):
    step = pl.program_id(0)
    block = grad_q_ref.shape[0]
    width = grad_q_ref.shape[1]
    half = all_normed.shape[0] // 2
    blocks = all_normed.shape[0] // block

    @pl.when(step == 0)
    def _():
        sums_ref[...] = jnp.zeros(sums_ref.shape, jnp.float32)

    where = pl.ds(pl.multiple_of(step * block, block), block)
    code = code_ref[...]
    mask = item_mask(code_row_ref[...])
    all_normed[where, :] = normed_a_ref[...]
    grad = jnp.zeros((block, width), jnp.float32)
    for index, ref in enumerate((grad_q_ref, grad_k_ref, grad_v_ref)):
        piece = ref[...]
        all_pieces[where, index * width : (index + 1) * width] = piece
        grad = grad + right_dot(piece, w_qkv_ref[:, index * width : (index + 1) * width])
    normed, inverse = normed_of(frames_ref[...].astype(jnp.float32))
    sums_ref[0] += item_sums(mask, grad)
    sums_ref[1] += item_sums(mask, grad * normed)
    out = grad_after_ref[...] + normed_back(
        grad, item_rows(mod_ref, SCALE_A, code), normed, inverse
    )
    wide[pl.ds(pl.multiple_of(half + step * block, block), block), :] = out

    @pl.when(step >= blocks // 2)
    def _():
        wide[pl.ds(pl.multiple_of(step * block - half, block), block), :] = out

    @pl.when(step == blocks - 1)
    def _():
        normed_t = all_normed[...].T
        first = grad_w_first_ref.shape[1]
        second = grad_w_second_ref.shape[2]
        grad_w_first_ref[...] = rows_dot(normed_t, all_pieces[:, :first]).astype(low_type)
        for side in range(2):
            at = first + side * second
            grad_w_second_ref[side] = rows_dot(normed_t, all_pieces[:, at : at + second]).astype(
                low_type
            )


def time_kernel(low_mod_ref, embedding_ref, w_mod_ref, out_ref, total):
    step = pl.program_id(0)

    @pl.when(step == 0)
    def _():
        total[...] = jnp.zeros_like(total)

    total[...] += right_dot(low_mod_ref[...], w_mod_ref[...])

    @pl.when(step == pl.num_programs(0) - 1)
    def _():
        embedding = embedding_ref[...]
        gate = 1.0 / (1.0 + jnp.exp(-embedding))
        out_ref[...] = total[...] * (gate + embedding * gate * (1.0 - gate))


def finish_kernel(
    start_ref,
    side_ref,
    spot_ref,
    wide_ref,
    own_ref,
    partner_ref,
    table_ref,
    up_ref,
    first_ref,
    second_ref,
    kv_ref,
    frames_grad_ref,
    text_grad_ref,
    grad_w_mod_ref,
    item_total_ref,
    sum_up_ref,
    sum_qkv_ref,
    sum_kv_ref,
):
    step = pl.program_id(0)
    rows = frames_grad_ref.shape[0]
    half = pl.num_programs(0) * rows // 2
    frames_grad_ref[...] = rows_from(wide_ref, half - start_ref[0], step * rows, rows)
    mine = step // (pl.num_programs(0) // 2) == side_ref[0]

    @pl.when(mine)
    def _():
        text_grad_ref[...] = own_ref[...]

    @pl.when(jnp.logical_not(mine))
    def _():
        text_grad_ref[...] = partner_ref[...].astype(jnp.float32)

    @pl.when(step == 0)
    def _():
        share, columns = grad_w_mod_ref.shape
        table = table_ref[:, : columns // 2]
        width = table_ref.shape[1] - columns // 2
        entry = lax.broadcasted_iota(jnp.int32, (width, share), 0)
        wanted = lax.broadcasted_iota(jnp.int32, (width, share), 1) + spot_ref[0] * share
        chosen = jnp.where(entry == wanted, 1.0, 0.0).astype(low_type)
        own = rows_dot(table_ref[:, columns // 2 :], chosen)
        item = lax.broadcasted_iota(jnp.int32, own.shape, 0)
        total_row = lax.broadcasted_iota(jnp.int32, (8, table.shape[0]), 1)
        total_half = lax.broadcasted_iota(jnp.int32, (8, table.shape[0]), 0)
        picked = jnp.where(lax.rem(total_row // 4, 2) == total_half, 1.0, 0.0).astype(low_type)
        item_total_ref[...] = rows_dot(picked, table)
        for part in range(2):
            kept = jnp.where(lax.rem(item // 4, 2) == part, own, 0.0).astype(low_type)
            span = slice(part * (columns // 2), (part + 1) * (columns // 2))
            grad_w_mod_ref[:, span] = left_dot(kept, table)
        chunk = up_ref.shape[3]
        for index in range(4):
            sum_up_ref[:, index * chunk : (index + 1) * chunk] = up_ref[index // 2, index % 2]
        first = first_ref.shape[1]
        second = second_ref.shape[2]
        sum_qkv_ref[:, :first] = first_ref[...]
        for part in range(2):
            at = first + part * second
            sum_qkv_ref[:, at : at + second] = second_ref[part]
            span = slice(part * kv_ref.shape[2], (part + 1) * kv_ref.shape[2])
            sum_kv_ref[:, span] = kv_ref[part]


def row_blocks(array, block=ROW_BLOCK):
    return pl.BlockSpec((block,) + tuple(array.shape[1:]), lambda step, *_: (step, 0))


def column_blocks(array, block=ROW_BLOCK):
    return pl.BlockSpec((array.shape[0], block), lambda step, *_: (0, step))


def shape_of(shape, kind):
    return jax.ShapeDtypeStruct(shape, kind)


MESH = pl.DeviceIdType.MESH


def place(label):
    spot = lax.axis_index("frames")
    side = lax.axis_index("text")
    if label == "text":
        return side, (spot, 1 - side)
    mine = lax.rem(spot // (1 << label), 2)
    return mine, (spot + (1 << label) * (1 - 2 * mine), side)


def greet(labels):
    barrier = pltpu.get_barrier_semaphore()
    for label in labels:
        pl.semaphore_signal(barrier, inc=1, device_id=place(label)[1], device_id_type=MESH)
    pl.semaphore_wait(barrier, len(labels))


class Reduction:
    def __init__(self, labels, hops, source, out, buffers, send, receive, base):
        self.labels, self.hops, self.current, self.out = list(labels), hops, source, out
        self.buffers, self.send, self.receive, self.base = buffers, send, receive, base

    def copy(self, hop):
        kind, label = self.hops[hop]
        mine, peer = place(label)
        source = self.current
        if kind == "split":
            source = source.at[(slice(None),) * self.labels.index(label) + (1 - mine,)]
        return pltpu.make_async_remote_copy(
            src_ref=source,
            dst_ref=self.buffers[hop],
            send_sem=self.send.at[self.base + hop],
            recv_sem=self.receive.at[self.base + hop],
            device_id=peer,
            device_id_type=MESH,
        )

    def start(self, hop):
        if hop < len(self.hops):
            self.copy(hop).start()

    def finish(self, hop):
        if hop >= len(self.hops):
            return
        self.copy(hop).wait()
        kind, label = self.hops[hop]
        mine = place(label)[0]
        buffer, current = self.buffers[hop], self.current
        if kind == "split":
            dim = self.labels.index(label)
            rest = len(self.labels) - 1

            def body(index, _):
                spot = tuple(lax.rem(index // (1 << (rest - 1 - d)), 2) for d in range(rest))
                buffer[spot] = current[spot[:dim] + (mine,) + spot[dim:]] + buffer[spot]
                return 0

            if rest:
                lax.fori_loop(0, 1 << rest, body, 0)
            else:
                buffer[...] = current[mine] + buffer[...]
            self.labels.pop(dim)
            self.current = buffer
            if hop == len(self.hops) - 1:
                self.out[...] = buffer[...]
        elif kind == "swap":
            self.out[...] = buffer[...]
        elif kind == "full":
            self.out[...] = current[...].astype(jnp.float32) + buffer[...].astype(jnp.float32)
        else:
            self.out[mine] = current[...].astype(jnp.float32)
            self.out[1 - mine] = buffer[...].astype(jnp.float32)


class Gathering:
    def __init__(self, hops, source, out, buffer, send, receive, base):
        self.hops, self.source, self.out, self.buffer = hops, source, out, buffer
        self.send, self.receive, self.base = send, receive, base

    def block(self, hop):
        return tuple(place(label)[0] for label in self.hops[hop:][::-1])

    def copy(self, hop):
        where = self.block(hop)
        return pltpu.make_async_remote_copy(
            src_ref=self.buffer.at[where],
            dst_ref=self.buffer.at[where],
            send_sem=self.send.at[self.base + hop],
            recv_sem=self.receive.at[self.base + hop],
            device_id=place(self.hops[hop])[1],
            device_id_type=MESH,
        )

    def start(self, hop):
        if hop == 0:
            self.buffer[self.block(0)] = self.source[...]
        if hop < len(self.hops):
            self.copy(hop).start()

    def finish(self, hop):
        if hop < len(self.hops):
            self.copy(hop).wait()
        if hop == len(self.hops) - 1:
            self.out[...] = self.buffer[...]


def greeted(plans):
    labels = set()
    for names, hops in plans:
        labels |= set(hops) if names is None else {label for _, label in hops}
    return sorted(labels, key=str)


def exchange_parts(arrays, plans):
    outs, scratch, total = [], [], 0
    for array, (labels, hops) in zip(arrays, plans):
        total += len(hops)
        if labels is None:
            shape = (2,) * len(hops) + array.shape
            scratch.append(pltpu.VMEM(shape, array.dtype))
            outs.append(jax.ShapeDtypeStruct(shape, array.dtype))
            continue
        names, shape = list(labels), list(array.shape)
        for kind, label in hops:
            if kind == "split":
                dim = names.index(label)
                names.pop(dim)
                shape.pop(dim)
            scratch.append(pltpu.VMEM(tuple(shape), array.dtype))
        kind = hops[-1][0]
        lead = (2,) if kind == "gather" else ()
        wide = array.dtype if kind in ("split", "swap") else jnp.float32
        outs.append(jax.ShapeDtypeStruct(lead + tuple(shape), wide))
    semaphores = pltpu.SemaphoreType.DMA((total,))
    return outs, scratch + [semaphores, semaphores]


def make_flows(plans, sources, outs, rest):
    send, receive = rest[-2:]
    flows, base, used = [], 0, 0
    for (labels, hops), source, out in zip(plans, sources, outs):
        if labels is None:
            flows.append(Gathering(hops, source, out, rest[used], send, receive, base))
            used += 1
        else:
            buffers = rest[used : used + len(hops)]
            flows.append(Reduction(labels, hops, source, out, buffers, send, receive, base))
            used += len(hops)
        base += len(hops)
    return flows


def with_exchange(kernel, counts, plans, ends, others):
    def body(*refs):
        groups, at = [], 0
        for count in counts:
            groups.append(refs[at : at + count])
            at += count
        scalars, inputs, sources, outputs, targets, scratch, rest = groups
        flows = make_flows(plans, sources, targets, rest)
        step = pl.program_id(0)

        @pl.when(step == 0)
        def _():
            greet(sorted(set(greeted(plans)) | set(others), key=str))
            for flow in flows:
                flow.start(0)

        kernel(*scalars, *inputs, *outputs, *scratch)
        for last in sorted({end for flow_ends in ends for end in flow_ends}):

            @pl.when(step == last)
            def _(last=last):
                for hop in range(max(len(flow_ends) for flow_ends in ends)):
                    for flow, flow_ends in zip(flows, ends):
                        if hop < len(flow_ends) and flow_ends[hop] == last:
                            flow.finish(hop)
                            flow.start(hop + 1)

    return body


def whole(array):
    return pl.BlockSpec(
        array.shape, lambda step, *_: (0,) * len(array.shape), pipeline_mode=pl.Buffered(1)
    )


def run(
    kernel,
    name,
    grid,
    scalars,
    operands,
    specs,
    outs,
    out_specs,
    scratch,
    flops,
    exchange=None,
    transcendentals=0,
    collective=None,
    others=(),
):
    operands, specs, outs = list(operands), list(specs), list(outs)
    out_specs, scratch = list(out_specs), list(scratch)
    traffic = sum(a.size * a.dtype.itemsize for a in operands + outs)
    effects = {}
    if exchange is not None:
        arrays, plans, ends, collective = exchange
        more_outs, more_scratch = exchange_parts(arrays, plans)
        counts = (
            len(scalars),
            len(operands),
            len(arrays),
            len(outs),
            len(more_outs),
            len(scratch),
            len(more_scratch),
        )
        kernel = with_exchange(kernel, counts, plans, ends, others)
        operands += arrays
        specs += [whole(array) for array in arrays]
        outs += more_outs
        out_specs += [whole(array) for array in more_outs]
        scratch += more_scratch
    if collective is not None:
        effects = dict(collective_id=collective, has_side_effects=True)
    return pl.pallas_call(
        kernel,
        out_shape=outs,
        grid_spec=pltpu.PrefetchScalarGridSpec(
            num_scalar_prefetch=len(scalars),
            grid=(grid,),
            in_specs=specs,
            out_specs=out_specs,
            scratch_shapes=scratch,
        ),
        compiler_params=pltpu.CompilerParams(vmem_limit_bytes=VMEM_LIMIT, **effects),
        cost_estimate=pl.CostEstimate(
            flops=flops, transcendentals=transcendentals, bytes_accessed=traffic
        ),
        name=name,
    )(*scalars, *operands)


def idle_kernel():
    pass


def swapped(value):
    return lax.ppermute(value, "text", [(0, 1), (1, 0)])


def on_device(
    frames_in,
    frame_item,
    text_in,
    text_len,
    time_embed,
    cotangent,
    w_mod,
    b_mod,
    w_qkv,
    w_out,
    b_out,
    w_q_cross,
    w_kv_cross,
    w_out_cross,
    b_out_cross,
    w_up,
    b_up,
    w_down,
    b_down,
):
    text_side = lax.axis_index("text")
    partner_side = 1 - text_side
    row_count, width = frames_in.shape
    half = row_count // 2
    hidden_width = w_up.shape[1]
    item_count = time_embed.shape[0]
    token_span = text_in.shape[1]
    token_rows = item_count * 2 * token_span
    share_count = lax.axis_size("frames")
    bits = share_count.bit_length() - 1
    spot = lax.axis_index("frames")
    segment = lax.dynamic_index_in_dim(frame_item, text_side, 0, keepdims=False)
    own_lengths = lax.dynamic_slice_in_dim(text_len, text_side * item_count, item_count)
    item_ids = jnp.arange(item_count, dtype=jnp.int32)

    own_text = lax.dynamic_slice_in_dim(text_in, text_side * item_count, item_count, 0)
    partner_text = lax.dynamic_slice_in_dim(text_in, partner_side * item_count, item_count, 0)
    fetched_text = swapped(partner_text)

    counts = jnp.sum((segment[None, :] == item_ids[:, None]).astype(jnp.int32), axis=1)
    big = jnp.argmax((counts == half).astype(jnp.int32)).astype(jnp.int32)
    start = jnp.sum((segment < big).astype(jnp.int32))
    start_scalar = start.reshape(1)
    segment = jnp.roll(jnp.mod(segment - big, item_count), -start)
    lengths = jnp.roll(own_lengths, -big)
    embedding = jnp.roll(time_embed, -big, axis=0).astype(jnp.float32)
    text = jnp.roll(jnp.concatenate([own_text, fetched_text], axis=1), -big, axis=0)
    text = text.reshape(token_rows, text.shape[2])

    code_column, code_row = segment[:, None], segment[None, :]
    self_codes = (code_column, code_row)
    slot = jnp.arange(2 * token_span, dtype=jnp.int32)
    position = jnp.where(
        slot < token_span,
        text_side * token_span + slot,
        partner_side * token_span + slot - token_span,
    )
    token_code = jnp.where(position[None, :] < lengths[:, None], item_ids[:, None], -1)
    cross_codes = (token_code.reshape(token_rows, 1), code_row)
    pairs = width // LANES
    blocks = row_count // ROW_BLOCK
    matmul_flops = 2 * row_count * width * width

    condition = jax.nn.silu(embedding).astype(low_type)
    mod_items = rows_dot(condition, w_mod) + b_mod.astype(jnp.float32)
    mod = mod_items.reshape(item_count, 8, width)

    def as_row(vector):
        return vector.astype(jnp.float32)[None, :]

    low_rows = shape_of((row_count, width), low_type)
    full_rows = shape_of((row_count, width), jnp.float32)
    square = shape_of((width, width), low_type)
    low_scratch = pltpu.VMEM((row_count, width), low_type)
    full_scratch = pltpu.VMEM((row_count, width), jnp.float32)
    wide_scratch = pltpu.VMEM((row_count + half + 8, width), jnp.float32)

    operands = (frames_in, cotangent, code_column, mod, w_qkv)
    packed_shape = shape_of((row_count, 3 * width), low_type)
    packed, normed_a, frames, upstream = run(
        enter_kernel,
        "enter",
        blocks,
        (start_scalar,),
        operands,
        [whole(frames_in), whole(cotangent), row_blocks(code_column), whole(mod), whole(w_qkv)],
        [packed_shape, low_rows, low_rows, low_rows],
        [row_blocks(packed_shape), row_blocks(low_rows), row_blocks(low_rows), row_blocks(low_rows)],
        [wide_scratch, wide_scratch],
        3 * matmul_flops,
    )
    packed_columns = (pairs, (0, pairs, 2 * pairs, 0))
    attended, self_log = attention_call(
        attend_kernel,
        "self_forward",
        (packed, packed, packed),
        packed_columns,
        self_codes,
        None,
        (row_count, "log"),
        half,
        row_count,
    )
    operands = (attended, frames, code_column, mod, w_out, as_row(b_out), w_q_cross)
    after_a, branch_a, normed_b, cross_q = run(
        middle_kernel,
        "middle",
        blocks,
        (),
        operands,
        [row_blocks(attended), row_blocks(frames), row_blocks(code_column)]
        + [whole(array) for array in operands[3:]],
        [full_rows, full_rows, low_rows, low_rows],
        [row_blocks(full_rows)] * 2 + [row_blocks(low_rows)] * 2,
        [],
        2 * matmul_flops,
    )
    text_kv = rows_dot(text, w_kv_cross).astype(low_type)
    cross_columns = (pairs, (0, 0, pairs, 0))
    cross_out, cross_log = attention_call(
        attend_kernel,
        "cross_forward",
        (cross_q, text_kv, text_kv),
        cross_columns,
        cross_codes,
        None,
        (row_count, "log"),
        2 * token_span,
        token_rows,
    )
    frame_labels = tuple(range(bits))[::-1]
    frame_dims = (2,) * bits
    rest_labels, rest_dims = frame_labels[:-1], frame_dims[:-1]
    low_bits = [("split", bit) for bit in range(1, bits)]

    def shares(array):
        rows, columns = array.shape[-2:]
        return array.reshape(array.shape[:-2] + frame_dims + (rows // share_count, columns))

    def spread(count, low, top):
        return tuple(low + (top - low) * (hop + 1) // count for hop in range(count))

    chunks = 4
    chunk = hidden_width // chunks
    down_share, up_share = hidden_width // share_count, width // share_count
    chunk_pairs, pair_count = chunk // down_share // 2, share_count // 2
    in_core = down_share % 8 == 0 and up_share % 8 == 0
    operands = (
        cross_out,
        after_a,
        upstream,
        code_column,
        code_row,
        mod,
        w_out_cross,
        as_row(b_out_cross),
        as_row(b_down),
        w_up,
        as_row(b_up),
        w_down,
    )
    b_up_shape = shape_of((1, hidden_width), jnp.float32)
    bias_shape = shape_of((8, width), jnp.float32)
    sums_shape = shape_of((3, 8, width), jnp.float32)
    core_scratch = []
    if in_core:
        down_shape = shape_of((chunks, chunk_pairs, down_share, width), low_type)
        up_shape = shape_of((2, 2, pair_count, up_share, chunk), low_type)
        weight_specs = [whole(down_shape), whole(up_shape)]
        core_scratch = [
            pltpu.VMEM((2, chunk_pairs, 2, down_share, width), low_type),
            pltpu.VMEM((2, pair_count, 2, up_share, chunk), low_type),
            pltpu.VMEM((chunks, chunk_pairs, down_share, width), low_type),
            pltpu.VMEM((chunks, pair_count, up_share, chunk), low_type),
            pltpu.SemaphoreType.DMA((chunks, 2)),
            pltpu.SemaphoreType.DMA((chunks, 2)),
        ]
    else:
        down_shape = shape_of((chunks, chunk, width), low_type)
        up_shape = shape_of((chunks, width, chunk), low_type)
        weight_specs = [
            pl.BlockSpec((1,) + shape.shape[1:], lambda step, *_: (step, 0, 0))
            for shape in (down_shape, up_shape)
        ]
    wide_shape = shape_of((row_count + half + 8, width), jnp.float32)
    outs = [wide_shape, full_rows, low_rows, down_shape, up_shape, square]
    outs += [b_up_shape, bias_shape, sums_shape]
    (
        wide_out,
        grad_after_b,
        grad_cross,
        part_down,
        part_up,
        grad_w_out_cross,
        grad_b_up,
        grad_b_mlp,
        sums_c,
    ) = run(
        mlp_kernel,
        "mlp",
        chunks,
        (),
        operands,
        [whole(array) for array in operands[:9]]
        + [
            column_blocks(w_up, chunk),
            column_blocks(operands[10], chunk),
            row_blocks(w_down, chunk),
        ],
        outs,
        [whole(wide_shape), whole(full_rows), whole(low_rows)]
        + weight_specs
        + [
            whole(square),
            column_blocks(b_up_shape, chunk),
            whole(bias_shape),
            whole(sums_shape),
        ],
        [
            low_scratch,
            pltpu.VMEM((width, row_count), low_type),
            low_scratch,
            full_scratch,
            pltpu.VMEM((row_count, chunk), low_type),
            pltpu.VMEM((row_count, chunk), low_type),
        ]
        + core_scratch,
        26 * matmul_flops,
        collective=0 if in_core else None,
    )
    up_labels = ("text", "half")
    if in_core:
        part_down = part_down.reshape(rest_dims + (down_share, width))
        part_up = part_up.reshape((2, 2) + rest_dims + (up_share, chunk))
    else:
        part_down, part_up = run(
            idle_kernel,
            "reduce_core",
            1,
            (),
            (),
            [],
            [],
            [],
            [],
            0,
            (
                [
                    shares(part_down.reshape(hidden_width, width)),
                    shares(part_up.reshape(2, 2, width, chunk)),
                ],
                [(frame_labels, [("split", 0)]), (up_labels + frame_labels, [("split", 0)])],
                [(0,), (0,)],
                6,
            ),
        )

    low_cross_q, grad_text_k, grad_text_v, part_down, part_up = attention_call(
        attend_back_kernel,
        "cross_backward",
        (cross_q, text_kv, text_kv, grad_cross),
        cross_columns,
        cross_codes,
        cross_log,
        (row_count, token_rows, token_rows),
        2 * token_span,
        token_rows,
        (
            [part_down, part_up],
            [(rest_labels, low_bits[:1]), (up_labels + rest_labels, [("split", "text")])],
            [(pairs - 1,), (pairs - 1,)],
            1,
        ),
    )
    half_text = (item_count, token_span, text.shape[1])
    own_shape, sent_shape = shape_of(half_text, jnp.float32), shape_of(half_text, low_type)
    kv_shape = shape_of((2, text.shape[1], width), low_type)
    operands = (grad_text_k, grad_text_v, text, w_kv_cross, wide_out)
    token_block = 2 * token_span
    item_spec = pl.BlockSpec(
        (1,) + half_text[1:], lambda step, big_ref, _: (lax.rem(step + big_ref[0], item_count), 0, 0)
    )
    own_text_grad, sent_text_grad, grad_w_kv, frames_out = run(
        text_back_kernel,
        "text_back",
        item_count,
        (big.reshape(1), start_scalar),
        operands,
        [row_blocks(array, token_block) for array in operands[:3]]
        + [whole(w_kv_cross), whole(wide_out)],
        [own_shape, sent_shape, kv_shape, full_rows],
        [item_spec, item_spec, whole(kv_shape), row_blocks(full_rows, row_count // item_count)],
        [pltpu.VMEM((token_rows, width), low_type)] * 2
        + [pltpu.VMEM((token_rows, text.shape[1]), low_type)],
        4 * 2 * token_rows * width * width,
    )
    operands = (
        low_cross_q,
        normed_b,
        after_a,
        grad_after_b,
        branch_a,
        attended,
        code_column,
        code_row,
        mod,
        w_q_cross,
        w_out,
    )
    (
        grad_after_a,
        grad_attended,
        grad_w_q_cross,
        grad_w_out,
        grad_b_middle,
        sums_b,
        part_down,
        part_up,
        partner_text_grad,
        part_kv,
    ) = run(
        back_middle_kernel,
        "back_middle",
        blocks,
        (),
        operands,
        [row_blocks(array) for array in operands[:7]]
        + [column_blocks(code_row)]
        + [whole(array) for array in operands[8:]],
        [full_rows, low_rows, square, square, bias_shape, sums_shape],
        [row_blocks(full_rows), row_blocks(low_rows), whole(square), whole(square)]
        + [whole(bias_shape), whole(sums_shape)],
        [low_scratch] * 4,
        4 * matmul_flops,
        (
            [part_down, part_up, sent_text_grad, shares(grad_w_kv)],
            [
                (rest_labels[:-1], low_bits[1:2]),
                (("half",) + rest_labels, low_bits[:1]),
                ((), [("swap", "text")]),
                (("text",) + frame_labels, [("split", 0)]),
            ],
            [(blocks - 1,), (blocks - 1,), (blocks - 1,), (1,)],
            2,
        ),
    )
    (
        grad_q,
        grad_k,
        grad_v,
        sum_w_down,
        sum_w_up,
        part_kv,
        part_q_cross,
        part_out_cross,
        part_out,
    ) = attention_call(
        attend_back_kernel,
        "self_backward",
        (packed, packed, packed, grad_attended),
        packed_columns,
        self_codes,
        self_log,
        (row_count, row_count, row_count),
        half,
        row_count,
        (
            [
                part_down,
                part_up,
                part_kv,
                shares(grad_w_q_cross),
                shares(grad_w_out_cross),
                shares(grad_w_out),
            ],
            [
                (rest_labels[:-2], low_bits[2:] + [("full", "text")]),
                (("half",) + rest_labels[:-1], low_bits[1:] + [("gather", "text")]),
                (("text",) + rest_labels, [("split", "text")]),
                (frame_labels, [("split", 0), ("split", 1)]),
                (frame_labels, [("split", 0), ("split", 1)]),
                (frame_labels, [("split", 0), ("split", 1)]),
            ],
            [
                spread(bits - 2, 1, pairs - 1),
                spread(bits - 1, 0, pairs - 1),
                (pairs - 2,),
                (0, pairs - 2),
                (0, pairs - 2),
                (0, pairs - 1),
            ],
            3,
        ),
    )
    operands = (
        grad_q,
        grad_k,
        grad_v,
        normed_a,
        frames,
        grad_after_a,
        code_column,
        code_row,
        mod,
        w_qkv,
    )
    second = 4 * LANES
    first_shape = shape_of((width, 3 * width - 2 * second), low_type)
    second_shape = shape_of((2, width, second), low_type)
    sums_a_shape = shape_of((2, 8, width), jnp.float32)
    (
        wide_grad,
        grad_w_first,
        grad_w_second,
        sums_a,
        part_kv,
        part_q_cross,
        part_out_cross,
        part_out,
    ) = run(
        leave_kernel,
        "leave",
        blocks,
        (),
        operands,
        [row_blocks(array) for array in operands[:7]]
        + [column_blocks(code_row)]
        + [whole(array) for array in operands[8:]],
        [wide_shape, first_shape, second_shape, sums_a_shape],
        [whole(wide_shape), whole(first_shape), whole(second_shape), whole(sums_a_shape)],
        [pltpu.VMEM((row_count, 3 * width), low_type), low_scratch],
        6 * matmul_flops,
        (
            [part_kv, part_q_cross, part_out_cross, part_out],
            [
                (rest_labels, low_bits[:2]),
                (rest_labels[:-1], low_bits[1:2]),
                (rest_labels[:-1], low_bits[1:2]),
                (rest_labels[:-1], low_bits[1:2]),
            ],
            [(1, blocks - 1), (blocks - 1,), (blocks - 1,), (blocks - 1,)],
            4,
        ),
    )

    grad_mod = jnp.concatenate([sums_a, sums_b, sums_c], axis=0)
    low_mod = grad_mod.astype(low_type)
    mod_columns = 8 * width
    mod_table = jnp.transpose(low_mod, (1, 0, 2)).reshape(8, mod_columns)
    embedding_rows = jnp.concatenate([embedding] * (8 // item_count), axis=0)
    table = jnp.roll(jnp.stack([mod_table[:item_count, : mod_columns // 2],
        mod_table[:item_count, mod_columns // 2 :]]), big, axis=1)
    conditions = jnp.roll(condition, big, axis=0)
    halves = jnp.concatenate(
        [
            table.reshape(2 * item_count, mod_columns // 2),
            jnp.concatenate([conditions, conditions], axis=0),
        ],
        axis=1,
    )
    gather_hops = tuple(range(1, bits))[::-1] + ("text", 0)
    bias_parts = [grad_b_middle[0], grad_b_mlp[1], grad_b_up[0], grad_b_mlp[0]]
    bias_table = jnp.concatenate([part.reshape(share_count, -1) for part in bias_parts], axis=1)
    bias_used = bias_table.shape[1]
    bias_table = jnp.pad(bias_table, ((0, 0), (0, 1024 - bias_used)))
    time_rows = shape_of((8, width), jnp.float32)
    first_hops = [("split", 0)] + low_bits + [("full", "text")]
    second_hops = [("split", 0), ("split", "text")] + low_bits + [("gather", "text")]
    steps = 8
    late = steps - 1

    def tail_ends(count, early=()):
        return tuple(early) + (late,) * (count - len(early))

    (
        time_grad,
        sum_kv,
        sum_q_cross,
        sum_out_cross,
        sum_out,
        sum_first,
        sum_second,
        bias_sum,
        all_table,
    ) = run(
        time_kernel,
        "time",
        steps,
        (),
        (mod_table, embedding_rows, w_mod),
        [column_blocks(mod_table, width), whole(embedding_rows), column_blocks(w_mod, width)],
        [time_rows],
        [whole(time_rows)],
        [pltpu.VMEM((8, width), jnp.float32)],
        8 * 2 * 8 * width * width,
        (
            [
                part_kv,
                part_q_cross,
                part_out_cross,
                part_out,
                shares(grad_w_first),
                shares(grad_w_second),
                bias_table.reshape(frame_dims + (8, 128)),
                halves,
            ],
            [
                (rest_labels[:-2], low_bits[2:] + [("gather", "text")]),
                (rest_labels[:-2], low_bits[2:] + [("full", "text")]),
                (rest_labels[:-2], low_bits[2:] + [("full", "text")]),
                (rest_labels[:-2], low_bits[2:] + [("full", "text")]),
                (frame_labels, first_hops),
                (("text",) + frame_labels, second_hops),
                (frame_labels, first_hops),
                (None, gather_hops),
            ],
            [
                tail_ends(bits - 2),
                tail_ends(bits - 2),
                tail_ends(bits - 2),
                tail_ends(bits - 2),
                tail_ends(len(first_hops), (3,)),
                tail_ends(len(second_hops), (3,)),
                tail_ends(len(first_hops), (3,)),
                tail_ends(len(gather_hops), (3,)),
            ],
            5,
        ),
    )
    time_grad = jnp.roll(time_grad[:item_count], big, axis=0)
    bias_sum = bias_sum.reshape(-1)
    all_table = all_table.reshape(-1, halves.shape[1])
    text_pair = item_count // 2
    text_shape = shape_of((2 * item_count,) + half_text[1:], jnp.float32)

    def text_spec(turn):
        return pl.BlockSpec(
            (text_pair,) + half_text[1:],
            (lambda step, *_: (lax.rem(step, 2), 0, 0)) if turn else (lambda step, *_: (step, 0, 0)),
        )

    operands = (
        wide_grad,
        own_text_grad,
        partner_text_grad,
        all_table,
        sum_w_up,
        sum_first,
        sum_second,
        sum_kv,
    )
    mod_shape = shape_of((up_share, mod_columns), jnp.float32)
    total_shape = shape_of((8, mod_columns // 2), jnp.float32)
    sum_up_shape = shape_of((up_share, hidden_width), jnp.float32)
    sum_qkv_shape = shape_of((up_share, 3 * width), jnp.float32)
    sum_kv_shape = shape_of((up_share, 2 * width), jnp.float32)
    more = [mod_shape, total_shape, sum_up_shape, sum_qkv_shape, sum_kv_shape]
    frames_grad, text_grad, grad_w_mod, item_total, sum_w_up, sum_qkv, sum_kv = run(
        finish_kernel,
        "finish",
        4,
        (start_scalar, text_side.reshape(1), spot.reshape(1)),
        operands,
        [whole(wide_grad), text_spec(True), text_spec(True)] + [whole(a) for a in operands[3:]],
        [full_rows, text_shape] + more,
        [row_blocks(full_rows, row_count // 4), text_spec(False)] + [whole(a) for a in more],
        [],
        0,
    )
    grad_b_mod = lax.dynamic_slice_in_dim(
        item_total[:2].reshape(mod_columns),
        spot * (mod_columns // share_count),
        mod_columns // share_count,
    )
    bias_cuts, done = [], 0
    for part in bias_parts:
        size = part.shape[0] // share_count
        bias_cuts.append(bias_sum[done : done + size])
        done += size
    return (
        frames_out,
        frames_grad,
        text_grad,
        time_grad,
        grad_w_mod,
        grad_b_mod,
        sum_qkv,
        sum_out,
        bias_cuts[0],
        sum_q_cross,
        sum_kv,
        sum_out_cross,
        bias_cuts[1],
        sum_w_up,
        bias_cuts[2],
        sum_w_down,
        bias_cuts[3],
    )


def solution(mesh):
    in_specs = (
        P(("frames", "text"), None),
        P("frames", None),
        P("frames", "text", None),
        P("frames"),
        P(("frames", "text"), None),
        P(("frames", "text"), None),
    ) + (P(),) * 13
    out_specs = (
        P(("frames", "text"), None),
        P(("frames", "text"), None),
        P("frames", "text", None),
        P(("frames", "text"), None),
        P("frames", None),
        P("frames"),
        P("frames", None),
        P("frames", None),
        P("frames"),
        P("frames", None),
        P("frames", None),
        P("frames", None),
        P("frames"),
        P("frames", None),
        P("frames"),
        P("frames", None),
        P("frames"),
    )
    return jax.shard_map(
        on_device, mesh=mesh, in_specs=in_specs, out_specs=out_specs, check_vma=False
    )
```

```python
import functools

import jax
import jax.numpy as jnp
from jax import lax
from jax.experimental import pallas as pl
from jax.experimental.pallas import tpu as pltpu
from jax.sharding import PartitionSpec as P

HEAD_DIM = 64
LANES = 128
VMEM_LIMIT = 60 << 20

epsilon = 1e-06
masked_add = -1000000000.0
highest = lax.Precision.HIGHEST
low_type = jnp.bfloat16


def rows_dot(left_side, right_side):
    return jnp.dot(left_side, right_side, preferred_element_type=jnp.float32)


def left_dot(left_side, right_side):
    return lax.dot_general(
        left_side, right_side, (((0,), (0,)), ((), ())), preferred_element_type=jnp.float32
    )


def right_dot(left_side, right_side):
    return lax.dot_general(
        left_side, right_side, (((1,), (1,)), ((), ())), preferred_element_type=jnp.float32
    )


def layer_norm(values):
    center = values - jnp.mean(values, axis=-1, keepdims=True)
    spread = jnp.mean(center * center, axis=-1, keepdims=True)
    return center * lax.rsqrt(spread + epsilon)


def modulate(values, shift_by, scale_by):
    return layer_norm(values) * (1.0 + scale_by) + shift_by


def gelu_tanh(inputs):
    return (
        0.5
        * inputs
        * (1.0 + jnp.tanh(0.7978845608028654 * (inputs + 0.044715 * inputs * inputs * inputs)))
    )


def head_lanes(value, head, scale=None):
    lane = lax.broadcasted_iota(jnp.int32, value.shape, 1)
    scaled = value if scale is None else value * jnp.asarray(scale, value.dtype)
    return jnp.where(lane // HEAD_DIM == head, scaled, jnp.zeros_like(scaled))


def fill_bias(code_column_ref, code_row_ref, bias_refs, key_split):
    half = code_row_ref.shape[1] // 2
    spans = ((0, key_split), (key_split, code_column_ref.shape[0]))
    for part, bias_ref in enumerate(bias_refs):
        if bias_ref is None:
            continue
        low, top = spans[part]
        bias_ref[...] = jnp.where(
            code_column_ref[low:top, :] == code_row_ref[:, part * half : (part + 1) * half],
            0.0,
            masked_add,
        )


def attend_kernel(
    q_ref, k_ref, v_ref, code_column_ref, code_row_ref, out_ref, log_ref, *bias_refs, key_split
):
    half = q_ref.shape[0] // 2
    scale = HEAD_DIM ** (-0.5)
    if len(bias_refs) == 1:
        bias_refs = (None,) + bias_refs

    @pl.when(pl.program_id(0) == 0)
    def _():
        fill_bias(code_column_ref, code_row_ref, bias_refs, key_split)

    value_t = v_ref[...].T
    key_spans = (slice(0, key_split), slice(key_split, k_ref.shape[0]))
    units = [(part, head) for part in range(2) for head in range(2)]

    def scores_of(part, head):
        queries = q_ref[part * half : (part + 1) * half, :]
        scores = right_dot(k_ref[key_spans[part], :], head_lanes(queries, head, scale))
        return scores if bias_refs[part] is None else scores + bias_refs[part][...]

    ahead = scores_of(*units[0])
    outs = []
    for index, (part, head) in enumerate(units):
        scores = ahead
        if index + 1 < len(units):
            ahead = scores_of(*units[index + 1])
        rows = slice(part * half, (part + 1) * half)
        peak = jnp.max(scores, axis=0, keepdims=True)
        exponent = jnp.exp(scores - peak)
        total = jnp.sum(exponent, axis=0, keepdims=True)
        log_ref[0, head : head + 1, rows] = peak + jnp.log(total)
        lanes = slice(HEAD_DIM * head, HEAD_DIM * (head + 1))
        outs.append(
            rows_dot(value_t[lanes, key_spans[part]], exponent.astype(low_type)) / total
        )
        if head == 1:
            out_ref[rows, :] = jnp.concatenate(outs, axis=0).T.astype(low_type)
            outs = []


def attend_back_kernel(
    q_ref,
    k_ref,
    v_ref,
    grad_ref,
    log_ref,
    code_column_ref,
    code_row_ref,
    grad_q_ref,
    grad_k_ref,
    grad_v_ref,
    *bias_refs,
    key_split,
):
    half = q_ref.shape[0] // 2
    scale = HEAD_DIM ** (-0.5)
    if len(bias_refs) == 1:
        bias_refs = (None,) + bias_refs

    @pl.when(pl.program_id(0) == 0)
    def _():
        fill_bias(code_column_ref, code_row_ref, bias_refs, key_split)

    key_t = k_ref[...].T
    key_spans = (slice(0, key_split), slice(key_split, k_ref.shape[0]))
    units = [(part, head) for part in range(2) for head in range(2)]

    def products_of(part, head):
        rows = slice(part * half, (part + 1) * half)
        query_head = head_lanes(q_ref[rows, :], head, scale)
        grad_head = head_lanes(grad_ref[rows, :], head)
        scores = right_dot(k_ref[key_spans[part], :], query_head)
        if bias_refs[part] is not None:
            scores = scores + bias_refs[part][...]
        grad_prob = right_dot(v_ref[key_spans[part], :], grad_head)
        return scores, grad_prob, query_head, grad_head

    ahead = products_of(*units[0])
    grad_q, grad_k, grad_v = [], [], []
    for index, (part, head) in enumerate(units):
        scores, grad_prob, query_head, grad_head = ahead
        if index + 1 < len(units):
            ahead = products_of(*units[index + 1])
        rows = slice(part * half, (part + 1) * half)
        prob = jnp.exp(scores - log_ref[0, head : head + 1, rows])
        weighted = prob * grad_prob
        delta = jnp.sum(weighted, axis=0, keepdims=True)
        grad_scores = (weighted - prob * delta).astype(low_type)
        grad_k.append(rows_dot(grad_scores, query_head))
        grad_v.append(rows_dot(prob.astype(low_type), grad_head))
        lanes = slice(HEAD_DIM * head, HEAD_DIM * (head + 1))
        grad_q.append(rows_dot(key_t[lanes, key_spans[part]], grad_scores) * scale)
        if head == 1:
            grad_q_ref[rows, :] = jnp.concatenate(grad_q, axis=0).T.astype(low_type)
            grad_k_ref[key_spans[part], :] = (grad_k[0] + grad_k[1]).astype(low_type)
            grad_v_ref[key_spans[part], :] = (grad_v[0] + grad_v[1]).astype(low_type)
            grad_q, grad_k, grad_v = [], [], []


def attention_call(
    kernel, name, operands, columns, codes, log_total, outs, key_split, key_rows, exchange=None
):
    rows = codes[1].shape[1]
    half = rows // 2
    pairs, offsets = columns
    specs = [
        pl.BlockSpec((array.shape[0], LANES), lambda step, offset=offset: (0, offset + step))
        for array, offset in zip(operands, offsets)
    ]
    extra = []
    log_spec = pl.BlockSpec((1, 8, rows), lambda step: (step, 0, 0))
    if log_total is not None:
        specs.append(log_spec)
        extra.append(log_total)
    specs += [whole(code) for code in codes]
    out_shape, out_specs = [], []
    for count in outs:
        if count == "log":
            out_shape.append(jax.ShapeDtypeStruct((pairs, 8, rows), jnp.float32))
            out_specs.append(log_spec)
        else:
            out_shape.append(jax.ShapeDtypeStruct((count, pairs * LANES), low_type))
            out_specs.append(pl.BlockSpec((count, LANES), lambda step: (0, step)))
    scratch = [pltpu.VMEM((key_rows - key_split, half), jnp.float32)]
    if key_split != half:
        scratch = [pltpu.VMEM((key_split, half), jnp.float32)] + scratch
    products = 2 if log_total is None else 5
    cells = half * key_rows
    return run(
        functools.partial(kernel, key_split=key_split),
        name,
        pairs,
        (),
        list(operands) + extra + list(codes),
        specs,
        out_shape,
        out_specs,
        scratch,
        products * pairs * 2 * cells * 256 * 2,
        exchange,
        pairs * 2 * cells,
    )


ROW_BLOCK = 256
SHIFT_A, SCALE_A, GATE_A, SHIFT_B, SCALE_B, SHIFT_C, SCALE_C, GATE_C = range(8)


def item_rows(mod_ref, part, code):
    out = mod_ref[0, part : part + 1, :]
    for item in range(1, mod_ref.shape[0]):
        out = jnp.where(code == item, mod_ref[item, part : part + 1, :], out)
    return out


def item_mask(code_row):
    ids = lax.broadcasted_iota(jnp.int32, (8, code_row.shape[1]), 0)
    return jnp.where(ids == code_row, 1.0, 0.0).astype(low_type)


def item_sums(mask, values):
    high = values.astype(low_type)
    rest = (values - high.astype(jnp.float32)).astype(low_type)
    return rows_dot(mask, high) + rows_dot(mask, rest)


def column_sum(values):
    return jnp.sum(values, axis=0, keepdims=True)


def normed_of(values):
    center = values - jnp.mean(values, axis=-1, keepdims=True)
    spread = jnp.mean(center * center, axis=-1, keepdims=True)
    inverse = lax.rsqrt(spread + epsilon)
    return center * inverse, inverse


def normed_back(grad, scale_by, normed, inverse):
    inner = grad * (1.0 + scale_by)
    return inverse * (
        inner
        - jnp.mean(inner, axis=-1, keepdims=True)
        - normed * jnp.mean(inner * normed, axis=-1, keepdims=True)
    )


def rolled_rows(source_ref, wide_ref):
    rows = source_ref.shape[0]
    wide_ref[:rows, :] = source_ref[...].astype(jnp.float32)
    wide_ref[rows : rows + rows // 2, :] = source_ref[: rows // 2, :].astype(jnp.float32)


def rows_from(wide_ref, first, offset, count):
    rest = lax.rem(first, 8)
    where = pl.ds(pl.multiple_of(first - rest + offset, 8), count + 8)
    rows = wide_ref[where, :].reshape(count // 8 + 1, 8, wide_ref.shape[1])
    turned = pltpu.roll(rows, lax.rem(8 - rest, 8), 1)
    near = lax.broadcasted_iota(jnp.int32, (1, 8, wide_ref.shape[1]), 1) < 8 - rest
    return jnp.where(near, turned[:-1], turned[1:]).reshape(count, wide_ref.shape[1])


def enter_kernel(
    start_ref,
    frames_ref,
    cotangent_ref,
    code_ref,
    mod_ref,
    w_qkv_ref,
    packed_ref,
    normed_ref,
    frames_out_ref,
    cotangent_out_ref,
    wide_frames,
    wide_cotangent,
):
    step = pl.program_id(0)
    block = packed_ref.shape[0]

    @pl.when(step == 0)
    def _():
        rolled_rows(frames_ref, wide_frames)
        rolled_rows(cotangent_ref, wide_cotangent)

    frames = rows_from(wide_frames, start_ref[0], step * block, block)
    frames_out_ref[...] = frames.astype(low_type)
    cotangent_out_ref[...] = rows_from(wide_cotangent, start_ref[0], step * block, block).astype(
        low_type
    )
    code = code_ref[...]
    normed, _ = normed_of(frames)
    modulated = normed * (1.0 + item_rows(mod_ref, SCALE_A, code)) + item_rows(
        mod_ref, SHIFT_A, code
    )
    low = modulated.astype(low_type)
    normed_ref[...] = low
    packed_ref[...] = rows_dot(low, w_qkv_ref[...]).astype(low_type)


def middle_kernel(
    attended_ref,
    frames_ref,
    code_ref,
    mod_ref,
    w_out_ref,
    b_out_ref,
    w_q_ref,
    after_ref,
    branch_ref,
    normed_ref,
    cross_q_ref,
):
    code = code_ref[...]
    branch = rows_dot(attended_ref[...], w_out_ref[...]) + b_out_ref[...]
    branch_ref[...] = branch
    after = frames_ref[...].astype(jnp.float32) + item_rows(mod_ref, GATE_A, code) * branch
    after_ref[...] = after
    normed, _ = normed_of(after)
    low = (
        normed * (1.0 + item_rows(mod_ref, SCALE_B, code)) + item_rows(mod_ref, SHIFT_B, code)
    ).astype(low_type)
    normed_ref[...] = low
    cross_q_ref[...] = rows_dot(low, w_q_ref[...]).astype(low_type)


GELU_FACTOR = 0.7978845608028654
GELU_CUBE = 0.044715


def gelu_both(inputs):
    square = inputs * inputs
    bend = jnp.tanh(inputs * (GELU_FACTOR + (GELU_FACTOR * GELU_CUBE) * square))
    half_up = 0.5 + 0.5 * bend
    slope = half_up + (0.5 * inputs) * (1.0 - bend * bend) * (
        GELU_FACTOR + (3.0 * GELU_FACTOR * GELU_CUBE) * square
    )
    return inputs * half_up, slope


def remote(source, target, send, receive, peer):
    return pltpu.make_async_remote_copy(
        src_ref=source,
        dst_ref=target,
        send_sem=send,
        recv_sem=receive,
        device_id=peer,
        device_id_type=MESH,
    )


def fill_table(table_ref, sums_ref):
    parts, _, width = sums_ref.shape
    items = table_ref.shape[0] // 2
    flat = jnp.concatenate([sums_ref[part, :items, :] for part in range(parts)], axis=1)
    middle = parts * width // 2
    both = jnp.concatenate([flat[:, :middle], flat[:, middle:]], axis=0)
    table_ref[:, :middle] = both.astype(low_type)


def mlp_kernel(
    cross_out_ref,
    after_a_ref,
    cotangent_ref,
    code_ref,
    code_row_ref,
    mod_ref,
    w_out_cross_ref,
    b_out_cross_ref,
    b_down_ref,
    w_up_ref,
    b_up_ref,
    w_down_ref,
    condition_ref,
    wide,
    grad_after_ref,
    grad_cross_ref,
    grad_w_down_ref,
    grad_w_up_ref,
    grad_w_out_cross_ref,
    grad_b_ref,
    sums_ref,
    table_ref,
    normed_c,
    normed_c_t,
    low_branch,
    back_sum,
    active,
    low_hidden,
    *core,
):
    after_b = grad_after_ref
    step = pl.program_id(0)
    steps = pl.num_programs(0)
    rows = cross_out_ref.shape[0]
    half = rows // 2
    block = ROW_BLOCK
    blocks = rows // block

    def span(index):
        return pl.ds(pl.multiple_of(index * block, block), block)

    def after_half(index):
        return pl.ds(pl.multiple_of(half + index * block, block), block)

    def core_copies(index):
        down, up, down_in, up_in, down_next, up_next, send, receive = core
        mine, peer = place(0)
        slot = lax.rem(index, 2)
        ends = ((down.at[slot, :, :, 1 - mine], down_in), (up.at[slot, :, 1 - mine], up_in))
        return [
            remote(out, into.at[index], send.at[index, which], receive.at[index, which], peer)
            for which, (out, into) in enumerate(ends)
        ]

    def next_copies(index):
        down, up, down_in, up_in, down_next, up_next, send, receive = core
        bit, across = place(1)
        side, beside = place("text")
        return [
            remote(
                down_in.at[index, :, 1 - bit],
                down_next.at[index],
                send.at[index, 2],
                receive.at[index, 2],
                across,
            ),
            remote(
                up_in.at[index, :, 1 - side],
                up_next.at[index],
                send.at[index, 3],
                receive.at[index, 3],
                beside,
            ),
        ]

    def settle(index):
        down, up, down_in, up_in = core[:4]
        mine = place(0)[0]
        slot = lax.rem(index, 2)
        for copy in core_copies(index):
            copy.wait()
        down_in[index] = down[slot, :, :, mine] + down_in[index]
        up_in[index] = up[slot, :, mine] + up_in[index]
        for copy in next_copies(index):
            copy.start()

    def finish(index):
        down_in, up_in, down_next, up_next = core[2:6]
        for copy in next_copies(index):
            copy.wait()
        grad_w_down_ref[index] = down_in[index, :, place(1)[0]] + down_next[index]
        grad_w_up_ref[index] = up_in[index, :, place("text")[0]] + up_next[index]

    @pl.when(step == 0)
    def _():
        if core:
            greet([0, 1, "text"])
            meet([0, 1, "text"])

        def body(index, _):
            where = span(index)
            code = code_ref[where, :]
            branch = rows_dot(cross_out_ref[where, :], w_out_cross_ref[...]) + b_out_cross_ref[...]
            after = after_a_ref[where, :] + branch
            after_b[where, :] = after
            normed, _ = normed_of(after)
            normed_c[where, :] = (
                normed * (1.0 + item_rows(mod_ref, SCALE_C, code))
                + item_rows(mod_ref, SHIFT_C, code)
            ).astype(low_type)
            low_branch[where, :] = (
                item_rows(mod_ref, GATE_C, code) * cotangent_ref[where, :].astype(jnp.float32)
            ).astype(low_type)
            wide[after_half(index), :] = jnp.zeros((block, wide.shape[1]), jnp.float32)
            back_sum[where, :] = jnp.zeros((block, back_sum.shape[1]), jnp.float32)
            return 0

        lax.fori_loop(0, blocks, body, 0)
        normed_c_t[...] = normed_c[...].T

    def products_of(index):
        where = pl.ds(index * block, block)
        hidden = rows_dot(normed_c[where, :], w_up_ref[...]) + b_up_ref[...]
        return hidden, right_dot(low_branch[where, :], w_down_ref[...])

    bias_total = jnp.zeros((1, w_up_ref.shape[1]), jnp.float32)
    ahead = products_of(0)
    for index in range(blocks):
        where = pl.ds(index * block, block)
        hidden, grad_active = ahead
        if index + 1 < blocks:
            ahead = products_of(index + 1)
        value, slope = gelu_both(hidden)
        low_value = value.astype(low_type)
        active[where, :] = low_value
        grad_hidden = slope * grad_active
        bias_total = bias_total + column_sum(grad_hidden)
        low = grad_hidden.astype(low_type)
        low_hidden[where, :] = low
        wide[after_half(index), :] += rows_dot(low_value, w_down_ref[...])
        back_sum[where, :] += right_dot(low, w_up_ref[...])

    @pl.when(step == 0)
    def _():
        grad_b_ref[...] = jnp.zeros(grad_b_ref.shape, jnp.float32)

    grad_b_ref[pl.ds(2 + step, 1), :] = bias_total
    down_part = left_dot(active[...], low_branch[...]).astype(low_type)
    up_part = rows_dot(normed_c_t[...], low_hidden[...]).astype(low_type)
    if core:
        slot = lax.rem(step, 2)
        core[0][slot] = down_part.reshape(core[0].shape[1:])
        core[1][slot] = up_part.reshape(core[1].shape[1:])
        for copy in core_copies(step):
            copy.start()

        @pl.when(step > 0)
        def _():
            settle(step - 1)

        @pl.when(step > 1)
        def _():
            finish(step - 2)
    else:
        grad_w_down_ref[0] = down_part
        grad_w_up_ref[0] = up_part

    @pl.when(step == steps - 1)
    def _():
        sums_ref[...] = jnp.zeros(sums_ref.shape, jnp.float32)

        def body(index, _):
            where = span(index)
            code = code_ref[where, :]
            mask = item_mask(code_row_ref[:, where])
            upstream = cotangent_ref[where, :].astype(jnp.float32)
            branch = wide[after_half(index), :] + b_down_ref[...]
            gate = item_rows(mod_ref, GATE_C, code)
            after = after_b[where, :]
            out = after + gate * branch
            wide[after_half(index), :] = out

            @pl.when(index >= blocks // 2)
            def _():
                wide[pl.ds(pl.multiple_of(index * block - half, block), block), :] = out

            sums_ref[2] += item_sums(mask, upstream * branch)
            grad_b_ref[0:1, :] += column_sum(gate * upstream)
            normed, inverse = normed_of(after)
            grad = back_sum[where, :]
            sums_ref[0] += item_sums(mask, grad)
            sums_ref[1] += item_sums(mask, grad * normed)
            total = upstream + normed_back(
                grad, item_rows(mod_ref, SCALE_C, code), normed, inverse
            )
            grad_after_ref[where, :] = total
            grad_b_ref[1:2, :] += column_sum(total)
            low = total.astype(low_type)
            low_branch[where, :] = low
            grad_cross_ref[where, :] = right_dot(low, w_out_cross_ref[...]).astype(low_type)
            return 0

        lax.fori_loop(0, blocks // 2, body, 0)
        if core:
            settle(step)
        lax.fori_loop(blocks // 2, blocks, body, 0)
        grad_w_out_cross_ref[...] = left_dot(cross_out_ref[...], low_branch[...]).astype(low_type)
        fill_table(table_ref, sums_ref)
        table_ref[:, table_ref.shape[1] - condition_ref.shape[1] :] = condition_ref[...]
        if core:
            finish(step - 1)
            finish(step)


def text_back_kernel(
    big_ref,
    start_ref,
    grad_k_ref,
    grad_v_ref,
    text_ref,
    w_kv_ref,
    wide_ref,
    own_ref,
    sent_ref,
    grad_w_ref,
    frames_out_ref,
    all_k,
    all_v,
    all_text,
):
    step = pl.program_id(0)
    rows = frames_out_ref.shape[0]
    half = pl.num_programs(0) * rows // 2
    frames_out_ref[...] = rows_from(wide_ref, half - start_ref[0], step * rows, rows)
    block, width = grad_k_ref.shape
    span = own_ref.shape[1]
    where = pl.ds(pl.multiple_of(step * block, block), block)
    keys, values = grad_k_ref[...], grad_v_ref[...]
    all_k[where, :] = keys
    all_v[where, :] = values
    all_text[where, :] = text_ref[...]
    total = right_dot(keys, w_kv_ref[:, :width]) + right_dot(values, w_kv_ref[:, width:])
    own_ref[0] = total[:span]
    sent_ref[0] = total[span:].astype(low_type)

    @pl.when(step == pl.num_programs(0) - 1)
    def _():
        text_t = all_text[...].T
        grad_w_ref[0] = rows_dot(text_t, all_k[...]).astype(low_type)
        grad_w_ref[1] = rows_dot(text_t, all_v[...]).astype(low_type)


def back_middle_kernel(
    low_q_ref,
    normed_b_ref,
    after_a_ref,
    grad_after_b_ref,
    branch_ref,
    attended_ref,
    code_ref,
    code_row_ref,
    mod_ref,
    w_q_ref,
    w_out_ref,
    bias_mlp_ref,
    grad_after_ref,
    grad_attended_ref,
    grad_w_q_ref,
    grad_w_out_ref,
    grad_b_ref,
    sums_ref,
    table_ref,
    all_q,
    all_normed,
    all_attended,
    all_branch,
):
    step = pl.program_id(0)
    block = low_q_ref.shape[0]

    @pl.when(step == 0)
    def _():
        sums_ref[...] = jnp.zeros(sums_ref.shape, jnp.float32)
        grad_b_ref[...] = jnp.zeros(grad_b_ref.shape, jnp.float32)

    where = pl.ds(pl.multiple_of(step * block, block), block)
    code = code_ref[...]
    mask = item_mask(code_row_ref[...])
    low_q = low_q_ref[...]
    all_q[where, :] = low_q
    all_normed[where, :] = normed_b_ref[...]
    all_attended[where, :] = attended_ref[...]
    grad = right_dot(low_q, w_q_ref[...])
    normed, inverse = normed_of(after_a_ref[...])
    sums_ref[1] += item_sums(mask, grad)
    sums_ref[2] += item_sums(mask, grad * normed)
    total = grad_after_b_ref[...] + normed_back(
        grad, item_rows(mod_ref, SCALE_B, code), normed, inverse
    )
    grad_after_ref[...] = total
    sums_ref[0] += item_sums(mask, total * branch_ref[...])
    grad_branch = item_rows(mod_ref, GATE_A, code) * total
    grad_b_ref[0:1, :] += column_sum(grad_branch)
    low = grad_branch.astype(low_type)
    all_branch[where, :] = low
    grad_attended_ref[...] = right_dot(low, w_out_ref[...]).astype(low_type)

    @pl.when(step == pl.num_programs(0) - 1)
    def _():
        grad_w_q_ref[...] = left_dot(all_normed[...], all_q[...]).astype(low_type)
        weight = left_dot(all_attended[...], all_branch[...]).astype(low_type)
        fill_table(table_ref, sums_ref)
        grad_b_ref[1:, :] = bias_mlp_ref[:-1, :]
        if len(grad_w_out_ref.shape) == 2:
            grad_w_out_ref[...] = weight
        else:
            shares, rows = grad_w_out_ref.shape[0], grad_w_out_ref.shape[1] - 16
            grad_w_out_ref[:, :rows, :] = weight.reshape(shares, rows, weight.shape[1])
            grad_w_out_ref[:, rows:, :] = jnp.broadcast_to(
                jnp.concatenate([grad_b_ref[...]] * 2, axis=0).astype(low_type)[None],
                (shares, 16, weight.shape[1]),
            )


def leave_kernel(
    grad_q_ref,
    grad_k_ref,
    grad_v_ref,
    frames_ref,
    grad_after_ref,
    code_ref,
    code_row_ref,
    mod_ref,
    w_qkv_ref,
    sums_b_ref,
    sums_c_ref,
    embedding_ref,
    w_mod_ref,
    wide,
    table_ref,
    time_ref,
    sums_ref,
    low_sums,
    total,
):
    step = pl.program_id(0)
    block, width = grad_q_ref.shape
    parts = low_sums.shape[0]
    blocks = pl.num_programs(0) - parts
    half = blocks * block // 2

    @pl.when(step == 0)
    def _():
        sums_ref[...] = jnp.zeros(sums_ref.shape, jnp.float32)
        total[...] = jnp.zeros_like(total)

    @pl.when(step < blocks)
    def _():
        code = code_ref[...]
        mask = item_mask(code_row_ref[...])
        grad = jnp.zeros((block, width), jnp.float32)
        for index, ref in enumerate((grad_q_ref, grad_k_ref, grad_v_ref)):
            grad = grad + right_dot(ref[...], w_qkv_ref[:, index * width : (index + 1) * width])
        normed, inverse = normed_of(frames_ref[...].astype(jnp.float32))
        sums_ref[0] += item_sums(mask, grad)
        sums_ref[1] += item_sums(mask, grad * normed)
        out = grad_after_ref[...] + normed_back(
            grad, item_rows(mod_ref, SCALE_A, code), normed, inverse
        )
        wide[pl.ds(pl.multiple_of(half + step * block, block), block), :] = out

        @pl.when(step >= blocks // 2)
        def _():
            wide[pl.ds(pl.multiple_of(step * block - half, block), block), :] = out

    @pl.when(step == blocks - 1)
    def _():
        fill_table(table_ref, sums_ref)
        at = 0
        for ref in (sums_ref, sums_b_ref, sums_c_ref):
            low_sums[at : at + ref.shape[0]] = ref[...].astype(low_type)
            at += ref.shape[0]

    @pl.when(step >= blocks)
    def _():
        total[...] += right_dot(low_sums[jnp.maximum(step - blocks, 0)], w_mod_ref[...])

    @pl.when(step == pl.num_programs(0) - 1)
    def _():
        embedding = embedding_ref[...]
        gate = 1.0 / (1.0 + jnp.exp(-embedding))
        time_ref[...] = total[...] * (gate + embedding * gate * (1.0 - gate))


def self_back_kernel(
    q_ref,
    k_ref,
    v_ref,
    grad_ref,
    log_ref,
    code_column_ref,
    code_row_ref,
    normed_ref,
    grad_q_ref,
    grad_k_ref,
    grad_v_ref,
    out_even_ref,
    out_odd_ref,
    bias_ref,
    normed_t,
    *core,
    key_split,
    met,
):
    step = pl.program_id(0)

    @pl.when(step == 0)
    def _():
        normed_t[...] = normed_ref[...].T

    attend_back_kernel(
        q_ref,
        k_ref,
        v_ref,
        grad_ref,
        log_ref,
        code_column_ref,
        code_row_ref,
        grad_q_ref,
        grad_k_ref,
        grad_v_ref,
        bias_ref,
        key_split=key_split,
    )
    pieces = jnp.concatenate([grad_q_ref[...], grad_k_ref[...], grad_v_ref[...]], axis=1)
    weight = rows_dot(normed_t[...], pieces).astype(low_type)
    if not core:
        out_even_ref[0] = weight
        return
    part, part_in, send, receive = core

    def core_copy(index):
        mine, peer = place(0)
        return remote(
            part.at[lax.rem(index, 2), :, :, 1 - mine],
            part_in.at[index],
            send.at[index],
            receive.at[index],
            peer,
        )

    def settle(index):
        core_copy(index).wait()
        total = part[lax.rem(index, 2), :, :, place(0)[0]] + part_in[index]

        @pl.when(lax.rem(index, 2) == 0)
        def _():
            out_even_ref[:, :, index // 2] = total

        @pl.when(lax.rem(index, 2) == 1)
        def _():
            for side in range(2):
                out_odd_ref[:, :, side, index // 2] = total[:, :, side]

    part[lax.rem(step, 2)] = weight.reshape(part.shape[1:])

    @pl.when(step == 0)
    def _():
        meet(met)

    core_copy(step).start()

    @pl.when(step > 0)
    def _():
        settle(step - 1)

    @pl.when(step == pl.num_programs(0) - 1)
    def _():
        settle(step)


def finish_kernel(
    start_ref,
    side_ref,
    spot_ref,
    wide_ref,
    own_ref,
    partner_ref,
    table_a_ref,
    table_b_ref,
    table_c_ref,
    up_ref,
    even_ref,
    odd_ref,
    kv_ref,
    frames_grad_ref,
    text_grad_ref,
    grad_w_mod_ref,
    item_total_ref,
    sum_up_ref,
    sum_qkv_ref,
    sum_kv_ref,
):
    tables = (table_a_ref, table_b_ref, table_c_ref)
    step = pl.program_id(0)
    rows = frames_grad_ref.shape[0]
    half = pl.num_programs(0) * rows // 2
    frames_grad_ref[...] = rows_from(wide_ref, half - start_ref[0], step * rows, rows)
    mine = step // (pl.num_programs(0) // 2) == side_ref[0]

    @pl.when(mine)
    def _():
        text_grad_ref[...] = own_ref[...]

    @pl.when(jnp.logical_not(mine))
    def _():
        text_grad_ref[...] = partner_ref[...].astype(jnp.float32)

    @pl.when(step == 0)
    def _():
        share, columns = grad_w_mod_ref.shape
        width = columns // 8
        entry = lax.broadcasted_iota(jnp.int32, (width, share), 0)
        wanted = lax.broadcasted_iota(jnp.int32, (width, share), 1) + spot_ref[0] * share
        chosen = jnp.where(entry == wanted, 1.0, 0.0).astype(low_type)
        own = rows_dot(tables[2][:, tables[2].shape[1] - width :], chosen)
        item = lax.broadcasted_iota(jnp.int32, own.shape, 0)
        shape = (8, tables[2].shape[0])
        row_half = lax.rem(lax.broadcasted_iota(jnp.int32, shape, 1) // 4, 2)
        picked = jnp.where(row_half == lax.broadcasted_iota(jnp.int32, shape, 0), 1.0, 0.0).astype(
            low_type
        )
        kept = [
            jnp.where(lax.rem(item // 4, 2) == part, own, 0.0).astype(low_type) for part in range(2)
        ]
        at = 0
        for table_ref, parts in zip(tables, (2, 3, 3)):
            cut = parts * width // 2
            table = table_ref[:, :cut]
            totals = rows_dot(picked, table)
            for part in range(2):
                grad_w_mod_ref[:, at : at + cut] = left_dot(kept[part], table)
                item_total_ref[:, at : at + cut] = totals[part : part + 1]
                at += cut
        chunk = up_ref.shape[3]
        for index in range(up_ref.shape[1]):
            for side in range(2):
                rows_here = slice(side * up_ref.shape[2], (side + 1) * up_ref.shape[2])
                sum_up_ref[rows_here, index * chunk : (index + 1) * chunk] = up_ref[side, index]
        piece = even_ref.shape[2] // 3
        for index in range(2 * even_ref.shape[0]):
            for kind in range(3):
                span = slice(kind * width + index * piece, kind * width + (index + 1) * piece)
                cut = slice(kind * piece, (kind + 1) * piece)
                if index % 2 == 0:
                    sum_qkv_ref[:, span] = even_ref[index // 2, :, cut]
                    continue
                for side in range(2):
                    rows_here = slice(side * odd_ref.shape[2], (side + 1) * odd_ref.shape[2])
                    sum_qkv_ref[rows_here, span] = odd_ref[side, index // 2, :, cut]
        for part in range(2):
            sum_kv_ref[:, part * width : (part + 1) * width] = kv_ref[part]


def row_blocks(array, block=ROW_BLOCK):
    return pl.BlockSpec((block,) + tuple(array.shape[1:]), lambda step, *_: (step, 0))


def column_blocks(array, block=ROW_BLOCK):
    return pl.BlockSpec((array.shape[0], block), lambda step, *_: (0, step))


def shape_of(shape, kind):
    return jax.ShapeDtypeStruct(shape, kind)


MESH = pl.DeviceIdType.MESH


def place(label):
    spot = lax.axis_index("frames")
    side = lax.axis_index("text")
    if label == "text":
        return side, (spot, 1 - side)
    mine = lax.rem(spot // (1 << label), 2)
    return mine, (spot + (1 << label) * (1 - 2 * mine), side)


def greet(labels):
    for label in labels:
        pl.semaphore_signal(
            pltpu.get_barrier_semaphore(),
            inc=1,
            device_id=place(label)[1],
            device_id_type=MESH,
        )


def meet(labels):
    pl.semaphore_wait(pltpu.get_barrier_semaphore(), len(labels))


class Reduction:
    def __init__(self, labels, hops, source, out, buffers, send, receive, base):
        self.labels, self.hops, self.current, self.out = list(labels), hops, source, out
        self.buffers, self.send, self.receive, self.base = buffers, send, receive, base

    def copy(self, hop):
        kind, label = self.hops[hop]
        mine, peer = place(label)
        source = self.current
        if kind == "split":
            source = source.at[(slice(None),) * self.labels.index(label) + (1 - mine,)]
        return pltpu.make_async_remote_copy(
            src_ref=source,
            dst_ref=self.buffers[hop],
            send_sem=self.send.at[self.base + hop],
            recv_sem=self.receive.at[self.base + hop],
            device_id=peer,
            device_id_type=MESH,
        )

    def start(self, hop):
        if hop < len(self.hops):
            self.copy(hop).start()

    def finish(self, hop):
        if hop >= len(self.hops):
            return
        self.copy(hop).wait()
        kind, label = self.hops[hop]
        mine = place(label)[0]
        buffer, current = self.buffers[hop], self.current
        if kind == "split":
            dim = self.labels.index(label)
            rest = len(self.labels) - 1

            def body(index, _):
                spot = tuple(lax.rem(index // (1 << (rest - 1 - d)), 2) for d in range(rest))
                buffer[spot] = current[spot[:dim] + (mine,) + spot[dim:]] + buffer[spot]
                return 0

            if rest:
                lax.fori_loop(0, 1 << rest, body, 0)
            else:
                buffer[...] = current[mine] + buffer[...]
            self.labels.pop(dim)
            self.current = buffer
            if hop == len(self.hops) - 1:
                self.out[...] = buffer[...]
        elif kind == "sum":
            buffer[...] = current[...] + buffer[...]
            self.current = buffer
            if hop == len(self.hops) - 1:
                self.out[...] = buffer[...]
        elif kind == "swap":
            self.out[...] = buffer[...]
        elif kind == "full":
            self.out[...] = current[...].astype(jnp.float32) + buffer[...].astype(jnp.float32)
        else:
            self.out[mine] = current[...].astype(jnp.float32)
            self.out[1 - mine] = buffer[...].astype(jnp.float32)


class Gathering:
    def __init__(self, hops, source, out, buffer, send, receive, base):
        self.hops, self.source, self.out, self.buffer = hops, source, out, buffer
        self.send, self.receive, self.base = send, receive, base

    def block(self, hop):
        return tuple(place(label)[0] for label in self.hops[hop:][::-1])

    def copy(self, hop):
        where = self.block(hop)
        return pltpu.make_async_remote_copy(
            src_ref=self.buffer.at[where],
            dst_ref=self.buffer.at[where],
            send_sem=self.send.at[self.base + hop],
            recv_sem=self.receive.at[self.base + hop],
            device_id=place(self.hops[hop])[1],
            device_id_type=MESH,
        )

    def start(self, hop):
        if hop == 0:
            self.buffer[self.block(0)] = self.source[...]
        if hop < len(self.hops):
            self.copy(hop).start()

    def finish(self, hop):
        if hop < len(self.hops):
            self.copy(hop).wait()
        if hop == len(self.hops) - 1:
            self.out[...] = self.buffer[...]


def greeted(plans):
    labels = set()
    for names, hops in plans:
        labels |= set(hops) if names is None else {label for _, label in hops}
    return sorted(labels, key=str)


def exchange_parts(arrays, plans):
    outs, scratch, total = [], [], 0
    for array, (labels, hops) in zip(arrays, plans):
        total += len(hops)
        if labels is None:
            shape = (2,) * len(hops) + array.shape
            scratch.append(pltpu.VMEM(shape, array.dtype))
            outs.append(jax.ShapeDtypeStruct(shape, array.dtype))
            continue
        names, shape = list(labels), list(array.shape)
        for kind, label in hops:
            if kind == "split":
                dim = names.index(label)
                names.pop(dim)
                shape.pop(dim)
            scratch.append(pltpu.VMEM(tuple(shape), array.dtype))
        kind = hops[-1][0]
        lead = (2,) if kind == "gather" else ()
        wide = array.dtype if kind in ("split", "swap", "sum") else jnp.float32
        outs.append(jax.ShapeDtypeStruct(lead + tuple(shape), wide))
    semaphores = pltpu.SemaphoreType.DMA((total,))
    return outs, scratch + [semaphores, semaphores]


def make_flows(plans, sources, outs, rest):
    send, receive = rest[-2:]
    flows, base, used = [], 0, 0
    for (labels, hops), source, out in zip(plans, sources, outs):
        if labels is None:
            flows.append(Gathering(hops, source, out, rest[used], send, receive, base))
            used += 1
        else:
            buffers = rest[used : used + len(hops)]
            flows.append(Reduction(labels, hops, source, out, buffers, send, receive, base))
            used += len(hops)
        base += len(hops)
    return flows


def with_exchange(kernel, counts, arrays, plans, ends, begins, others):
    labels = sorted(set(greeted(plans)) | set(others), key=str)

    def body(*refs):
        groups, at = [], 0
        for count in counts:
            groups.append(refs[at : at + count])
            at += count
        scalars, inputs, given, outputs, targets, scratch, rest = groups
        given = list(given)
        sources = [outputs[a] if isinstance(a, int) else given.pop(0) for a in arrays]
        flows = make_flows(plans, sources, targets, rest)
        step = pl.program_id(0)

        @pl.when(step == 0)
        def _():
            greet(labels)

        kernel(*scalars, *inputs, *outputs, *scratch)

        @pl.when(step == 0)
        def _():
            if not others:
                meet(labels)

        times = set(begins) | {end for flow_ends in ends for end in flow_ends}
        for now in sorted(times):

            @pl.when(step == now)
            def _(now=now):
                for flow, begin in zip(flows, begins):
                    if begin == now:
                        flow.start(0)
                for hop in range(max(len(flow_ends) for flow_ends in ends)):
                    for flow, flow_ends in zip(flows, ends):
                        if hop < len(flow_ends) and flow_ends[hop] == now:
                            flow.finish(hop)
                            flow.start(hop + 1)

    return body


def whole(array):
    return pl.BlockSpec(
        array.shape, lambda step, *_: (0,) * len(array.shape), pipeline_mode=pl.Buffered(1)
    )


def run(
    kernel,
    name,
    grid,
    scalars,
    operands,
    specs,
    outs,
    out_specs,
    scratch,
    flops,
    exchange=None,
    transcendentals=0,
    collective=None,
    others=(),
):
    operands, specs, outs = list(operands), list(specs), list(outs)
    out_specs, scratch = list(out_specs), list(scratch)
    traffic = sum(a.size * a.dtype.itemsize for a in operands + outs)
    effects = {}
    if exchange is not None:
        arrays, plans, ends, collective = exchange[:4]
        begins = exchange[4] if len(exchange) > 4 else (0,) * len(arrays)
        shapes = [outs[a] if isinstance(a, int) else a for a in arrays]
        more_outs, more_scratch = exchange_parts(shapes, plans)
        given = [a for a in arrays if not isinstance(a, int)]
        counts = (
            len(scalars),
            len(operands),
            len(given),
            len(outs),
            len(more_outs),
            len(scratch),
            len(more_scratch),
        )
        kernel = with_exchange(kernel, counts, arrays, plans, ends, begins, others)
        operands += given
        specs += [whole(array) for array in given]
        outs += more_outs
        out_specs += [whole(array) for array in more_outs]
        scratch += more_scratch
    if collective is not None:
        effects = dict(collective_id=collective, has_side_effects=True)
    return pl.pallas_call(
        kernel,
        out_shape=outs,
        grid_spec=pltpu.PrefetchScalarGridSpec(
            num_scalar_prefetch=len(scalars),
            grid=(grid,),
            in_specs=specs,
            out_specs=out_specs,
            scratch_shapes=scratch,
        ),
        compiler_params=pltpu.CompilerParams(vmem_limit_bytes=GRANTS[name] << 20, **effects),
        cost_estimate=pl.CostEstimate(
            flops=flops, transcendentals=transcendentals, bytes_accessed=traffic
        ),
        name=name,
    )(*scalars, *operands)


GRANTS = dict(
    enter=34,
    self_forward=20,
    middle=24,
    cross_forward=20,
    mlp=60,
    reduce_core=60,
    cross_backward=60,
    text_back=60,
    back_middle=60,
    self_backward=60,
    leave=60,
    finish=60,
)


def idle_kernel():
    pass


def swapped(value):
    return lax.ppermute(value, "text", [(0, 1), (1, 0)])


def on_device(
    frames_in,
    frame_item,
    text_in,
    text_len,
    time_embed,
    cotangent,
    w_mod,
    b_mod,
    w_qkv,
    w_out,
    b_out,
    w_q_cross,
    w_kv_cross,
    w_out_cross,
    b_out_cross,
    w_up,
    b_up,
    w_down,
    b_down,
):
    text_side = lax.axis_index("text")
    partner_side = 1 - text_side
    row_count, width = frames_in.shape
    half = row_count // 2
    hidden_width = w_up.shape[1]
    item_count = time_embed.shape[0]
    token_span = text_in.shape[1]
    token_rows = item_count * 2 * token_span
    share_count = lax.axis_size("frames")
    bits = share_count.bit_length() - 1
    spot = lax.axis_index("frames")
    segment = lax.dynamic_index_in_dim(frame_item, text_side, 0, keepdims=False)
    own_lengths = lax.dynamic_slice_in_dim(text_len, text_side * item_count, item_count)
    item_ids = jnp.arange(item_count, dtype=jnp.int32)

    own_text = lax.dynamic_slice_in_dim(text_in, text_side * item_count, item_count, 0)
    partner_text = lax.dynamic_slice_in_dim(text_in, partner_side * item_count, item_count, 0)
    fetched_text = swapped(partner_text)

    counts = jnp.sum((segment[None, :] == item_ids[:, None]).astype(jnp.int32), axis=1)
    big = jnp.argmax((counts == half).astype(jnp.int32)).astype(jnp.int32)
    start = jnp.sum((segment < big).astype(jnp.int32))
    start_scalar = start.reshape(1)
    segment = jnp.roll(jnp.mod(segment - big, item_count), -start)
    lengths = jnp.roll(own_lengths, -big)
    embedding = jnp.roll(time_embed, -big, axis=0).astype(jnp.float32)
    text = jnp.roll(jnp.concatenate([own_text, fetched_text], axis=1), -big, axis=0)
    text = text.reshape(token_rows, text.shape[2])

    code_column, code_row = segment[:, None], segment[None, :]
    self_codes = (code_column, code_row)
    slot = jnp.arange(2 * token_span, dtype=jnp.int32)
    position = jnp.where(
        slot < token_span,
        text_side * token_span + slot,
        partner_side * token_span + slot - token_span,
    )
    token_code = jnp.where(position[None, :] < lengths[:, None], item_ids[:, None], -1)
    cross_codes = (token_code.reshape(token_rows, 1), code_row)
    pairs = width // LANES
    blocks = row_count // ROW_BLOCK
    matmul_flops = 2 * row_count * width * width

    condition = jax.nn.silu(embedding).astype(low_type)
    mod_items = rows_dot(condition, w_mod) + b_mod.astype(jnp.float32)
    mod = mod_items.reshape(item_count, 8, width)

    def as_row(vector):
        return vector.astype(jnp.float32)[None, :]

    low_rows = shape_of((row_count, width), low_type)
    full_rows = shape_of((row_count, width), jnp.float32)
    square = shape_of((width, width), low_type)
    low_scratch = pltpu.VMEM((row_count, width), low_type)
    full_scratch = pltpu.VMEM((row_count, width), jnp.float32)
    wide_scratch = pltpu.VMEM((row_count + half + 8, width), jnp.float32)

    operands = (frames_in, cotangent, code_column, mod, w_qkv)
    packed_shape = shape_of((row_count, 3 * width), low_type)
    packed, normed_a, frames, upstream = run(
        enter_kernel,
        "enter",
        blocks,
        (start_scalar,),
        operands,
        [whole(frames_in), whole(cotangent), row_blocks(code_column), whole(mod), whole(w_qkv)],
        [packed_shape, low_rows, low_rows, low_rows],
        [row_blocks(packed_shape), row_blocks(low_rows), row_blocks(low_rows), row_blocks(low_rows)],
        [wide_scratch, wide_scratch],
        3 * matmul_flops,
    )
    packed_columns = (pairs, (0, pairs, 2 * pairs, 0))
    attended, self_log = attention_call(
        attend_kernel,
        "self_forward",
        (packed, packed, packed),
        packed_columns,
        self_codes,
        None,
        (row_count, "log"),
        half,
        row_count,
    )
    operands = (attended, frames, code_column, mod, w_out, as_row(b_out), w_q_cross)
    after_a, branch_a, normed_b, cross_q = run(
        middle_kernel,
        "middle",
        blocks,
        (),
        operands,
        [row_blocks(attended), row_blocks(frames), row_blocks(code_column)]
        + [whole(array) for array in operands[3:]],
        [full_rows, full_rows, low_rows, low_rows],
        [row_blocks(full_rows)] * 2 + [row_blocks(low_rows)] * 2,
        [],
        2 * matmul_flops,
    )
    text_kv = rows_dot(text, w_kv_cross).astype(low_type)
    cross_columns = (pairs, (0, 0, pairs, 0))
    cross_out, cross_log = attention_call(
        attend_kernel,
        "cross_forward",
        (cross_q, text_kv, text_kv),
        cross_columns,
        cross_codes,
        None,
        (row_count, "log"),
        2 * token_span,
        token_rows,
    )
    frame_labels = tuple(range(bits))[::-1]
    frame_dims = (2,) * bits
    rest_labels, rest_dims = frame_labels[:-1], frame_dims[:-1]
    low_bits = [("split", bit) for bit in range(1, bits)]

    def shares(array):
        rows, columns = array.shape[-2:]
        return array.reshape(array.shape[:-2] + frame_dims + (rows // share_count, columns))

    def text_shares(array):
        rows, columns = array.shape[-2:]
        cut = (2, rows // share_count // 2, columns)
        return array.reshape(array.shape[:-2] + frame_dims + cut)

    def spread(count, low, top):
        return tuple(low + (top - low) * (hop + 1) // count for hop in range(count))

    chunks = 4
    chunk = hidden_width // chunks
    down_share, up_share = hidden_width // share_count, width // share_count
    chunk_pairs, pair_count = chunk // down_share // 2, share_count // 2
    in_core = down_share % 16 == 0 and up_share % 16 == 0
    operands = (
        cross_out,
        after_a,
        upstream,
        code_column,
        code_row,
        mod,
        w_out_cross,
        as_row(b_out_cross),
        as_row(b_down),
        w_up,
        as_row(b_up),
        w_down,
        jnp.concatenate([condition, condition], axis=0),
    )
    bias_shape = shape_of((8, width), jnp.float32)
    sums_shape = shape_of((3, 8, width), jnp.float32)
    core_scratch = []
    if in_core:
        down_shape = shape_of((chunks, chunk_pairs // 2, down_share, width), low_type)
        up_shape = shape_of((chunks, pair_count, up_share // 2, chunk), low_type)
        weight_specs = [whole(down_shape), whole(up_shape)]
        core_scratch = [
            pltpu.VMEM((2, chunk_pairs // 2, 2, 2, down_share, width), low_type),
            pltpu.VMEM((2, pair_count, 2, 2, up_share // 2, chunk), low_type),
            pltpu.VMEM((chunks, chunk_pairs // 2, 2, down_share, width), low_type),
            pltpu.VMEM((chunks, pair_count, 2, up_share // 2, chunk), low_type),
            pltpu.VMEM(down_shape.shape, low_type),
            pltpu.VMEM(up_shape.shape, low_type),
            pltpu.SemaphoreType.DMA((chunks, 4)),
            pltpu.SemaphoreType.DMA((chunks, 4)),
        ]
    else:
        down_shape = shape_of((chunks, chunk, width), low_type)
        up_shape = shape_of((chunks, width, chunk), low_type)
        weight_specs = [
            pl.BlockSpec((1,) + shape.shape[1:], lambda step, *_: (step, 0, 0))
            for shape in (down_shape, up_shape)
        ]
    wide_shape = shape_of((row_count + half + 8, width), jnp.float32)
    outs = [wide_shape, full_rows, low_rows, down_shape, up_shape, square]
    table_c_shape = shape_of((2 * item_count, 3 * width // 2 + width), low_type)
    table_b_shape = shape_of((2 * item_count, 3 * width // 2), low_type)
    table_a_shape = shape_of((2 * item_count, width), low_type)
    outs += [bias_shape, sums_shape, table_c_shape]
    (
        wide_out,
        grad_after_b,
        grad_cross,
        part_down,
        part_up,
        grad_w_out_cross,
        grad_b_mlp,
        sums_c,
        table_c,
    ) = run(
        mlp_kernel,
        "mlp",
        chunks,
        (),
        operands,
        [whole(array) for array in operands[:9]]
        + [
            column_blocks(w_up, chunk),
            column_blocks(operands[10], chunk),
            row_blocks(w_down, chunk),
            whole(operands[12]),
        ],
        outs,
        [whole(wide_shape), whole(full_rows), whole(low_rows)]
        + weight_specs
        + [
            whole(square),
            whole(bias_shape),
            whole(sums_shape),
            whole(table_c_shape),
        ],
        [
            low_scratch,
            pltpu.VMEM((width, row_count), low_type),
            low_scratch,
            full_scratch,
            pltpu.VMEM((row_count, chunk), low_type),
            pltpu.VMEM((row_count, chunk), low_type),
        ]
        + core_scratch,
        26 * matmul_flops,
        collective=0 if in_core else None,
    )
    chunk_labels = ("chunk", "block")
    if in_core:
        part_down = part_down.reshape(rest_dims[:-1] + (down_share, width))
        part_up = part_up.reshape((2, 2) + rest_dims + (up_share // 2, chunk))
    else:
        part_down, part_up = run(
            idle_kernel,
            "reduce_core",
            1,
            (),
            (),
            [],
            [],
            [],
            [],
            0,
            (
                [
                    shares(part_down.reshape(hidden_width, width)),
                    text_shares(part_up.reshape(2, 2, width, chunk)),
                ],
                [
                    (frame_labels, [("split", 0), ("split", 1)]),
                    (
                        chunk_labels + frame_labels + ("text",),
                        [("split", 0), ("split", "text")],
                    ),
                ],
                [(0, 0), (0, 0)],
                6,
            ),
        )

    gather_hops = tuple(range(1, bits))[::-1] + ("text", 0)
    all_labels = tuple(range(bits)) + ("text",)
    (
        low_cross_q,
        grad_text_k,
        grad_text_v,
        table_c,
        part_down,
        part_up,
    ) = attention_call(
        attend_back_kernel,
        "cross_backward",
        (cross_q, text_kv, text_kv, grad_cross),
        cross_columns,
        cross_codes,
        cross_log,
        (row_count, token_rows, token_rows),
        2 * token_span,
        token_rows,
        (
            [table_c, part_down, part_up],
            [
                (None, gather_hops[:-2]),
                (rest_labels[:-1], low_bits[1:2]),
                (chunk_labels + rest_labels, low_bits[:1]),
            ],
            [
                spread(bits - 1, -1, pairs - 1),
                (pairs - 3,),
                (pairs - 3,),
            ],
            1,
        ),
    )
    half_text = (item_count, token_span, text.shape[1])
    own_shape, sent_shape = shape_of(half_text, jnp.float32), shape_of(half_text, low_type)
    kv_shape = shape_of((2, text.shape[1], width), low_type)
    operands = (grad_text_k, grad_text_v, text, w_kv_cross, wide_out)
    token_block = 2 * token_span
    item_spec = pl.BlockSpec(
        (1,) + half_text[1:], lambda step, big_ref, _: (lax.rem(step + big_ref[0], item_count), 0, 0)
    )
    own_text_grad, sent_text_grad, grad_w_kv, frames_out = run(
        text_back_kernel,
        "text_back",
        item_count,
        (big.reshape(1), start_scalar),
        operands,
        [row_blocks(array, token_block) for array in operands[:3]]
        + [whole(w_kv_cross), whole(wide_out)],
        [own_shape, sent_shape, kv_shape, full_rows],
        [item_spec, item_spec, whole(kv_shape), row_blocks(full_rows, row_count // item_count)],
        [pltpu.VMEM((token_rows, width), low_type)] * 2
        + [pltpu.VMEM((token_rows, text.shape[1]), low_type)],
        4 * 2 * token_rows * width * width,
    )
    operands = (
        low_cross_q,
        normed_b,
        after_a,
        grad_after_b,
        branch_a,
        attended,
        code_column,
        code_row,
        mod,
        w_q_cross,
        w_out,
        grad_b_mlp,
    )
    out_rows = up_share + 16
    out_shape = shape_of((share_count, out_rows, width), low_type) if in_core else square
    (
        grad_after_a,
        grad_attended,
        grad_w_q_cross,
        grad_w_out,
        grad_b_middle,
        sums_b,
        table_b,
        table_c,
        part_down,
        part_up,
        partner_text_grad,
        part_kv,
    ) = run(
        back_middle_kernel,
        "back_middle",
        blocks,
        (),
        operands,
        [row_blocks(array) for array in operands[:7]]
        + [column_blocks(code_row)]
        + [whole(array) for array in operands[8:]],
        [full_rows, low_rows, square, out_shape, bias_shape, sums_shape, table_b_shape],
        [row_blocks(full_rows), row_blocks(low_rows), whole(square), whole(out_shape)]
        + [whole(bias_shape), whole(sums_shape), whole(table_b_shape)],
        [low_scratch] * 4,
        4 * matmul_flops,
        (
            [table_c, part_down, part_up, sent_text_grad, shares(grad_w_kv)],
            [
                (None, gather_hops[-2:]),
                (rest_labels[:-2], low_bits[2:]),
                (chunk_labels + rest_labels[:-1], low_bits[1:2]),
                ((), [("swap", "text")]),
                (("pair",) + frame_labels, [("split", 0), ("split", 1)]),
            ],
            [
                (blocks - 2, blocks - 1),
                spread(bits - 3, 0, blocks - 1),
                (blocks - 1,),
                (blocks - 1,),
                (0, blocks - 1),
            ],
            2,
        ),
    )
    piece = 3 * LANES
    even_pairs = pairs - pairs // 2
    if not in_core:
        grad_w_out = jnp.concatenate(
            [
                grad_w_out.reshape(share_count, up_share, width),
                jnp.broadcast_to(
                    jnp.concatenate([grad_b_middle] * 2, axis=0).astype(low_type)[None],
                    (share_count, 16, width),
                ),
            ],
            axis=1,
        )
    part_out = grad_w_out.reshape(frame_dims + (2, out_rows // 2, width))
    if in_core:
        lead = pair_count // 2
        even_shape = shape_of((lead, 2, even_pairs, 2, up_share // 2, piece), low_type)
        odd_shape = shape_of((lead, 2, 2, pairs // 2, up_share // 2, piece), low_type)
        core_scratch = [
            pltpu.VMEM((2, lead, 2, 2, 2, up_share // 2, piece), low_type),
            pltpu.VMEM((pairs, lead, 2, 2, up_share // 2, piece), low_type),
            pltpu.SemaphoreType.DMA((pairs,)),
            pltpu.SemaphoreType.DMA((pairs,)),
        ]
        weight_specs = [whole(even_shape), whole(odd_shape)]
    else:
        even_shape = shape_of((pairs, width, piece), low_type)
        odd_shape = shape_of((8, LANES), low_type)
        core_scratch = []
        weight_specs = [
            pl.BlockSpec((1, width, piece), lambda step, *_: (step, 0, 0)),
            whole(odd_shape),
        ]
    pair_block = pl.BlockSpec((row_count, LANES), lambda step: (0, step))
    (
        grad_q,
        grad_k,
        grad_v,
        part_even,
        part_odd,
        table_b,
        sum_w_down,
        sum_w_up,
        part_kv,
        part_q_cross,
        part_out_cross,
        part_out,
    ) = run(
        functools.partial(self_back_kernel, key_split=half, met=all_labels),
        "self_backward",
        pairs,
        (),
        (packed, packed, packed, grad_attended, self_log, code_column, code_row, normed_a),
        [
            pl.BlockSpec((row_count, LANES), lambda step, offset=offset: (0, offset + step))
            for offset in packed_columns[1]
        ]
        + [pl.BlockSpec((1, 8, row_count), lambda step: (step, 0, 0))]
        + [whole(array) for array in (code_column, code_row, normed_a)],
        [low_rows, low_rows, low_rows, even_shape, odd_shape],
        [pair_block] * 3 + weight_specs,
        [pltpu.VMEM((half, half), jnp.float32), pltpu.VMEM((width, row_count), low_type)]
        + core_scratch,
        8 * matmul_flops,
        (
            [
                table_b,
                part_down,
                part_up,
                part_kv,
                text_shares(grad_w_q_cross),
                shares(grad_w_out_cross),
                part_out,
            ],
            [
                (None, gather_hops),
                ((), [("full", "text")]),
                (chunk_labels + rest_labels[:-2], low_bits[2:] + [("gather", "text")]),
                (("pair",) + rest_labels[:-1], low_bits[1:2]),
                (frame_labels + ("text",), [("split", 0), ("split", "text")]),
                (frame_labels, [("split", 0), ("split", 2)]),
                (frame_labels + ("text",), [("split", 0), ("split", 1)]),
            ],
            [
                spread(bits + 1, 0, pairs - 1),
                (pairs - 4,),
                spread(bits - 2, 0, pairs - 2),
                (pairs - 3,),
                (0, pairs - 2),
                (0, pairs - 1),
                (0, pairs - 2),
            ],
            3,
        ),
        others=all_labels if in_core else (),
    )
    even_labels, odd_labels = rest_labels, rest_labels + ("text",)
    if in_core:
        part_even = part_even.reshape(rest_dims + (even_pairs, up_share, piece))
        part_odd = part_odd.reshape(rest_dims + (2, pairs // 2, up_share // 2, piece))
    else:
        by_pair = part_even.reshape((pairs,) + frame_dims + (up_share, piece))
        part_even = jnp.moveaxis(by_pair[0::2], 0, bits)
        part_odd = by_pair[1::2].reshape(
            (pairs // 2,) + frame_dims + (2, up_share // 2, piece)
        )
        part_even, part_odd = run(
            idle_kernel,
            "reduce_core",
            1,
            (),
            (),
            [],
            [],
            [],
            [],
            0,
            (
                [part_even, jnp.moveaxis(part_odd, 0, bits + 1)],
                [
                    (frame_labels, [("split", 0)]),
                    (frame_labels + ("text",), [("split", 0)]),
                ],
                [(0,), (0,)],
                7,
            ),
        )
    embedding_rows = jnp.concatenate([embedding] * (8 // item_count), axis=0)
    operands = (
        grad_q,
        grad_k,
        grad_v,
        frames,
        grad_after_a,
        code_column,
        code_row,
        mod,
        w_qkv,
        sums_b,
        sums_c,
        embedding_rows,
        w_mod,
    )
    mod_columns = 8 * width
    time_rows = shape_of((8, width), jnp.float32)
    last_block = blocks - 1
    steps = blocks + 8
    late = steps - 1

    def early(array):
        return pl.BlockSpec(
            (ROW_BLOCK, array.shape[1]), lambda step: (jnp.minimum(step, last_block), 0)
        )

    (
        wide_grad,
        _,
        time_grad,
        table_a,
        sum_even,
        sum_odd,
        sum_kv,
        sum_q_cross,
        sum_out_cross,
        sum_out,
    ) = run(
        leave_kernel,
        "leave",
        steps,
        (),
        operands,
        [early(array) for array in operands[:6]]
        + [pl.BlockSpec((1, ROW_BLOCK), lambda step: (0, jnp.minimum(step, last_block)))]
        + [whole(array) for array in operands[7:12]]
        + [pl.BlockSpec((width, width), lambda step: (0, jnp.maximum(step - blocks, 0)))],
        [wide_shape, table_a_shape, time_rows],
        [whole(wide_shape), whole(table_a_shape), whole(time_rows)],
        [
            pltpu.VMEM((2, 8, width), jnp.float32),
            pltpu.VMEM((8, 8, width), low_type),
            pltpu.VMEM((8, width), jnp.float32),
        ],
        4 * matmul_flops,
        (
            [1, part_even, part_odd, part_kv, part_q_cross, part_out_cross, part_out],
            [
                (None, gather_hops),
                (even_labels, low_bits + [("full", "text")]),
                (odd_labels, [("split", "text")] + low_bits + [("gather", "text")]),
                (("pair",) + rest_labels[:-2], low_bits[2:] + [("full", "text")]),
                (rest_labels, low_bits + [("gather", "text")]),
                (
                    rest_labels[:-2] + rest_labels[-1:],
                    low_bits[2:] + low_bits[:1] + [("full", "text")],
                ),
                (
                    rest_labels[:-1] + ("text",),
                    [("split", "text")] + low_bits[1:] + [("gather", "text")],
                ),
            ],
            [
                spread(bits + 1, blocks + 2, late),
                (blocks + 1,) + spread(bits - 1, blocks + 4, late),
                (blocks + 1,) + spread(bits, blocks + 4, late),
                spread(bits - 1, blocks, late),
                spread(bits, last_block, late),
                spread(bits - 1, blocks, late),
                spread(bits, last_block, late),
            ],
            4,
            (last_block,) + (0,) * 6,
        ),
    )
    time_grad = jnp.roll(time_grad[:item_count], big, axis=0)
    text_pair = item_count // 2
    text_shape = shape_of((2 * item_count,) + half_text[1:], jnp.float32)

    def text_spec(turn):
        return pl.BlockSpec(
            (text_pair,) + half_text[1:],
            (lambda step, *_: (lax.rem(step, 2), 0, 0)) if turn else (lambda step, *_: (step, 0, 0)),
        )

    operands = (
        wide_grad,
        own_text_grad,
        partner_text_grad,
        table_a.reshape(-1, width),
        table_b.reshape(-1, table_b.shape[-1]),
        table_c.reshape(-1, table_c.shape[-1]),
        sum_w_up.reshape(2, chunks, up_share // 2, chunk),
        sum_even,
        sum_odd,
        sum_kv,
    )
    mod_shape = shape_of((up_share, mod_columns), jnp.float32)
    total_shape = shape_of((1, mod_columns), jnp.float32)
    sum_up_shape = shape_of((up_share, hidden_width), jnp.float32)
    sum_qkv_shape = shape_of((up_share, 3 * width), jnp.float32)
    sum_kv_shape = shape_of((up_share, 2 * width), jnp.float32)
    more = [mod_shape, total_shape, sum_up_shape, sum_qkv_shape, sum_kv_shape]
    frames_grad, text_grad, grad_w_mod, item_total, sum_w_up, sum_qkv, sum_kv = run(
        finish_kernel,
        "finish",
        4,
        (start_scalar, text_side.reshape(1), spot.reshape(1)),
        operands,
        [whole(wide_grad), text_spec(True), text_spec(True)] + [whole(a) for a in operands[3:]],
        [full_rows, text_shape] + more,
        [row_blocks(full_rows, row_count // 4), text_spec(False)] + [whole(a) for a in more],
        [],
        0,
    )
    grad_b_mod = lax.dynamic_slice_in_dim(
        item_total[0], spot * (mod_columns // share_count), mod_columns // share_count
    )

    def bias_share(rows):
        size = rows.size // share_count
        return lax.dynamic_slice_in_dim(rows.reshape(-1), spot * size, size)

    sum_out = sum_out.reshape(out_rows, width)
    bias = sum_out[up_share:]
    bias_cuts = [
        bias_share(rows) for rows in (bias[0], bias[2], bias[3 : 3 + chunks], bias[1])
    ]
    return (
        frames_out,
        frames_grad,
        text_grad,
        time_grad,
        grad_w_mod,
        grad_b_mod,
        sum_qkv,
        sum_out[:up_share],
        bias_cuts[0],
        sum_q_cross.reshape(up_share, width),
        sum_kv,
        sum_out_cross,
        bias_cuts[1],
        sum_w_up,
        bias_cuts[2],
        sum_w_down,
        bias_cuts[3],
    )


def solution(mesh):
    in_specs = (
        P(("frames", "text"), None),
        P("frames", None),
        P("frames", "text", None),
        P("frames"),
        P(("frames", "text"), None),
        P(("frames", "text"), None),
    ) + (P(),) * 13
    out_specs = (
        P(("frames", "text"), None),
        P(("frames", "text"), None),
        P("frames", "text", None),
        P(("frames", "text"), None),
        P("frames", None),
        P("frames"),
        P("frames", None),
        P("frames", None),
        P("frames"),
        P("frames", None),
        P("frames", None),
        P("frames", None),
        P("frames"),
        P("frames", None),
        P("frames"),
        P("frames", None),
        P("frames"),
    )
    return jax.shard_map(
        on_device, mesh=mesh, in_specs=in_specs, out_specs=out_specs, check_vma=False
    )
```

```python
import functools

import jax
import jax.numpy as jnp
from jax import lax
from jax.experimental import pallas as pl
from jax.experimental.pallas import tpu as pltpu
from jax.sharding import PartitionSpec as P

HEAD_DIM = 64
LANES = 128
VMEM_LIMIT = 60 << 20

epsilon = 1e-06
masked_add = -1000000000.0
highest = lax.Precision.HIGHEST
low_type = jnp.bfloat16


def rows_dot(left_side, right_side):
    return jnp.dot(left_side, right_side, preferred_element_type=jnp.float32)


def left_dot(left_side, right_side):
    return lax.dot_general(
        left_side, right_side, (((0,), (0,)), ((), ())), preferred_element_type=jnp.float32
    )


def right_dot(left_side, right_side):
    return lax.dot_general(
        left_side, right_side, (((1,), (1,)), ((), ())), preferred_element_type=jnp.float32
    )


def layer_norm(values):
    center = values - jnp.mean(values, axis=-1, keepdims=True)
    spread = jnp.mean(center * center, axis=-1, keepdims=True)
    return center * lax.rsqrt(spread + epsilon)


def modulate(values, shift_by, scale_by):
    return layer_norm(values) * (1.0 + scale_by) + shift_by


def gelu_tanh(inputs):
    return (
        0.5
        * inputs
        * (1.0 + jnp.tanh(0.7978845608028654 * (inputs + 0.044715 * inputs * inputs * inputs)))
    )


def head_lanes(value, head, scale=None):
    lane = lax.broadcasted_iota(jnp.int32, value.shape, 1)
    scaled = value if scale is None else value * jnp.asarray(scale, value.dtype)
    return jnp.where(lane // HEAD_DIM == head, scaled, jnp.zeros_like(scaled))


def fill_bias(code_column_ref, code_row_ref, bias_refs, key_split):
    half = code_row_ref.shape[1] // 2
    spans = ((0, key_split), (key_split, code_column_ref.shape[0]))
    for part, bias_ref in enumerate(bias_refs):
        if bias_ref is None:
            continue
        low, top = spans[part]
        bias_ref[...] = jnp.where(
            code_column_ref[low:top, :] == code_row_ref[:, part * half : (part + 1) * half],
            0.0,
            masked_add,
        )


def attend_kernel(
    q_ref, k_ref, v_ref, code_column_ref, code_row_ref, out_ref, log_ref, *bias_refs, key_split
):
    half = q_ref.shape[0] // 2
    scale = HEAD_DIM ** (-0.5)
    if len(bias_refs) == 1:
        bias_refs = (None,) + bias_refs

    @pl.when(pl.program_id(0) == 0)
    def _():
        fill_bias(code_column_ref, code_row_ref, bias_refs, key_split)

    value_t = v_ref[...].T
    key_spans = (slice(0, key_split), slice(key_split, k_ref.shape[0]))
    units = [(part, head) for part in range(2) for head in range(2)]

    def scores_of(part, head):
        queries = q_ref[part * half : (part + 1) * half, :]
        scores = right_dot(k_ref[key_spans[part], :], head_lanes(queries, head, scale))
        return scores if bias_refs[part] is None else scores + bias_refs[part][...]

    ahead = scores_of(*units[0])
    outs = []
    for index, (part, head) in enumerate(units):
        scores = ahead
        if index + 1 < len(units):
            ahead = scores_of(*units[index + 1])
        rows = slice(part * half, (part + 1) * half)
        peak = jnp.max(scores, axis=0, keepdims=True)
        exponent = jnp.exp(scores - peak)
        total = jnp.sum(exponent, axis=0, keepdims=True)
        log_ref[0, head : head + 1, rows] = peak + jnp.log(total)
        lanes = slice(HEAD_DIM * head, HEAD_DIM * (head + 1))
        outs.append(
            rows_dot(value_t[lanes, key_spans[part]], exponent.astype(low_type)) / total
        )
        if head == 1:
            out_ref[rows, :] = jnp.concatenate(outs, axis=0).T.astype(low_type)
            outs = []


def attend_back_kernel(
    q_ref,
    k_ref,
    v_ref,
    grad_ref,
    log_ref,
    code_column_ref,
    code_row_ref,
    grad_q_ref,
    grad_k_ref,
    grad_v_ref,
    *bias_refs,
    key_split,
):
    half = q_ref.shape[0] // 2
    scale = HEAD_DIM ** (-0.5)
    if len(bias_refs) == 1:
        bias_refs = (None,) + bias_refs

    @pl.when(pl.program_id(0) == 0)
    def _():
        fill_bias(code_column_ref, code_row_ref, bias_refs, key_split)

    key_t = k_ref[...].T
    key_spans = (slice(0, key_split), slice(key_split, k_ref.shape[0]))
    units = [(part, head) for part in range(2) for head in range(2)]

    def products_of(part, head):
        rows = slice(part * half, (part + 1) * half)
        query_head = head_lanes(q_ref[rows, :], head, scale)
        grad_head = head_lanes(grad_ref[rows, :], head)
        scores = right_dot(k_ref[key_spans[part], :], query_head)
        if bias_refs[part] is not None:
            scores = scores + bias_refs[part][...]
        grad_prob = right_dot(v_ref[key_spans[part], :], grad_head)
        return scores, grad_prob, query_head, grad_head

    ahead = products_of(*units[0])
    grad_q, grad_k, grad_v = [], [], []
    for index, (part, head) in enumerate(units):
        scores, grad_prob, query_head, grad_head = ahead
        if index + 1 < len(units):
            ahead = products_of(*units[index + 1])
        rows = slice(part * half, (part + 1) * half)
        prob = jnp.exp(scores - log_ref[0, head : head + 1, rows])
        weighted = prob * grad_prob
        delta = jnp.sum(weighted, axis=0, keepdims=True)
        grad_scores = (weighted - prob * delta).astype(low_type)
        grad_k.append(rows_dot(grad_scores, query_head))
        grad_v.append(rows_dot(prob.astype(low_type), grad_head))
        lanes = slice(HEAD_DIM * head, HEAD_DIM * (head + 1))
        grad_q.append(rows_dot(key_t[lanes, key_spans[part]], grad_scores) * scale)
        if head == 1:
            grad_q_ref[rows, :] = jnp.concatenate(grad_q, axis=0).T.astype(low_type)
            grad_k_ref[key_spans[part], :] = (grad_k[0] + grad_k[1]).astype(low_type)
            grad_v_ref[key_spans[part], :] = (grad_v[0] + grad_v[1]).astype(low_type)
            grad_q, grad_k, grad_v = [], [], []


def attention_call(
    kernel, name, operands, columns, codes, log_total, outs, key_split, key_rows, exchange=None
):
    rows = codes[1].shape[1]
    half = rows // 2
    pairs, offsets = columns
    specs = [
        pl.BlockSpec((array.shape[0], LANES), lambda step, offset=offset: (0, offset + step))
        for array, offset in zip(operands, offsets)
    ]
    extra = []
    log_spec = pl.BlockSpec((1, 8, rows), lambda step: (step, 0, 0))
    if log_total is not None:
        specs.append(log_spec)
        extra.append(log_total)
    specs += [whole(code) for code in codes]
    out_shape, out_specs = [], []
    for count in outs:
        if count == "log":
            out_shape.append(jax.ShapeDtypeStruct((pairs, 8, rows), jnp.float32))
            out_specs.append(log_spec)
        else:
            out_shape.append(jax.ShapeDtypeStruct((count, pairs * LANES), low_type))
            out_specs.append(pl.BlockSpec((count, LANES), lambda step: (0, step)))
    scratch = [pltpu.VMEM((key_rows - key_split, half), jnp.float32)]
    if key_split != half:
        scratch = [pltpu.VMEM((key_split, half), jnp.float32)] + scratch
    products = 2 if log_total is None else 5
    cells = half * key_rows
    return run(
        functools.partial(kernel, key_split=key_split),
        name,
        pairs,
        (),
        list(operands) + extra + list(codes),
        specs,
        out_shape,
        out_specs,
        scratch,
        products * pairs * 2 * cells * 256 * 2,
        exchange,
        pairs * 2 * cells,
    )


ITEMS = 4

ROW_BLOCK = 256
SHIFT_A, SCALE_A, GATE_A, SHIFT_B, SCALE_B, SHIFT_C, SCALE_C, GATE_C = range(8)


def item_rows(mod_ref, part, code):
    out = mod_ref[part, 0:1, :]
    for item in range(1, ITEMS):
        out = jnp.where(code == item, mod_ref[part, item : item + 1, :], out)
    return out


def item_mask(code_row):
    ids = lax.broadcasted_iota(jnp.int32, (8, code_row.shape[1]), 0)
    return jnp.where(ids == code_row, 1.0, 0.0).astype(low_type)


def item_sums(mask, values):
    high = values.astype(low_type)
    rest = (values - high.astype(jnp.float32)).astype(low_type)
    return rows_dot(mask, high) + rows_dot(mask, rest)


def column_sum(values):
    return jnp.sum(values, axis=0, keepdims=True)


def normed_of(values):
    center = values - jnp.mean(values, axis=-1, keepdims=True)
    spread = jnp.mean(center * center, axis=-1, keepdims=True)
    inverse = lax.rsqrt(spread + epsilon)
    return center * inverse, inverse


def normed_back(grad, scale_by, normed, inverse):
    inner = grad * (1.0 + scale_by)
    return inverse * (
        inner
        - jnp.mean(inner, axis=-1, keepdims=True)
        - normed * jnp.mean(inner * normed, axis=-1, keepdims=True)
    )


def rolled_rows(source_ref, wide_ref):
    rows = source_ref.shape[0]
    wide_ref[:rows, :] = source_ref[...].astype(jnp.float32)
    wide_ref[rows : rows + rows // 2, :] = source_ref[: rows // 2, :].astype(jnp.float32)


def rows_from(wide_ref, first, offset, count):
    rest = lax.rem(first, 8)
    where = pl.ds(pl.multiple_of(first - rest + offset, 8), count + 8)
    rows = wide_ref[where, :].reshape(count // 8 + 1, 8, wide_ref.shape[1])
    turned = pltpu.roll(rows, lax.rem(8 - rest, 8), 1)
    near = lax.broadcasted_iota(jnp.int32, (1, 8, wide_ref.shape[1]), 1) < 8 - rest
    return jnp.where(near, turned[:-1], turned[1:]).reshape(count, wide_ref.shape[1])


def prepare_kernel(
    length_ref,
    item_ref,
    embed_ref,
    w_mod_ref,
    b_mod_ref,
    mod_ref,
    start_ref,
    big_ref,
    code_column_ref,
    code_row_ref,
    token_code_ref,
    condition_ref,
    embedding_ref,
    plain,
):
    side = lax.axis_index("text")

    @pl.when(pl.program_id(0) == 0)
    def _():
        rows = item_ref.shape[1]
        segment = item_ref[pl.ds(side, 1), :]
        counts = [
            jnp.sum(jnp.where(segment == item, 1.0, 0.0)).astype(jnp.int32)
            for item in range(ITEMS)
        ]
        big = sum(item * (count == rows // 2).astype(jnp.int32) for item, count in enumerate(counts))
        start = sum(
            count * (item < big).astype(jnp.int32) for item, count in enumerate(counts)
        )
        start_ref[0] = start
        big_ref[0] = big
        local = lax.rem(segment - big + ITEMS, ITEMS).astype(jnp.float32)
        local = pltpu.roll(
            jnp.broadcast_to(local, (8, rows)), lax.rem(rows - start, rows), 1
        )
        code_row_ref[...] = local[0:1].astype(jnp.int32)
        code_column_ref[...] = local.T[:, 0:1].astype(jnp.int32)
        tokens = token_code_ref.shape[0] // ITEMS
        spot = lax.broadcasted_iota(jnp.int32, (tokens, 128), 0)
        span = tokens // 2
        position = jnp.where(
            spot < span, side * span + spot, (1 - side) * span + spot - span
        )
        plain[...] = embed_ref[...].astype(jnp.float32)
        for item in range(ITEMS):
            origin = lax.rem(big + item, ITEMS)
            valid = position < length_ref[side * ITEMS + origin]
            code = jnp.where(valid, item, -1)
            token_code_ref[item * tokens : (item + 1) * tokens, :] = code[:, 0:1]
            row = plain[pl.ds(origin, 1), :]
            low = row / (1.0 + jnp.exp(-row))
            for copy in (item, item + ITEMS):
                embedding_ref[copy : copy + 1, :] = row
                mod_ref[0, copy : copy + 1, :] = low
        condition_ref[...] = mod_ref[0].astype(low_type)

    mod_ref[0] = rows_dot(condition_ref[...], w_mod_ref[...]) + b_mod_ref[...].astype(jnp.float32)


def text_forward_kernel(big_ref, side_ref, own_ref, fetched_ref, w_kv_ref, text_ref, kv_ref):
    span = own_ref.shape[1]
    for part, ref in enumerate((own_ref, fetched_ref)):
        rows = slice(part * span, (part + 1) * span)
        text = ref[0]
        text_ref[rows, :] = text
        kv_ref[rows, :] = rows_dot(text, w_kv_ref[...]).astype(low_type)


def enter_kernel(
    start_ref,
    frames_ref,
    cotangent_ref,
    code_ref,
    mod_ref,
    w_qkv_ref,
    packed_ref,
    normed_ref,
    frames_out_ref,
    cotangent_out_ref,
    wide_frames,
    wide_cotangent,
):
    step = pl.program_id(0)
    block = packed_ref.shape[0]

    @pl.when(step == 0)
    def _():
        rolled_rows(frames_ref, wide_frames)
        rolled_rows(cotangent_ref, wide_cotangent)

    frames = rows_from(wide_frames, start_ref[0], step * block, block)
    frames_out_ref[...] = frames.astype(low_type)
    cotangent_out_ref[...] = rows_from(wide_cotangent, start_ref[0], step * block, block).astype(
        low_type
    )
    code = code_ref[...]
    normed, _ = normed_of(frames)
    modulated = normed * (1.0 + item_rows(mod_ref, SCALE_A, code)) + item_rows(
        mod_ref, SHIFT_A, code
    )
    low = modulated.astype(low_type)
    normed_ref[...] = low
    packed_ref[...] = rows_dot(low, w_qkv_ref[...]).astype(low_type)


def middle_kernel(
    attended_ref,
    frames_ref,
    code_ref,
    mod_ref,
    w_out_ref,
    b_out_ref,
    w_q_ref,
    after_ref,
    branch_ref,
    normed_ref,
    cross_q_ref,
):
    code = code_ref[...]
    branch = rows_dot(attended_ref[...], w_out_ref[...]) + b_out_ref[...]
    branch_ref[...] = branch
    after = frames_ref[...].astype(jnp.float32) + item_rows(mod_ref, GATE_A, code) * branch
    after_ref[...] = after
    normed, _ = normed_of(after)
    low = (
        normed * (1.0 + item_rows(mod_ref, SCALE_B, code)) + item_rows(mod_ref, SHIFT_B, code)
    ).astype(low_type)
    normed_ref[...] = low
    cross_q_ref[...] = rows_dot(low, w_q_ref[...]).astype(low_type)


GELU_FACTOR = 0.7978845608028654
GELU_CUBE = 0.044715


def gelu_both(inputs):
    square = inputs * inputs
    bend = jnp.tanh(inputs * (GELU_FACTOR + (GELU_FACTOR * GELU_CUBE) * square))
    half_up = 0.5 + 0.5 * bend
    slope = half_up + (0.5 * inputs) * (1.0 - bend * bend) * (
        GELU_FACTOR + (3.0 * GELU_FACTOR * GELU_CUBE) * square
    )
    return inputs * half_up, slope


def remote(source, target, send, receive, peer):
    return pltpu.make_async_remote_copy(
        src_ref=source,
        dst_ref=target,
        send_sem=send,
        recv_sem=receive,
        device_id=peer,
        device_id_type=MESH,
    )


def fill_table(table_ref, sums_ref):
    parts, _, width = sums_ref.shape
    items = table_ref.shape[0] // 2
    flat = jnp.concatenate([sums_ref[part, :items, :] for part in range(parts)], axis=1)
    middle = parts * width // 2
    both = jnp.concatenate([flat[:, :middle], flat[:, middle:]], axis=0)
    table_ref[:, :middle] = both.astype(low_type)


def mlp_kernel(
    cross_out_ref,
    after_a_ref,
    cotangent_ref,
    code_ref,
    code_row_ref,
    mod_ref,
    w_out_cross_ref,
    b_out_cross_ref,
    b_down_ref,
    w_up_ref,
    b_up_ref,
    w_down_ref,
    condition_ref,
    wide,
    grad_after_ref,
    grad_cross_ref,
    grad_w_down_ref,
    grad_w_up_ref,
    grad_w_out_cross_ref,
    grad_b_ref,
    sums_ref,
    table_ref,
    normed_c,
    normed_c_t,
    low_branch,
    back_sum,
    active,
    low_hidden,
    *core,
):
    after_b = grad_after_ref
    step = pl.program_id(0)
    steps = pl.num_programs(0)
    rows = cross_out_ref.shape[0]
    half = rows // 2
    block = ROW_BLOCK
    blocks = rows // block

    def span(index):
        return pl.ds(pl.multiple_of(index * block, block), block)

    def after_half(index):
        return pl.ds(pl.multiple_of(half + index * block, block), block)

    def core_copies(index):
        down, up, down_in, up_in, down_next, up_next, send, receive = core
        mine, peer = place(0)
        slot = lax.rem(index, 2)
        ends = ((down.at[slot, :, :, 1 - mine], down_in), (up.at[slot, :, 1 - mine], up_in))
        return [
            remote(out, into.at[index], send.at[index, which], receive.at[index, which], peer)
            for which, (out, into) in enumerate(ends)
        ]

    def next_copies(index):
        down, up, down_in, up_in, down_next, up_next, send, receive = core
        bit, across = place(1)
        side, beside = place("text")
        return [
            remote(
                down_in.at[index, :, 1 - bit],
                down_next.at[index],
                send.at[index, 2],
                receive.at[index, 2],
                across,
            ),
            remote(
                up_in.at[index, :, 1 - side],
                up_next.at[index],
                send.at[index, 3],
                receive.at[index, 3],
                beside,
            ),
        ]

    def settle(index):
        down, up, down_in, up_in = core[:4]
        mine = place(0)[0]
        slot = lax.rem(index, 2)
        for copy in core_copies(index):
            copy.wait()
        down_in[index] = down[slot, :, :, mine] + down_in[index]
        up_in[index] = up[slot, :, mine] + up_in[index]
        for copy in next_copies(index):
            copy.start()

    def finish(index):
        down_in, up_in, down_next, up_next = core[2:6]
        for copy in next_copies(index):
            copy.wait()
        grad_w_down_ref[index] = down_in[index, :, place(1)[0]] + down_next[index]
        grad_w_up_ref[index] = up_in[index, :, place("text")[0]] + up_next[index]

    @pl.when(step == 0)
    def _():
        if core:
            greet([0, 1, "text"])
            meet([0, 1, "text"])

        def body(index, _):
            where = span(index)
            code = code_ref[where, :]
            branch = rows_dot(cross_out_ref[where, :], w_out_cross_ref[...]) + b_out_cross_ref[...]
            after = after_a_ref[where, :] + branch
            after_b[where, :] = after
            normed, _ = normed_of(after)
            normed_c[where, :] = (
                normed * (1.0 + item_rows(mod_ref, SCALE_C, code))
                + item_rows(mod_ref, SHIFT_C, code)
            ).astype(low_type)
            low_branch[where, :] = (
                item_rows(mod_ref, GATE_C, code) * cotangent_ref[where, :].astype(jnp.float32)
            ).astype(low_type)
            wide[after_half(index), :] = jnp.zeros((block, wide.shape[1]), jnp.float32)
            back_sum[where, :] = jnp.zeros((block, back_sum.shape[1]), jnp.float32)
            return 0

        lax.fori_loop(0, blocks, body, 0)
        normed_c_t[...] = normed_c[...].T

    def products_of(index):
        where = pl.ds(index * block, block)
        hidden = rows_dot(normed_c[where, :], w_up_ref[...]) + b_up_ref[...]
        return hidden, right_dot(low_branch[where, :], w_down_ref[...])

    bias_total = jnp.zeros((1, w_up_ref.shape[1]), jnp.float32)
    ahead = products_of(0)
    for index in range(blocks):
        where = pl.ds(index * block, block)
        hidden, grad_active = ahead
        if index + 1 < blocks:
            ahead = products_of(index + 1)
        value, slope = gelu_both(hidden)
        low_value = value.astype(low_type)
        active[where, :] = low_value
        grad_hidden = slope * grad_active
        bias_total = bias_total + column_sum(grad_hidden)
        low = grad_hidden.astype(low_type)
        low_hidden[where, :] = low
        wide[after_half(index), :] += rows_dot(low_value, w_down_ref[...])
        back_sum[where, :] += right_dot(low, w_up_ref[...])

    @pl.when(step == 0)
    def _():
        grad_b_ref[...] = jnp.zeros(grad_b_ref.shape, jnp.float32)

    grad_b_ref[pl.ds(2 + step, 1), :] = bias_total
    down_part = left_dot(active[...], low_branch[...]).astype(low_type)
    up_part = rows_dot(normed_c_t[...], low_hidden[...]).astype(low_type)
    if core:
        slot = lax.rem(step, 2)
        core[0][slot] = down_part.reshape(core[0].shape[1:])
        core[1][slot] = up_part.reshape(core[1].shape[1:])
        for copy in core_copies(step):
            copy.start()

        @pl.when(step > 0)
        def _():
            settle(step - 1)

        @pl.when(step > 1)
        def _():
            finish(step - 2)
    else:
        grad_w_down_ref[0] = down_part
        grad_w_up_ref[0] = up_part

    @pl.when(step == steps - 1)
    def _():
        sums_ref[...] = jnp.zeros(sums_ref.shape, jnp.float32)

        def body(index, _):
            where = span(index)
            code = code_ref[where, :]
            mask = item_mask(code_row_ref[:, where])
            upstream = cotangent_ref[where, :].astype(jnp.float32)
            branch = wide[after_half(index), :] + b_down_ref[...]
            gate = item_rows(mod_ref, GATE_C, code)
            after = after_b[where, :]
            out = after + gate * branch
            wide[after_half(index), :] = out

            @pl.when(index >= blocks // 2)
            def _():
                wide[pl.ds(pl.multiple_of(index * block - half, block), block), :] = out

            sums_ref[2] += item_sums(mask, upstream * branch)
            grad_b_ref[0:1, :] += column_sum(gate * upstream)
            normed, inverse = normed_of(after)
            grad = back_sum[where, :]
            sums_ref[0] += item_sums(mask, grad)
            sums_ref[1] += item_sums(mask, grad * normed)
            total = upstream + normed_back(
                grad, item_rows(mod_ref, SCALE_C, code), normed, inverse
            )
            grad_after_ref[where, :] = total
            grad_b_ref[1:2, :] += column_sum(total)
            low = total.astype(low_type)
            low_branch[where, :] = low
            grad_cross_ref[where, :] = right_dot(low, w_out_cross_ref[...]).astype(low_type)
            return 0

        lax.fori_loop(0, blocks // 2, body, 0)
        if core:
            settle(step)
        lax.fori_loop(blocks // 2, blocks, body, 0)
        grad_w_out_cross_ref[...] = left_dot(cross_out_ref[...], low_branch[...]).astype(low_type)
        fill_table(table_ref, sums_ref)
        table_ref[:, table_ref.shape[1] - condition_ref.shape[1] :] = condition_ref[...]
        if core:
            finish(step - 1)
            finish(step)


def text_back_kernel(
    big_ref,
    start_ref,
    grad_k_ref,
    grad_v_ref,
    text_ref,
    w_kv_ref,
    wide_ref,
    own_ref,
    sent_ref,
    grad_w_ref,
    frames_out_ref,
    all_k,
    all_v,
    all_text,
):
    step = pl.program_id(0)
    rows = frames_out_ref.shape[0]
    half = pl.num_programs(0) * rows // 2
    frames_out_ref[...] = rows_from(wide_ref, half - start_ref[0], step * rows, rows)
    block, width = grad_k_ref.shape
    span = own_ref.shape[1]
    where = pl.ds(pl.multiple_of(step * block, block), block)
    keys, values = grad_k_ref[...], grad_v_ref[...]
    all_k[where, :] = keys
    all_v[where, :] = values
    all_text[where, :] = text_ref[...]
    total = right_dot(keys, w_kv_ref[:, :width]) + right_dot(values, w_kv_ref[:, width:])
    own_ref[0] = total[:span]
    sent_ref[0] = total[span:].astype(low_type)

    @pl.when(step == pl.num_programs(0) - 1)
    def _():
        text_t = all_text[...].T
        grad_w_ref[0] = rows_dot(text_t, all_k[...]).astype(low_type)
        grad_w_ref[1] = rows_dot(text_t, all_v[...]).astype(low_type)


def back_middle_kernel(
    low_q_ref,
    normed_b_ref,
    after_a_ref,
    grad_after_b_ref,
    branch_ref,
    attended_ref,
    code_ref,
    code_row_ref,
    mod_ref,
    w_q_ref,
    w_out_ref,
    bias_mlp_ref,
    grad_after_ref,
    grad_attended_ref,
    grad_w_q_ref,
    grad_w_out_ref,
    grad_b_ref,
    sums_ref,
    table_ref,
    all_q,
    all_normed,
    all_attended,
    all_branch,
):
    step = pl.program_id(0)
    block = low_q_ref.shape[0]

    @pl.when(step == 0)
    def _():
        sums_ref[...] = jnp.zeros(sums_ref.shape, jnp.float32)
        grad_b_ref[...] = jnp.zeros(grad_b_ref.shape, jnp.float32)

    where = pl.ds(pl.multiple_of(step * block, block), block)
    code = code_ref[...]
    mask = item_mask(code_row_ref[...])
    low_q = low_q_ref[...]
    all_q[where, :] = low_q
    all_normed[where, :] = normed_b_ref[...]
    all_attended[where, :] = attended_ref[...]
    grad = right_dot(low_q, w_q_ref[...])
    normed, inverse = normed_of(after_a_ref[...])
    sums_ref[1] += item_sums(mask, grad)
    sums_ref[2] += item_sums(mask, grad * normed)
    total = grad_after_b_ref[...] + normed_back(
        grad, item_rows(mod_ref, SCALE_B, code), normed, inverse
    )
    grad_after_ref[...] = total
    sums_ref[0] += item_sums(mask, total * branch_ref[...])
    grad_branch = item_rows(mod_ref, GATE_A, code) * total
    grad_b_ref[0:1, :] += column_sum(grad_branch)
    low = grad_branch.astype(low_type)
    all_branch[where, :] = low
    grad_attended_ref[...] = right_dot(low, w_out_ref[...]).astype(low_type)

    @pl.when(step == pl.num_programs(0) - 1)
    def _():
        grad_w_q_ref[...] = left_dot(all_normed[...], all_q[...]).astype(low_type)
        weight = left_dot(all_attended[...], all_branch[...]).astype(low_type)
        fill_table(table_ref, sums_ref)
        grad_b_ref[1:, :] = bias_mlp_ref[:-1, :]
        if len(grad_w_out_ref.shape) == 2:
            grad_w_out_ref[...] = weight
        else:
            shares, rows = grad_w_out_ref.shape[0], grad_w_out_ref.shape[1] - 16
            grad_w_out_ref[:, :rows, :] = weight.reshape(shares, rows, weight.shape[1])
            grad_w_out_ref[:, rows:, :] = jnp.broadcast_to(
                jnp.concatenate([grad_b_ref[...]] * 2, axis=0).astype(low_type)[None],
                (shares, 16, weight.shape[1]),
            )


def leave_kernel(
    grad_q_ref,
    grad_k_ref,
    grad_v_ref,
    frames_ref,
    grad_after_ref,
    code_ref,
    code_row_ref,
    mod_ref,
    w_qkv_ref,
    sums_b_ref,
    sums_c_ref,
    embedding_ref,
    w_mod_ref,
    wide,
    table_ref,
    time_ref,
    sums_ref,
    low_sums,
    total,
):
    step = pl.program_id(0)
    block, width = grad_q_ref.shape
    parts = low_sums.shape[0]
    blocks = pl.num_programs(0) - parts
    half = blocks * block // 2

    @pl.when(step == 0)
    def _():
        sums_ref[...] = jnp.zeros(sums_ref.shape, jnp.float32)
        total[...] = jnp.zeros_like(total)

    @pl.when(step < blocks)
    def _():
        code = code_ref[...]
        mask = item_mask(code_row_ref[...])
        grad = jnp.zeros((block, width), jnp.float32)
        for index, ref in enumerate((grad_q_ref, grad_k_ref, grad_v_ref)):
            grad = grad + right_dot(ref[...], w_qkv_ref[:, index * width : (index + 1) * width])
        normed, inverse = normed_of(frames_ref[...].astype(jnp.float32))
        sums_ref[0] += item_sums(mask, grad)
        sums_ref[1] += item_sums(mask, grad * normed)
        out = grad_after_ref[...] + normed_back(
            grad, item_rows(mod_ref, SCALE_A, code), normed, inverse
        )
        wide[pl.ds(pl.multiple_of(half + step * block, block), block), :] = out

        @pl.when(step >= blocks // 2)
        def _():
            wide[pl.ds(pl.multiple_of(step * block - half, block), block), :] = out

    @pl.when(step == blocks - 1)
    def _():
        fill_table(table_ref, sums_ref)
        at = 0
        for ref in (sums_ref, sums_b_ref, sums_c_ref):
            low_sums[at : at + ref.shape[0]] = ref[...].astype(low_type)
            at += ref.shape[0]

    @pl.when(step >= blocks)
    def _():
        total[...] += right_dot(low_sums[jnp.maximum(step - blocks, 0)], w_mod_ref[...])

    @pl.when(step == pl.num_programs(0) - 1)
    def _():
        embedding = embedding_ref[...]
        gate = 1.0 / (1.0 + jnp.exp(-embedding))
        time_ref[...] = total[...] * (gate + embedding * gate * (1.0 - gate))


def self_back_kernel(
    q_ref,
    k_ref,
    v_ref,
    grad_ref,
    log_ref,
    code_column_ref,
    code_row_ref,
    normed_ref,
    grad_q_ref,
    grad_k_ref,
    grad_v_ref,
    out_even_ref,
    out_odd_ref,
    bias_ref,
    normed_t,
    *core,
    key_split,
    met,
):
    step = pl.program_id(0)

    @pl.when(step == 0)
    def _():
        normed_t[...] = normed_ref[...].T

    attend_back_kernel(
        q_ref,
        k_ref,
        v_ref,
        grad_ref,
        log_ref,
        code_column_ref,
        code_row_ref,
        grad_q_ref,
        grad_k_ref,
        grad_v_ref,
        bias_ref,
        key_split=key_split,
    )
    pieces = jnp.concatenate([grad_q_ref[...], grad_k_ref[...], grad_v_ref[...]], axis=1)
    weight = rows_dot(normed_t[...], pieces).astype(low_type)
    if not core:
        out_even_ref[0] = weight
        return
    part, part_in, send, receive = core

    def core_copy(index):
        mine, peer = place(0)
        return remote(
            part.at[lax.rem(index, 2), :, :, 1 - mine],
            part_in.at[index],
            send.at[index],
            receive.at[index],
            peer,
        )

    def settle(index):
        core_copy(index).wait()
        total = part[lax.rem(index, 2), :, :, place(0)[0]] + part_in[index]

        @pl.when(lax.rem(index, 2) == 0)
        def _():
            out_even_ref[:, :, index // 2] = total

        @pl.when(lax.rem(index, 2) == 1)
        def _():
            for side in range(2):
                out_odd_ref[:, :, side, index // 2] = total[:, :, side]

    part[lax.rem(step, 2)] = weight.reshape(part.shape[1:])

    @pl.when(step == 0)
    def _():
        meet(met)

    core_copy(step).start()

    @pl.when(step > 0)
    def _():
        settle(step - 1)

    @pl.when(step == pl.num_programs(0) - 1)
    def _():
        settle(step)


def finish_kernel(
    start_ref,
    side_ref,
    spot_ref,
    big_ref,
    wide_ref,
    own_ref,
    partner_ref,
    table_a_ref,
    table_b_ref,
    table_c_ref,
    up_ref,
    even_ref,
    odd_ref,
    kv_ref,
    out_ref,
    time_ref,
    frames_grad_ref,
    text_grad_ref,
    grad_w_mod_ref,
    grad_b_mod_ref,
    sum_up_ref,
    sum_qkv_ref,
    sum_kv_ref,
    sum_out_ref,
    bias_ref,
    time_out_ref,
    item_total_ref,
):
    tables = (table_a_ref, table_b_ref, table_c_ref)
    step = pl.program_id(0)
    rows = frames_grad_ref.shape[0]
    half = pl.num_programs(0) * rows // 2
    frames_grad_ref[...] = rows_from(wide_ref, half - start_ref[0], step * rows, rows)
    mine = step // (pl.num_programs(0) // 2) == side_ref[0]

    @pl.when(mine)
    def _():
        text_grad_ref[...] = own_ref[...]

    @pl.when(jnp.logical_not(mine))
    def _():
        text_grad_ref[...] = partner_ref[...].astype(jnp.float32)

    @pl.when(step == 0)
    def _():
        share, columns = grad_w_mod_ref.shape
        width = columns // 8
        entry = lax.broadcasted_iota(jnp.int32, (width, share), 0)
        wanted = lax.broadcasted_iota(jnp.int32, (width, share), 1) + spot_ref[0] * share
        chosen = jnp.where(entry == wanted, 1.0, 0.0).astype(low_type)
        own = rows_dot(tables[2][:, tables[2].shape[1] - width :], chosen)
        item = lax.broadcasted_iota(jnp.int32, own.shape, 0)
        shape = (8, tables[2].shape[0])
        row_half = lax.rem(lax.broadcasted_iota(jnp.int32, shape, 1) // 4, 2)
        picked = jnp.where(row_half == lax.broadcasted_iota(jnp.int32, shape, 0), 1.0, 0.0).astype(
            low_type
        )
        kept = [
            jnp.where(lax.rem(item // 4, 2) == part, own, 0.0).astype(low_type) for part in range(2)
        ]
        at = 0
        for table_ref, parts in zip(tables, (2, 3, 3)):
            cut = parts * width // 2
            table = table_ref[:, :cut]
            totals = rows_dot(picked, table)
            for part in range(2):
                grad_w_mod_ref[:, at : at + cut] = left_dot(kept[part], table)
                item_total_ref[:, at : at + cut] = totals[part : part + 1]
                at += cut
        chunk = up_ref.shape[3]
        for index in range(up_ref.shape[1]):
            for side in range(2):
                rows_here = slice(side * up_ref.shape[2], (side + 1) * up_ref.shape[2])
                sum_up_ref[rows_here, index * chunk : (index + 1) * chunk] = up_ref[side, index]
        piece = even_ref.shape[2] // 3
        for index in range(2 * even_ref.shape[0]):
            for kind in range(3):
                span = slice(kind * width + index * piece, kind * width + (index + 1) * piece)
                cut = slice(kind * piece, (kind + 1) * piece)
                if index % 2 == 0:
                    sum_qkv_ref[:, span] = even_ref[index // 2, :, cut]
                    continue
                for side in range(2):
                    rows_here = slice(side * odd_ref.shape[2], (side + 1) * odd_ref.shape[2])
                    sum_qkv_ref[rows_here, span] = odd_ref[side, index // 2, :, cut]
        size = grad_b_mod_ref.shape[1]
        totals = jnp.broadcast_to(item_total_ref[...], (8, columns))
        turn = lax.rem(columns - spot_ref[0] * size, columns)
        grad_b_mod_ref[...] = pltpu.roll(totals, turn, 1)[0:1, :size]
        sum_out_ref[...] = out_ref[:share, :]
        spread_bias = out_ref[share : share + 8, :]
        turned = pltpu.roll(spread_bias, lax.rem(width - spot_ref[0] * share, width), 1)
        at = spot_ref[0] * 4 * share
        offset = lax.rem(at, width)
        wanted = at // width
        up_rows = pltpu.roll(spread_bias, lax.rem(width - offset, width), 1)
        row = lax.broadcasted_iota(jnp.int32, up_rows.shape, 0)
        up = jnp.sum(jnp.where(row == wanted + 3, up_rows, 0.0), axis=0, keepdims=True)
        bias_ref[0:1, :share] = turned[0:1, :share]
        bias_ref[1:2, :share] = turned[2:3, :share]
        bias_ref[2:3, :share] = turned[1:2, :share]
        bias_ref[3:4, : 4 * share] = up[:, : 4 * share]
        for item in range(ITEMS):
            time_out_ref[item : item + 1, :] = time_ref[
                pl.ds(lax.rem(item - big_ref[0] + ITEMS, ITEMS), 1), :
            ]
        for part in range(2):
            for side in range(2):
                rows_here = slice(side * kv_ref.shape[2], (side + 1) * kv_ref.shape[2])
                sum_kv_ref[rows_here, part * width : (part + 1) * width] = kv_ref[side, part]


def row_blocks(array, block=ROW_BLOCK):
    return pl.BlockSpec((block,) + tuple(array.shape[1:]), lambda step, *_: (step, 0))


def column_blocks(array, block=ROW_BLOCK):
    return pl.BlockSpec((array.shape[0], block), lambda step, *_: (0, step))


def shape_of(shape, kind):
    return jax.ShapeDtypeStruct(shape, kind)


MESH = pl.DeviceIdType.MESH


def place(label):
    spot = lax.axis_index("frames")
    side = lax.axis_index("text")
    if label == "text":
        return side, (spot, 1 - side)
    mine = lax.rem(spot // (1 << label), 2)
    return mine, (spot + (1 << label) * (1 - 2 * mine), side)


def greet(labels):
    for label in labels:
        pl.semaphore_signal(
            pltpu.get_barrier_semaphore(),
            inc=1,
            device_id=place(label)[1],
            device_id_type=MESH,
        )


def meet(labels):
    pl.semaphore_wait(pltpu.get_barrier_semaphore(), len(labels))


class Reduction:
    def __init__(self, labels, hops, source, out, buffers, send, receive, base):
        self.labels, self.hops, self.current, self.out = list(labels), hops, source, out
        self.buffers, self.send, self.receive, self.base = buffers, send, receive, base

    def copy(self, hop):
        kind, label = self.hops[hop]
        mine, peer = place(label)
        source = self.current
        if kind == "split":
            source = source.at[(slice(None),) * self.labels.index(label) + (1 - mine,)]
        return pltpu.make_async_remote_copy(
            src_ref=source,
            dst_ref=self.buffers[hop],
            send_sem=self.send.at[self.base + hop],
            recv_sem=self.receive.at[self.base + hop],
            device_id=peer,
            device_id_type=MESH,
        )

    def start(self, hop):
        if hop < len(self.hops):
            self.copy(hop).start()

    def finish(self, hop):
        if hop >= len(self.hops):
            return
        self.copy(hop).wait()
        kind, label = self.hops[hop]
        mine = place(label)[0]
        buffer, current = self.buffers[hop], self.current
        if kind == "split":
            dim = self.labels.index(label)
            rest = len(self.labels) - 1

            target = self.out if hop == len(self.hops) - 1 else buffer

            def body(index, _):
                spot = tuple(lax.rem(index // (1 << (rest - 1 - d)), 2) for d in range(rest))
                target[spot] = current[spot[:dim] + (mine,) + spot[dim:]] + buffer[spot]
                return 0

            if rest:
                lax.fori_loop(0, 1 << rest, body, 0)
            else:
                target[...] = current[mine] + buffer[...]
            self.labels.pop(dim)
            self.current = buffer
        elif kind == "sum":
            buffer[...] = current[...] + buffer[...]
            self.current = buffer
            if hop == len(self.hops) - 1:
                self.out[...] = buffer[...]
        elif kind == "swap":
            self.out[...] = buffer[...]
        elif kind == "full":
            self.out[...] = current[...].astype(jnp.float32) + buffer[...].astype(jnp.float32)
        else:
            self.out[mine] = current[...].astype(jnp.float32)
            self.out[1 - mine] = buffer[...].astype(jnp.float32)


class Gathering:
    def __init__(self, hops, source, out, buffer, send, receive, base):
        self.hops, self.source, self.out, self.buffer = hops, source, out, buffer
        self.send, self.receive, self.base = send, receive, base

    def block(self, hop):
        return tuple(place(label)[0] for label in self.hops[hop:][::-1])

    def copy(self, hop):
        where = self.block(hop)
        return pltpu.make_async_remote_copy(
            src_ref=self.buffer.at[where],
            dst_ref=self.buffer.at[where],
            send_sem=self.send.at[self.base + hop],
            recv_sem=self.receive.at[self.base + hop],
            device_id=place(self.hops[hop])[1],
            device_id_type=MESH,
        )

    def start(self, hop):
        if hop == 0:
            self.buffer[self.block(0)] = self.source[...]
        if hop < len(self.hops):
            self.copy(hop).start()

    def finish(self, hop):
        if hop < len(self.hops):
            self.copy(hop).wait()
        if hop == len(self.hops) - 1:
            self.out[...] = self.buffer[...]


def greeted(plans):
    labels = set()
    for names, hops in plans:
        labels |= set(hops) if names is None else {label for _, label in hops}
    return sorted(labels, key=str)


def exchange_parts(arrays, plans):
    outs, scratch, total = [], [], 0
    for array, (labels, hops) in zip(arrays, plans):
        total += len(hops)
        if labels is None:
            shape = (2,) * len(hops) + array.shape
            scratch.append(pltpu.VMEM(shape, array.dtype))
            outs.append(jax.ShapeDtypeStruct(shape, array.dtype))
            continue
        names, shape = list(labels), list(array.shape)
        for kind, label in hops:
            if kind == "split":
                dim = names.index(label)
                names.pop(dim)
                shape.pop(dim)
            scratch.append(pltpu.VMEM(tuple(shape), array.dtype))
        kind = hops[-1][0]
        lead = (2,) if kind == "gather" else ()
        wide = array.dtype if kind in ("split", "swap", "sum") else jnp.float32
        outs.append(jax.ShapeDtypeStruct(lead + tuple(shape), wide))
    semaphores = pltpu.SemaphoreType.DMA((total,))
    return outs, scratch + [semaphores, semaphores]


def make_flows(plans, sources, outs, rest):
    send, receive = rest[-2:]
    flows, base, used = [], 0, 0
    for (labels, hops), source, out in zip(plans, sources, outs):
        if labels is None:
            flows.append(Gathering(hops, source, out, rest[used], send, receive, base))
            used += 1
        else:
            buffers = rest[used : used + len(hops)]
            flows.append(Reduction(labels, hops, source, out, buffers, send, receive, base))
            used += len(hops)
        base += len(hops)
    return flows


def with_exchange(kernel, counts, arrays, plans, ends, begins, others):
    labels = sorted(set(greeted(plans)) | set(others), key=str)

    def body(*refs):
        groups, at = [], 0
        for count in counts:
            groups.append(refs[at : at + count])
            at += count
        scalars, inputs, given, outputs, targets, scratch, rest = groups
        given = list(given)
        sources = [outputs[a] if isinstance(a, int) else given.pop(0) for a in arrays]
        flows = make_flows(plans, sources, targets, rest)
        step = pl.program_id(0)

        @pl.when(step == 0)
        def _():
            greet(labels)

        kernel(*scalars, *inputs, *outputs, *scratch)

        @pl.when(step == 0)
        def _():
            if not others:
                meet(labels)

        times = set(begins) | {end for flow_ends in ends for end in flow_ends}
        for now in sorted(times):

            @pl.when(step == now)
            def _(now=now):
                for flow, begin in zip(flows, begins):
                    if begin == now:
                        flow.start(0)
                for hop in range(max(len(flow_ends) for flow_ends in ends)):
                    for flow, flow_ends in zip(flows, ends):
                        if hop < len(flow_ends) and flow_ends[hop] == now:
                            flow.finish(hop)
                            flow.start(hop + 1)

    return body


def whole(array):
    return pl.BlockSpec(
        array.shape, lambda step, *_: (0,) * len(array.shape), pipeline_mode=pl.Buffered(1)
    )


def run(
    kernel,
    name,
    grid,
    scalars,
    operands,
    specs,
    outs,
    out_specs,
    scratch,
    flops,
    exchange=None,
    transcendentals=0,
    collective=None,
    others=(),
):
    operands, specs, outs = list(operands), list(specs), list(outs)
    out_specs, scratch = list(out_specs), list(scratch)
    traffic = sum(a.size * a.dtype.itemsize for a in operands + outs)
    effects = {}
    if exchange is not None:
        arrays, plans, ends, collective = exchange[:4]
        begins = exchange[4] if len(exchange) > 4 else (0,) * len(arrays)
        shapes = [outs[a] if isinstance(a, int) else a for a in arrays]
        more_outs, more_scratch = exchange_parts(shapes, plans)
        given = [a for a in arrays if not isinstance(a, int)]
        counts = (
            len(scalars),
            len(operands),
            len(given),
            len(outs),
            len(more_outs),
            len(scratch),
            len(more_scratch),
        )
        kernel = with_exchange(kernel, counts, arrays, plans, ends, begins, others)
        operands += given
        specs += [whole(array) for array in given]
        outs += more_outs
        out_specs += [whole(array) for array in more_outs]
        scratch += more_scratch
    if collective is not None:
        effects = dict(collective_id=collective, has_side_effects=True)
    return pl.pallas_call(
        kernel,
        out_shape=outs,
        grid_spec=pltpu.PrefetchScalarGridSpec(
            num_scalar_prefetch=len(scalars),
            grid=(grid,),
            in_specs=specs,
            out_specs=out_specs,
            scratch_shapes=scratch,
        ),
        compiler_params=pltpu.CompilerParams(vmem_limit_bytes=GRANTS[name] << 20, **effects),
        cost_estimate=pl.CostEstimate(
            flops=flops, transcendentals=transcendentals, bytes_accessed=traffic
        ),
        name=name,
    )(*scalars, *operands)


GRANTS = dict(
    prepare=24,
    text_forward=24,
    enter=34,
    self_forward=20,
    middle=24,
    cross_forward=20,
    mlp=60,
    reduce_core=60,
    cross_backward=60,
    text_back=60,
    back_middle=60,
    self_backward=60,
    leave=60,
    finish=60,
)


def idle_kernel():
    pass


def swapped(value):
    return lax.ppermute(value, "text", [(0, 1), (1, 0)])


def on_device(
    frames_in,
    frame_item,
    text_in,
    text_len,
    time_embed,
    cotangent,
    w_mod,
    b_mod,
    w_qkv,
    w_out,
    b_out,
    w_q_cross,
    w_kv_cross,
    w_out_cross,
    b_out_cross,
    w_up,
    b_up,
    w_down,
    b_down,
):
    text_side = lax.axis_index("text")
    partner_side = 1 - text_side
    row_count, width = frames_in.shape
    half = row_count // 2
    hidden_width = w_up.shape[1]
    item_count = time_embed.shape[0]
    token_span = text_in.shape[1]
    token_rows = item_count * 2 * token_span
    share_count = lax.axis_size("frames")
    bits = share_count.bit_length() - 1
    spot = lax.axis_index("frames")
    partner_text = lax.dynamic_slice_in_dim(text_in, partner_side * item_count, item_count, 0)
    fetched_text = swapped(partner_text)
    pairs = width // LANES
    blocks = row_count // ROW_BLOCK
    matmul_flops = 2 * row_count * width * width

    scalar = jax.ShapeDtypeStruct((1,), jnp.int32)
    scalar_spec = pl.BlockSpec(memory_space=pltpu.SMEM)
    column = jax.ShapeDtypeStruct((row_count, 1), jnp.int32)
    token_column = jax.ShapeDtypeStruct((token_rows, 1), jnp.int32)
    row = jax.ShapeDtypeStruct((1, row_count), jnp.int32)
    both = (2 * item_count, width)
    mod_shape = jax.ShapeDtypeStruct((8, 2 * item_count, width), jnp.float32)
    outs = [
        mod_shape,
        scalar,
        scalar,
        column,
        row,
        token_column,
        jax.ShapeDtypeStruct(both, low_type),
        jax.ShapeDtypeStruct(both, jnp.float32),
    ]
    b_mod_row = b_mod.reshape(1, -1)
    mod, start_scalar, big_scalar, code_column, code_row, token_code, condition, embedding_rows = run(
        prepare_kernel,
        "prepare",
        8,
        (text_len,),
        (frame_item, time_embed, w_mod, b_mod_row),
        [
            whole(frame_item),
            whole(time_embed),
            column_blocks(w_mod, width),
            column_blocks(b_mod_row, width),
        ],
        outs,
        [pl.BlockSpec((1,) + mod_shape.shape[1:], lambda step, *_: (step, 0, 0))]
        + [scalar_spec] * 2
        + [whole(shape) for shape in outs[3:]],
        [pltpu.VMEM((item_count, width), jnp.float32)],
        0,
    )
    self_codes = (code_column, code_row)
    cross_codes = (token_code, code_row)

    def as_row(vector):
        return vector.astype(jnp.float32)[None, :]

    low_rows = shape_of((row_count, width), low_type)
    full_rows = shape_of((row_count, width), jnp.float32)
    square = shape_of((width, width), low_type)
    low_scratch = pltpu.VMEM((row_count, width), low_type)
    full_scratch = pltpu.VMEM((row_count, width), jnp.float32)
    wide_scratch = pltpu.VMEM((row_count + half + 8, width), jnp.float32)

    operands = (frames_in, cotangent, code_column, mod, w_qkv)
    packed_shape = shape_of((row_count, 3 * width), low_type)
    packed, normed_a, frames, upstream = run(
        enter_kernel,
        "enter",
        blocks,
        (start_scalar,),
        operands,
        [whole(frames_in), whole(cotangent), row_blocks(code_column), whole(mod), whole(w_qkv)],
        [packed_shape, low_rows, low_rows, low_rows],
        [row_blocks(packed_shape), row_blocks(low_rows), row_blocks(low_rows), row_blocks(low_rows)],
        [wide_scratch, wide_scratch],
        3 * matmul_flops,
    )
    packed_columns = (pairs, (0, pairs, 2 * pairs, 0))
    attended, self_log = attention_call(
        attend_kernel,
        "self_forward",
        (packed, packed, packed),
        packed_columns,
        self_codes,
        None,
        (row_count, "log"),
        half,
        row_count,
    )
    operands = (attended, frames, code_column, mod, w_out, as_row(b_out), w_q_cross)
    after_a, branch_a, normed_b, cross_q = run(
        middle_kernel,
        "middle",
        blocks,
        (),
        operands,
        [row_blocks(attended), row_blocks(frames), row_blocks(code_column)]
        + [whole(array) for array in operands[3:]],
        [full_rows, full_rows, low_rows, low_rows],
        [row_blocks(full_rows)] * 2 + [row_blocks(low_rows)] * 2,
        [],
        2 * matmul_flops,
    )
    text_rows = shape_of((token_rows, text_in.shape[2]), low_type)
    kv_rows = shape_of((token_rows, 2 * width), low_type)
    token_block = 2 * token_span
    side_scalar = text_side.reshape(1)
    text, text_kv = run(
        text_forward_kernel,
        "text_forward",
        item_count,
        (big_scalar, side_scalar),
        (text_in, fetched_text, w_kv_cross),
        [
            pl.BlockSpec(
                (1,) + text_in.shape[1:],
                lambda step, big_ref, side_ref: (
                    side_ref[0] * item_count + lax.rem(step + big_ref[0], item_count),
                    0,
                    0,
                ),
            ),
            pl.BlockSpec(
                (1,) + text_in.shape[1:],
                lambda step, big_ref, side_ref: (lax.rem(step + big_ref[0], item_count), 0, 0),
            ),
            whole(w_kv_cross),
        ],
        [text_rows, kv_rows],
        [row_blocks(text_rows, token_block), row_blocks(kv_rows, token_block)],
        [],
        2 * 2 * token_rows * width * width,
    )
    cross_columns = (pairs, (0, 0, pairs, 0))
    cross_out, cross_log = attention_call(
        attend_kernel,
        "cross_forward",
        (cross_q, text_kv, text_kv),
        cross_columns,
        cross_codes,
        None,
        (row_count, "log"),
        2 * token_span,
        token_rows,
    )
    frame_labels = tuple(range(bits))[::-1]
    frame_dims = (2,) * bits
    rest_labels, rest_dims = frame_labels[:-1], frame_dims[:-1]
    low_bits = [("split", bit) for bit in range(1, bits)]

    def shares(array):
        rows, columns = array.shape[-2:]
        return array.reshape(array.shape[:-2] + frame_dims + (rows // share_count, columns))

    def text_shares(array):
        rows, columns = array.shape[-2:]
        cut = (2, rows // share_count // 2, columns)
        return array.reshape(array.shape[:-2] + frame_dims + cut)

    def spread(count, low, top):
        return tuple(low + (top - low) * (hop + 1) // count for hop in range(count))

    chunks = 4
    chunk = hidden_width // chunks
    down_share, up_share = hidden_width // share_count, width // share_count
    chunk_pairs, pair_count = chunk // down_share // 2, share_count // 2
    in_core = down_share % 16 == 0 and up_share % 16 == 0
    operands = (
        cross_out,
        after_a,
        upstream,
        code_column,
        code_row,
        mod,
        w_out_cross,
        as_row(b_out_cross),
        as_row(b_down),
        w_up,
        as_row(b_up),
        w_down,
        condition,
    )
    bias_shape = shape_of((8, width), jnp.float32)
    sums_shape = shape_of((3, 8, width), jnp.float32)
    core_scratch = []
    if in_core:
        down_shape = shape_of((chunks, chunk_pairs // 2, down_share, width), low_type)
        up_shape = shape_of((chunks, pair_count, up_share // 2, chunk), low_type)
        weight_specs = [whole(down_shape), whole(up_shape)]
        core_scratch = [
            pltpu.VMEM((2, chunk_pairs // 2, 2, 2, down_share, width), low_type),
            pltpu.VMEM((2, pair_count, 2, 2, up_share // 2, chunk), low_type),
            pltpu.VMEM((chunks, chunk_pairs // 2, 2, down_share, width), low_type),
            pltpu.VMEM((chunks, pair_count, 2, up_share // 2, chunk), low_type),
            pltpu.VMEM(down_shape.shape, low_type),
            pltpu.VMEM(up_shape.shape, low_type),
            pltpu.SemaphoreType.DMA((chunks, 4)),
            pltpu.SemaphoreType.DMA((chunks, 4)),
        ]
    else:
        down_shape = shape_of((chunks, chunk, width), low_type)
        up_shape = shape_of((chunks, width, chunk), low_type)
        weight_specs = [
            pl.BlockSpec((1,) + shape.shape[1:], lambda step, *_: (step, 0, 0))
            for shape in (down_shape, up_shape)
        ]
    wide_shape = shape_of((row_count + half + 8, width), jnp.float32)
    outs = [wide_shape, full_rows, low_rows, down_shape, up_shape, square]
    table_c_shape = shape_of((2 * item_count, 3 * width // 2 + width), low_type)
    table_b_shape = shape_of((2 * item_count, 3 * width // 2), low_type)
    table_a_shape = shape_of((2 * item_count, width), low_type)
    outs += [bias_shape, sums_shape, table_c_shape]
    (
        wide_out,
        grad_after_b,
        grad_cross,
        part_down,
        part_up,
        grad_w_out_cross,
        grad_b_mlp,
        sums_c,
        table_c,
    ) = run(
        mlp_kernel,
        "mlp",
        chunks,
        (),
        operands,
        [whole(array) for array in operands[:9]]
        + [
            column_blocks(w_up, chunk),
            column_blocks(operands[10], chunk),
            row_blocks(w_down, chunk),
            whole(operands[12]),
        ],
        outs,
        [whole(wide_shape), whole(full_rows), whole(low_rows)]
        + weight_specs
        + [
            whole(square),
            whole(bias_shape),
            whole(sums_shape),
            whole(table_c_shape),
        ],
        [
            low_scratch,
            pltpu.VMEM((width, row_count), low_type),
            low_scratch,
            full_scratch,
            pltpu.VMEM((row_count, chunk), low_type),
            pltpu.VMEM((row_count, chunk), low_type),
        ]
        + core_scratch,
        26 * matmul_flops,
        collective=0 if in_core else None,
    )
    chunk_labels = ("chunk", "block")
    if in_core:
        part_down = part_down.reshape(rest_dims[:-1] + (2, down_share // 2, width))
        part_up = part_up.reshape((2, 2) + rest_dims + (up_share // 2, chunk))
    else:
        part_down, part_up = run(
            idle_kernel,
            "reduce_core",
            1,
            (),
            (),
            [],
            [],
            [],
            [],
            0,
            (
                [
                    text_shares(part_down.reshape(hidden_width, width)),
                    text_shares(part_up.reshape(2, 2, width, chunk)),
                ],
                [
                    (frame_labels + ("text",), [("split", 0), ("split", 1)]),
                    (
                        chunk_labels + frame_labels + ("text",),
                        [("split", 0), ("split", "text")],
                    ),
                ],
                [(0, 0), (0, 0)],
                6,
            ),
        )

    gather_hops = tuple(range(1, bits))[::-1] + ("text", 0)
    all_labels = tuple(range(bits)) + ("text",)
    (
        low_cross_q,
        grad_text_k,
        grad_text_v,
        table_c,
        part_down,
        part_up,
    ) = attention_call(
        attend_back_kernel,
        "cross_backward",
        (cross_q, text_kv, text_kv, grad_cross),
        cross_columns,
        cross_codes,
        cross_log,
        (row_count, token_rows, token_rows),
        2 * token_span,
        token_rows,
        (
            [table_c, part_down, part_up],
            [
                (None, gather_hops[:-2]),
                (rest_labels[:-1] + ("text",), [("split", "text")]),
                (chunk_labels + rest_labels, low_bits[:1]),
            ],
            [
                spread(bits - 1, -1, pairs - 1),
                (pairs - 3,),
                (pairs - 3,),
            ],
            1,
        ),
    )
    half_text = (item_count, token_span, text.shape[1])
    own_shape, sent_shape = shape_of(half_text, jnp.float32), shape_of(half_text, low_type)
    kv_shape = shape_of((2, text.shape[1], width), low_type)
    operands = (grad_text_k, grad_text_v, text, w_kv_cross, wide_out)
    item_spec = pl.BlockSpec(
        (1,) + half_text[1:], lambda step, big_ref, _: (lax.rem(step + big_ref[0], item_count), 0, 0)
    )
    own_text_grad, sent_text_grad, grad_w_kv, frames_out = run(
        text_back_kernel,
        "text_back",
        item_count,
        (big_scalar, start_scalar),
        operands,
        [row_blocks(array, token_block) for array in operands[:3]]
        + [whole(w_kv_cross), whole(wide_out)],
        [own_shape, sent_shape, kv_shape, full_rows],
        [item_spec, item_spec, whole(kv_shape), row_blocks(full_rows, row_count // item_count)],
        [pltpu.VMEM((token_rows, width), low_type)] * 2
        + [pltpu.VMEM((token_rows, text.shape[1]), low_type)],
        4 * 2 * token_rows * width * width,
    )
    operands = (
        low_cross_q,
        normed_b,
        after_a,
        grad_after_b,
        branch_a,
        attended,
        code_column,
        code_row,
        mod,
        w_q_cross,
        w_out,
        grad_b_mlp,
    )
    out_rows = up_share + 16
    out_shape = shape_of((share_count, out_rows, width), low_type) if in_core else square
    (
        grad_after_a,
        grad_attended,
        grad_w_q_cross,
        grad_w_out,
        grad_b_middle,
        sums_b,
        table_b,
        table_c,
        part_down,
        part_up,
        part_kv,
    ) = run(
        back_middle_kernel,
        "back_middle",
        blocks,
        (),
        operands,
        [row_blocks(array) for array in operands[:7]]
        + [column_blocks(code_row)]
        + [whole(array) for array in operands[8:]],
        [full_rows, low_rows, square, out_shape, bias_shape, sums_shape, table_b_shape],
        [row_blocks(full_rows), row_blocks(low_rows), whole(square), whole(out_shape)]
        + [whole(bias_shape), whole(sums_shape), whole(table_b_shape)],
        [low_scratch] * 4,
        4 * matmul_flops,
        (
            [table_c, part_down, part_up, text_shares(grad_w_kv)],
            [
                (None, gather_hops[-2:]),
                (rest_labels[:-1], low_bits[1:2]),
                (chunk_labels + rest_labels[:-1], low_bits[1:2]),
                (("pair",) + frame_labels + ("text",), [("split", 0), ("split", 1)]),
            ],
            [
                (blocks - 2, blocks - 1),
                (blocks - 1,),
                (blocks - 1,),
                (0, blocks - 1),
            ],
            2,
        ),
    )
    piece = 3 * LANES
    even_pairs = pairs - pairs // 2
    if not in_core:
        grad_w_out = jnp.concatenate(
            [
                grad_w_out.reshape(share_count, up_share, width),
                jnp.broadcast_to(
                    jnp.concatenate([grad_b_middle] * 2, axis=0).astype(low_type)[None],
                    (share_count, 16, width),
                ),
            ],
            axis=1,
        )
    part_out = grad_w_out.reshape(frame_dims + (2, out_rows // 2, width))
    if in_core:
        lead = pair_count // 2
        even_shape = shape_of((lead, 2, even_pairs, 2, up_share // 2, piece), low_type)
        odd_shape = shape_of((lead, 2, 2, pairs // 2, up_share // 2, piece), low_type)
        core_scratch = [
            pltpu.VMEM((2, lead, 2, 2, 2, up_share // 2, piece), low_type),
            pltpu.VMEM((pairs, lead, 2, 2, up_share // 2, piece), low_type),
            pltpu.SemaphoreType.DMA((pairs,)),
            pltpu.SemaphoreType.DMA((pairs,)),
        ]
        weight_specs = [whole(even_shape), whole(odd_shape)]
    else:
        even_shape = shape_of((pairs, width, piece), low_type)
        odd_shape = shape_of((8, LANES), low_type)
        core_scratch = []
        weight_specs = [
            pl.BlockSpec((1, width, piece), lambda step, *_: (step, 0, 0)),
            whole(odd_shape),
        ]
    pair_block = pl.BlockSpec((row_count, LANES), lambda step: (0, step))
    (
        grad_q,
        grad_k,
        grad_v,
        part_even,
        part_odd,
        table_b,
        sum_w_down,
        sum_w_up,
        part_kv,
        part_q_cross,
        part_out_cross,
        part_out,
    ) = run(
        functools.partial(self_back_kernel, key_split=half, met=all_labels),
        "self_backward",
        pairs,
        (),
        (packed, packed, packed, grad_attended, self_log, code_column, code_row, normed_a),
        [
            pl.BlockSpec((row_count, LANES), lambda step, offset=offset: (0, offset + step))
            for offset in packed_columns[1]
        ]
        + [pl.BlockSpec((1, 8, row_count), lambda step: (step, 0, 0))]
        + [whole(array) for array in (code_column, code_row, normed_a)],
        [low_rows, low_rows, low_rows, even_shape, odd_shape],
        [pair_block] * 3 + weight_specs,
        [pltpu.VMEM((half, half), jnp.float32), pltpu.VMEM((width, row_count), low_type)]
        + core_scratch,
        8 * matmul_flops,
        (
            [
                table_b,
                part_down,
                part_up,
                part_kv,
                text_shares(grad_w_q_cross),
                text_shares(grad_w_out_cross),
                part_out,
            ],
            [
                (None, gather_hops),
                (rest_labels[:-2], low_bits[2:] + [("gather", "text")]),
                (chunk_labels + rest_labels[:-2], low_bits[2:] + [("gather", "text")]),
                (("pair",) + rest_labels[:-1] + ("text",), [("split", "text")]),
                (frame_labels + ("text",), [("split", 0), ("split", "text"), ("split", 1)]),
                (frame_labels + ("text",), [("split", 0), ("split", 1), ("split", "text")]),
                (frame_labels + ("text",), [("split", 0), ("split", 1)]),
            ],
            [
                spread(bits + 1, 0, pairs - 1),
                spread(bits - 2, 0, pairs - 2),
                spread(bits - 2, 0, pairs - 2),
                (pairs - 2,),
                (0, pairs - 3, pairs - 1),
                (0, pairs - 3, pairs - 1),
                (0, pairs - 2),
            ],
            3,
        ),
        others=all_labels if in_core else (),
    )
    even_labels, odd_labels = rest_labels, rest_labels + ("text",)
    if in_core:
        part_even = part_even.reshape(rest_dims + (even_pairs, up_share, piece))
        part_odd = part_odd.reshape(rest_dims + (2, pairs // 2, up_share // 2, piece))
    else:
        by_pair = part_even.reshape((pairs,) + frame_dims + (up_share, piece))
        part_even = jnp.moveaxis(by_pair[0::2], 0, bits)
        part_odd = by_pair[1::2].reshape(
            (pairs // 2,) + frame_dims + (2, up_share // 2, piece)
        )
        part_even, part_odd = run(
            idle_kernel,
            "reduce_core",
            1,
            (),
            (),
            [],
            [],
            [],
            [],
            0,
            (
                [part_even, jnp.moveaxis(part_odd, 0, bits + 1)],
                [
                    (frame_labels, [("split", 0)]),
                    (frame_labels + ("text",), [("split", 0)]),
                ],
                [(0,), (0,)],
                7,
            ),
        )
    operands = (
        grad_q,
        grad_k,
        grad_v,
        frames,
        grad_after_a,
        code_column,
        code_row,
        mod,
        w_qkv,
        sums_b,
        sums_c,
        embedding_rows,
        w_mod,
    )
    mod_columns = 8 * width
    time_rows = shape_of((8, width), jnp.float32)
    last_block = blocks - 1
    steps = blocks + 8
    late = steps - 1

    def early(array):
        return pl.BlockSpec(
            (ROW_BLOCK, array.shape[1]), lambda step: (jnp.minimum(step, last_block), 0)
        )

    (
        wide_grad,
        _,
        time_grad,
        table_a,
        sum_even,
        sum_odd,
        sum_kv,
        sum_q_cross,
        sum_out_cross,
        sum_out,
        partner_text_grad,
    ) = run(
        leave_kernel,
        "leave",
        steps,
        (),
        operands,
        [early(array) for array in operands[:6]]
        + [pl.BlockSpec((1, ROW_BLOCK), lambda step: (0, jnp.minimum(step, last_block)))]
        + [whole(array) for array in operands[7:12]]
        + [pl.BlockSpec((width, width), lambda step: (0, jnp.maximum(step - blocks, 0)))],
        [wide_shape, table_a_shape, time_rows],
        [whole(wide_shape), whole(table_a_shape), whole(time_rows)],
        [
            pltpu.VMEM((2, 8, width), jnp.float32),
            pltpu.VMEM((8, 8, width), low_type),
            pltpu.VMEM((8, width), jnp.float32),
        ],
        4 * matmul_flops,
        (
            [1, part_even, part_odd, part_kv, part_q_cross, part_out_cross, part_out, sent_text_grad],
            [
                (None, gather_hops),
                (even_labels, low_bits + [("full", "text")]),
                (odd_labels, [("split", "text")] + low_bits + [("gather", "text")]),
                (("pair",) + rest_labels[:-1], low_bits[1:] + [("gather", "text")]),
                (rest_labels[:-1], low_bits[1:] + [("gather", "text")]),
                (rest_labels[:-1], low_bits[1:] + [("gather", "text")]),
                (
                    rest_labels[:-1] + ("text",),
                    [("split", "text")] + low_bits[1:] + [("gather", "text")],
                ),
                ((), [("swap", "text")]),
            ],
            [
                spread(bits + 1, blocks + 2, late),
                (blocks + 1,) + spread(bits - 1, blocks + 4, late),
                (blocks + 1,) + spread(bits, blocks + 4, late),
                spread(bits - 1, last_block - 2, late),
                spread(bits - 1, last_block - 2, late),
                spread(bits - 1, last_block - 2, late),
                spread(bits, last_block, late),
                (late,),
            ],
            4,
            (last_block,) + (0,) * 6 + (blocks + 1,),
        ),
    )
    text_pair = item_count // 2
    text_shape = shape_of((2 * item_count,) + half_text[1:], jnp.float32)

    def text_spec(turn):
        return pl.BlockSpec(
            (text_pair,) + half_text[1:],
            (lambda step, *_: (lax.rem(step, 2), 0, 0)) if turn else (lambda step, *_: (step, 0, 0)),
        )

    operands = (
        wide_grad,
        own_text_grad,
        partner_text_grad,
        table_a.reshape(-1, width),
        table_b.reshape(-1, table_b.shape[-1]),
        table_c.reshape(-1, table_c.shape[-1]),
        sum_w_up.reshape(2, chunks, up_share // 2, chunk),
        sum_even,
        sum_odd,
        sum_kv,
        sum_out.reshape(out_rows, width),
        time_grad,
    )
    mod_shape = shape_of((up_share, mod_columns), jnp.float32)
    b_mod_shape = shape_of((1, mod_columns // share_count), jnp.float32)
    sum_up_shape = shape_of((up_share, hidden_width), jnp.float32)
    sum_qkv_shape = shape_of((up_share, 3 * width), jnp.float32)
    sum_kv_shape = shape_of((up_share, 2 * width), jnp.float32)
    sum_out_shape = shape_of((up_share, width), jnp.float32)
    biases_shape = shape_of((4, 4 * up_share), jnp.float32)
    time_shape = shape_of((item_count, width), jnp.float32)
    more = [mod_shape, b_mod_shape, sum_up_shape, sum_qkv_shape, sum_kv_shape]
    more += [sum_out_shape, biases_shape, time_shape]
    (
        frames_grad,
        text_grad,
        grad_w_mod,
        grad_b_mod,
        sum_w_up,
        sum_qkv,
        sum_kv,
        sum_out,
        biases,
        time_grad,
    ) = run(
        finish_kernel,
        "finish",
        4,
        (start_scalar, side_scalar, spot.reshape(1), big_scalar),
        operands,
        [whole(wide_grad), text_spec(True), text_spec(True)] + [whole(a) for a in operands[3:]],
        [full_rows, text_shape] + more,
        [row_blocks(full_rows, row_count // 4), text_spec(False)] + [whole(a) for a in more],
        [pltpu.VMEM((1, mod_columns), jnp.float32)],
        0,
    )
    bias_cuts = [
        biases[0, :up_share],
        biases[1, :up_share],
        biases[3],
        biases[2, :up_share],
    ]
    return (
        frames_out,
        frames_grad,
        text_grad,
        time_grad,
        grad_w_mod,
        grad_b_mod[0],
        sum_qkv,
        sum_out,
        bias_cuts[0],
        sum_q_cross.reshape(up_share, width),
        sum_kv,
        sum_out_cross.reshape(up_share, width),
        bias_cuts[1],
        sum_w_up,
        bias_cuts[2],
        sum_w_down.reshape(down_share, width),
        bias_cuts[3],
    )


def solution(mesh):
    in_specs = (
        P(("frames", "text"), None),
        P("frames", None),
        P("frames", "text", None),
        P("frames"),
        P(("frames", "text"), None),
        P(("frames", "text"), None),
    ) + (P(),) * 13
    out_specs = (
        P(("frames", "text"), None),
        P(("frames", "text"), None),
        P("frames", "text", None),
        P(("frames", "text"), None),
        P("frames", None),
        P("frames"),
        P("frames", None),
        P("frames", None),
        P("frames"),
        P("frames", None),
        P("frames", None),
        P("frames", None),
        P("frames"),
        P("frames", None),
        P("frames"),
        P("frames", None),
        P("frames"),
    )
    return jax.shard_map(
        on_device, mesh=mesh, in_specs=in_specs, out_specs=out_specs, check_vma=False
    )
```

```python
import functools

import jax
import jax.numpy as jnp
from jax import lax
from jax.experimental import pallas as pl
from jax.experimental.pallas import tpu as pltpu
from jax.sharding import PartitionSpec as P

HEAD_DIM = 64
LANES = 128
VMEM_LIMIT = 60 << 20

epsilon = 1e-06
masked_add = -1000000000.0
highest = lax.Precision.HIGHEST
low_type = jnp.bfloat16


def rows_dot(left_side, right_side):
    return jnp.dot(left_side, right_side, preferred_element_type=jnp.float32)


def left_dot(left_side, right_side):
    return lax.dot_general(
        left_side, right_side, (((0,), (0,)), ((), ())), preferred_element_type=jnp.float32
    )


def right_dot(left_side, right_side):
    return lax.dot_general(
        left_side, right_side, (((1,), (1,)), ((), ())), preferred_element_type=jnp.float32
    )


def layer_norm(values):
    center = values - jnp.mean(values, axis=-1, keepdims=True)
    spread = jnp.mean(center * center, axis=-1, keepdims=True)
    return center * lax.rsqrt(spread + epsilon)


def modulate(values, shift_by, scale_by):
    return layer_norm(values) * (1.0 + scale_by) + shift_by


def gelu_tanh(inputs):
    return (
        0.5
        * inputs
        * (1.0 + jnp.tanh(0.7978845608028654 * (inputs + 0.044715 * inputs * inputs * inputs)))
    )


def head_lanes(value, head, scale=None):
    lane = lax.broadcasted_iota(jnp.int32, value.shape, 1)
    scaled = value if scale is None else value * jnp.asarray(scale, value.dtype)
    return jnp.where(lane // HEAD_DIM == head, scaled, jnp.zeros_like(scaled))


def fill_bias(code_column_ref, code_row_ref, bias_refs, key_split):
    half = code_row_ref.shape[1] // 2
    spans = ((0, key_split), (key_split, code_column_ref.shape[0]))
    for part, bias_ref in enumerate(bias_refs):
        if bias_ref is None:
            continue
        low, top = spans[part]
        bias_ref[...] = jnp.where(
            code_column_ref[low:top, :] == code_row_ref[:, part * half : (part + 1) * half],
            0.0,
            masked_add,
        )


def attend_kernel(
    q_ref, k_ref, v_ref, code_column_ref, code_row_ref, out_ref, log_ref, *bias_refs, key_split
):
    half = q_ref.shape[0] // 2
    scale = HEAD_DIM ** (-0.5)
    if len(bias_refs) == 1:
        bias_refs = (None,) + bias_refs

    @pl.when(pl.program_id(0) == 0)
    def _():
        fill_bias(code_column_ref, code_row_ref, bias_refs, key_split)

    value_t = v_ref[...].T
    key_spans = (slice(0, key_split), slice(key_split, k_ref.shape[0]))
    units = [(part, head) for part in range(2) for head in range(2)]

    def scores_of(part, head):
        queries = q_ref[part * half : (part + 1) * half, :]
        scores = right_dot(k_ref[key_spans[part], :], head_lanes(queries, head, scale))
        return scores if bias_refs[part] is None else scores + bias_refs[part][...]

    ahead = scores_of(*units[0])
    outs = []
    for index, (part, head) in enumerate(units):
        scores = ahead
        if index + 1 < len(units):
            ahead = scores_of(*units[index + 1])
        rows = slice(part * half, (part + 1) * half)
        peak = jnp.max(scores, axis=0, keepdims=True)
        exponent = jnp.exp(scores - peak)
        total = jnp.sum(exponent, axis=0, keepdims=True)
        log_ref[0, head : head + 1, rows] = peak + jnp.log(total)
        lanes = slice(HEAD_DIM * head, HEAD_DIM * (head + 1))
        outs.append(
            rows_dot(value_t[lanes, key_spans[part]], exponent.astype(low_type)) / total
        )
        if head == 1:
            out_ref[rows, :] = jnp.concatenate(outs, axis=0).T.astype(low_type)
            outs = []


def attend_back_kernel(
    q_ref,
    k_ref,
    v_ref,
    grad_ref,
    log_ref,
    code_column_ref,
    code_row_ref,
    grad_q_ref,
    grad_k_ref,
    grad_v_ref,
    *bias_refs,
    key_split,
):
    half = q_ref.shape[0] // 2
    scale = HEAD_DIM ** (-0.5)
    if len(bias_refs) == 1:
        bias_refs = (None,) + bias_refs

    @pl.when(pl.program_id(0) == 0)
    def _():
        fill_bias(code_column_ref, code_row_ref, bias_refs, key_split)

    key_t = k_ref[...].T
    key_spans = (slice(0, key_split), slice(key_split, k_ref.shape[0]))
    units = [(part, head) for part in range(2) for head in range(2)]

    def products_of(part, head):
        rows = slice(part * half, (part + 1) * half)
        query_head = head_lanes(q_ref[rows, :], head, scale)
        grad_head = head_lanes(grad_ref[rows, :], head)
        scores = right_dot(k_ref[key_spans[part], :], query_head)
        if bias_refs[part] is not None:
            scores = scores + bias_refs[part][...]
        grad_prob = right_dot(v_ref[key_spans[part], :], grad_head)
        return scores, grad_prob, query_head, grad_head

    ahead = products_of(*units[0])
    grad_q, grad_k, grad_v = [], [], []
    for index, (part, head) in enumerate(units):
        scores, grad_prob, query_head, grad_head = ahead
        if index + 1 < len(units):
            ahead = products_of(*units[index + 1])
        rows = slice(part * half, (part + 1) * half)
        prob = jnp.exp(scores - log_ref[0, head : head + 1, rows])
        weighted = prob * grad_prob
        delta = jnp.sum(weighted, axis=0, keepdims=True)
        grad_scores = (weighted - prob * delta).astype(low_type)
        grad_k.append(rows_dot(grad_scores, query_head))
        grad_v.append(rows_dot(prob.astype(low_type), grad_head))
        lanes = slice(HEAD_DIM * head, HEAD_DIM * (head + 1))
        grad_q.append(rows_dot(key_t[lanes, key_spans[part]], grad_scores) * scale)
        if head == 1:
            grad_q_ref[rows, :] = jnp.concatenate(grad_q, axis=0).T.astype(low_type)
            grad_k_ref[key_spans[part], :] = (grad_k[0] + grad_k[1]).astype(low_type)
            grad_v_ref[key_spans[part], :] = (grad_v[0] + grad_v[1]).astype(low_type)
            grad_q, grad_k, grad_v = [], [], []


def attention_call(
    kernel, name, operands, columns, codes, log_total, outs, key_split, key_rows, exchange=None
):
    rows = codes[1].shape[1]
    half = rows // 2
    pairs, offsets = columns
    specs = [
        pl.BlockSpec((array.shape[0], LANES), lambda step, offset=offset: (0, offset + step))
        for array, offset in zip(operands, offsets)
    ]
    extra = []
    log_spec = pl.BlockSpec((1, 8, rows), lambda step: (step, 0, 0))
    if log_total is not None:
        specs.append(log_spec)
        extra.append(log_total)
    specs += [whole(code) for code in codes]
    out_shape, out_specs = [], []
    for count in outs:
        if count == "log":
            out_shape.append(jax.ShapeDtypeStruct((pairs, 8, rows), jnp.float32))
            out_specs.append(log_spec)
        else:
            out_shape.append(jax.ShapeDtypeStruct((count, pairs * LANES), low_type))
            out_specs.append(pl.BlockSpec((count, LANES), lambda step: (0, step)))
    scratch = [pltpu.VMEM((key_rows - key_split, half), jnp.float32)]
    if key_split != half:
        scratch = [pltpu.VMEM((key_split, half), jnp.float32)] + scratch
    products = 2 if log_total is None else 5
    cells = half * key_rows
    return run(
        functools.partial(kernel, key_split=key_split),
        name,
        pairs,
        (),
        list(operands) + extra + list(codes),
        specs,
        out_shape,
        out_specs,
        scratch,
        products * pairs * 2 * cells * 256 * 2,
        exchange,
        pairs * 2 * cells,
    )


ITEMS = 4

ROW_BLOCK = 256
SHIFT_A, SCALE_A, GATE_A, SHIFT_B, SCALE_B, SHIFT_C, SCALE_C, GATE_C = range(8)


def item_rows(mod_ref, part, code):
    out = mod_ref[part, 0:1, :]
    for item in range(1, ITEMS):
        out = jnp.where(code == item, mod_ref[part, item : item + 1, :], out)
    return out


def item_mask(code_row):
    ids = lax.broadcasted_iota(jnp.int32, (8, code_row.shape[1]), 0)
    return jnp.where(ids == code_row, 1.0, 0.0).astype(low_type)


def item_sums(mask, values):
    high = values.astype(low_type)
    rest = (values - high.astype(jnp.float32)).astype(low_type)
    return rows_dot(mask, high) + rows_dot(mask, rest)


def column_sum(values):
    return jnp.sum(values, axis=0, keepdims=True)


def normed_of(values):
    center = values - jnp.mean(values, axis=-1, keepdims=True)
    spread = jnp.mean(center * center, axis=-1, keepdims=True)
    inverse = lax.rsqrt(spread + epsilon)
    return center * inverse, inverse


def normed_back(grad, scale_by, normed, inverse):
    inner = grad * (1.0 + scale_by)
    return inverse * (
        inner
        - jnp.mean(inner, axis=-1, keepdims=True)
        - normed * jnp.mean(inner * normed, axis=-1, keepdims=True)
    )


def rolled_rows(source_ref, wide_ref):
    rows = source_ref.shape[0]
    wide_ref[:rows, :] = source_ref[...].astype(jnp.float32)
    wide_ref[rows : rows + rows // 2, :] = source_ref[: rows // 2, :].astype(jnp.float32)


def rows_from(wide_ref, first, offset, count):
    rest = lax.rem(first, 8)
    where = pl.ds(pl.multiple_of(first - rest + offset, 8), count + 8)
    rows = wide_ref[where, :].reshape(count // 8 + 1, 8, wide_ref.shape[1])
    turned = pltpu.roll(rows, lax.rem(8 - rest, 8), 1)
    near = lax.broadcasted_iota(jnp.int32, (1, 8, wide_ref.shape[1]), 1) < 8 - rest
    return jnp.where(near, turned[:-1], turned[1:]).reshape(count, wide_ref.shape[1])


def prepare_kernel(
    length_ref,
    item_ref,
    embed_ref,
    w_mod_ref,
    b_mod_ref,
    mod_ref,
    start_ref,
    big_ref,
    code_column_ref,
    code_row_ref,
    token_code_ref,
    condition_ref,
    embedding_ref,
    plain,
):
    side = lax.axis_index("text")

    @pl.when(pl.program_id(0) == 0)
    def _():
        rows = item_ref.shape[1]
        segment = item_ref[pl.ds(side, 1), :]
        counts = [
            jnp.sum(jnp.where(segment == item, 1.0, 0.0)).astype(jnp.int32)
            for item in range(ITEMS)
        ]
        big = sum(item * (count == rows // 2).astype(jnp.int32) for item, count in enumerate(counts))
        start = sum(
            count * (item < big).astype(jnp.int32) for item, count in enumerate(counts)
        )
        start_ref[0] = start
        big_ref[0] = big
        local = lax.rem(segment - big + ITEMS, ITEMS).astype(jnp.float32)
        local = pltpu.roll(
            jnp.broadcast_to(local, (8, rows)), lax.rem(rows - start, rows), 1
        )
        code_row_ref[...] = local[0:1].astype(jnp.int32)
        code_column_ref[...] = local.T[:, 0:1].astype(jnp.int32)
        tokens = token_code_ref.shape[0] // ITEMS
        spot = lax.broadcasted_iota(jnp.int32, (tokens, 128), 0)
        span = tokens // 2
        position = jnp.where(
            spot < span, side * span + spot, (1 - side) * span + spot - span
        )
        plain[...] = embed_ref[...].astype(jnp.float32)
        for item in range(ITEMS):
            origin = lax.rem(big + item, ITEMS)
            valid = position < length_ref[side * ITEMS + origin]
            code = jnp.where(valid, item, -1)
            token_code_ref[item * tokens : (item + 1) * tokens, :] = code[:, 0:1]
            row = plain[pl.ds(origin, 1), :]
            low = row / (1.0 + jnp.exp(-row))
            for copy in (item, item + ITEMS):
                embedding_ref[copy : copy + 1, :] = row
                mod_ref[0, copy : copy + 1, :] = low
        condition_ref[...] = mod_ref[0].astype(low_type)

    mod_ref[0] = rows_dot(condition_ref[...], w_mod_ref[...]) + b_mod_ref[...].astype(jnp.float32)


def text_forward_kernel(big_ref, side_ref, own_ref, fetched_ref, w_kv_ref, text_ref, kv_ref):
    span = own_ref.shape[1]
    for part, ref in enumerate((own_ref, fetched_ref)):
        rows = slice(part * span, (part + 1) * span)
        text = ref[0]
        text_ref[rows, :] = text
        kv_ref[rows, :] = rows_dot(text, w_kv_ref[...]).astype(low_type)


def enter_kernel(
    start_ref,
    frames_ref,
    cotangent_ref,
    code_ref,
    mod_ref,
    w_qkv_ref,
    packed_ref,
    normed_ref,
    frames_out_ref,
    cotangent_out_ref,
    wide_frames,
    wide_cotangent,
):
    step = pl.program_id(0)
    block = packed_ref.shape[0]

    @pl.when(step == 0)
    def _():
        rolled_rows(frames_ref, wide_frames)
        rolled_rows(cotangent_ref, wide_cotangent)

    frames = rows_from(wide_frames, start_ref[0], step * block, block)
    frames_out_ref[...] = frames.astype(low_type)
    cotangent_out_ref[...] = rows_from(wide_cotangent, start_ref[0], step * block, block).astype(
        low_type
    )
    code = code_ref[...]
    normed, _ = normed_of(frames)
    modulated = normed * (1.0 + item_rows(mod_ref, SCALE_A, code)) + item_rows(
        mod_ref, SHIFT_A, code
    )
    low = modulated.astype(low_type)
    normed_ref[...] = low
    packed_ref[...] = rows_dot(low, w_qkv_ref[...]).astype(low_type)


def middle_kernel(
    attended_ref,
    frames_ref,
    code_ref,
    mod_ref,
    w_out_ref,
    b_out_ref,
    w_q_ref,
    after_ref,
    branch_ref,
    normed_ref,
    cross_q_ref,
):
    code = code_ref[...]
    branch = rows_dot(attended_ref[...], w_out_ref[...]) + b_out_ref[...]
    branch_ref[...] = branch
    after = frames_ref[...].astype(jnp.float32) + item_rows(mod_ref, GATE_A, code) * branch
    after_ref[...] = after
    normed, _ = normed_of(after)
    low = (
        normed * (1.0 + item_rows(mod_ref, SCALE_B, code)) + item_rows(mod_ref, SHIFT_B, code)
    ).astype(low_type)
    normed_ref[...] = low
    cross_q_ref[...] = rows_dot(low, w_q_ref[...]).astype(low_type)


GELU_FACTOR = 0.7978845608028654
GELU_CUBE = 0.044715


def gelu_both(inputs):
    square = inputs * inputs
    bend = jnp.tanh(inputs * (GELU_FACTOR + (GELU_FACTOR * GELU_CUBE) * square))
    half_up = 0.5 + 0.5 * bend
    slope = half_up + (0.5 * inputs) * (1.0 - bend * bend) * (
        GELU_FACTOR + (3.0 * GELU_FACTOR * GELU_CUBE) * square
    )
    return inputs * half_up, slope


def remote(source, target, send, receive, peer):
    return pltpu.make_async_remote_copy(
        src_ref=source,
        dst_ref=target,
        send_sem=send,
        recv_sem=receive,
        device_id=peer,
        device_id_type=MESH,
    )


def fill_table(table_ref, sums_ref):
    parts, _, width = sums_ref.shape
    items = table_ref.shape[0] // 2
    flat = jnp.concatenate([sums_ref[part, :items, :] for part in range(parts)], axis=1)
    middle = parts * width // 2
    both = jnp.concatenate([flat[:, :middle], flat[:, middle:]], axis=0)
    table_ref[:, :middle] = both.astype(low_type)


def mlp_kernel(
    cross_out_ref,
    after_a_ref,
    cotangent_ref,
    code_ref,
    code_row_ref,
    mod_ref,
    w_out_cross_ref,
    b_out_cross_ref,
    b_down_ref,
    w_up_ref,
    b_up_ref,
    w_down_ref,
    condition_ref,
    wide_out,
    grad_after_out,
    grad_cross_out,
    grad_w_down_ref,
    grad_w_up_ref,
    grad_w_out_cross_ref,
    grad_b_ref,
    sums_ref,
    table_ref,
    normed_c,
    normed_c_t,
    low_branch,
    back_sum,
    active,
    low_hidden,
    wide,
    grad_after_ref,
    grad_cross_ref,
    flush_sem,
    *core,
):
    after_b = grad_after_ref
    step = pl.program_id(0)
    steps = pl.num_programs(0)
    rows = cross_out_ref.shape[0]
    half = rows // 2
    block = ROW_BLOCK
    blocks = rows // block

    def span(index):
        return pl.ds(pl.multiple_of(index * block, block), block)

    def after_half(index):
        return pl.ds(pl.multiple_of(half + index * block, block), block)

    def core_copies(index):
        down, up, down_in, up_in, down_next, up_next, send, receive = core
        mine, peer = place(0)
        slot = lax.rem(index, 2)
        ends = ((down.at[slot, :, :, 1 - mine], down_in), (up.at[slot, :, 1 - mine], up_in))
        return [
            remote(out, into.at[index], send.at[index, which], receive.at[index, which], peer)
            for which, (out, into) in enumerate(ends)
        ]

    def next_copies(index):
        down, up, down_in, up_in, down_next, up_next, send, receive = core
        bit, across = place(1)
        side, beside = place("text")
        return [
            remote(
                down_in.at[index, :, 1 - bit],
                down_next.at[index],
                send.at[index, 2],
                receive.at[index, 2],
                across,
            ),
            remote(
                up_in.at[index, :, 1 - side],
                up_next.at[index],
                send.at[index, 3],
                receive.at[index, 3],
                beside,
            ),
        ]

    def settle(index):
        down, up, down_in, up_in = core[:4]
        mine = place(0)[0]
        slot = lax.rem(index, 2)
        for copy in core_copies(index):
            copy.wait()
        down_in[index] = down[slot, :, :, mine] + down_in[index]
        up_in[index] = up[slot, :, mine] + up_in[index]
        for copy in next_copies(index):
            copy.start()

    def finish(index):
        down_in, up_in, down_next, up_next = core[2:6]
        for copy in next_copies(index):
            copy.wait()
        grad_w_down_ref[index] = down_in[index, :, place(1)[0]] + down_next[index]
        grad_w_up_ref[index] = up_in[index, :, place("text")[0]] + up_next[index]

    @pl.when(step == 0)
    def _():
        if core:
            greet([0, 1, "text"])
            meet([0, 1, "text"])

        def body(index, _):
            where = span(index)
            code = code_ref[where, :]
            branch = rows_dot(cross_out_ref[where, :], w_out_cross_ref[...]) + b_out_cross_ref[...]
            after = after_a_ref[where, :] + branch
            after_b[where, :] = after
            normed, _ = normed_of(after)
            normed_c[where, :] = (
                normed * (1.0 + item_rows(mod_ref, SCALE_C, code))
                + item_rows(mod_ref, SHIFT_C, code)
            ).astype(low_type)
            low_branch[where, :] = (
                item_rows(mod_ref, GATE_C, code) * cotangent_ref[where, :].astype(jnp.float32)
            ).astype(low_type)
            wide[after_half(index), :] = jnp.zeros((block, wide.shape[1]), jnp.float32)
            back_sum[where, :] = jnp.zeros((block, back_sum.shape[1]), jnp.float32)
            return 0

        lax.fori_loop(0, blocks, body, 0)
        normed_c_t[...] = normed_c[...].T

    def products_of(index):
        where = pl.ds(index * block, block)
        hidden = rows_dot(normed_c[where, :], w_up_ref[...]) + b_up_ref[...]
        return hidden, right_dot(low_branch[where, :], w_down_ref[...])

    bias_total = jnp.zeros((1, w_up_ref.shape[1]), jnp.float32)
    ahead = products_of(0)
    for index in range(blocks):
        where = pl.ds(index * block, block)
        hidden, grad_active = ahead
        if index + 1 < blocks:
            ahead = products_of(index + 1)
        value, slope = gelu_both(hidden)
        low_value = value.astype(low_type)
        active[where, :] = low_value
        grad_hidden = slope * grad_active
        bias_total = bias_total + column_sum(grad_hidden)
        low = grad_hidden.astype(low_type)
        low_hidden[where, :] = low
        wide[after_half(index), :] += rows_dot(low_value, w_down_ref[...])
        back_sum[where, :] += right_dot(low, w_up_ref[...])

    @pl.when(step == 0)
    def _():
        grad_b_ref[...] = jnp.zeros(grad_b_ref.shape, jnp.float32)

    grad_b_ref[pl.ds(2 + step, 1), :] = bias_total
    down_part = left_dot(active[...], low_branch[...]).astype(low_type)
    up_part = rows_dot(normed_c_t[...], low_hidden[...]).astype(low_type)
    if core:
        slot = lax.rem(step, 2)
        core[0][slot] = down_part.reshape(core[0].shape[1:])
        core[1][slot] = up_part.reshape(core[1].shape[1:])
        for copy in core_copies(step):
            copy.start()

        @pl.when(step > 0)
        def _():
            settle(step - 1)

        @pl.when(step > 1)
        def _():
            finish(step - 2)
    else:
        grad_w_down_ref[0] = down_part
        grad_w_up_ref[0] = up_part

    @pl.when(step == steps - 1)
    def _():
        sums_ref[...] = jnp.zeros(sums_ref.shape, jnp.float32)

        def body(index, _):
            where = span(index)
            code = code_ref[where, :]
            mask = item_mask(code_row_ref[:, where])
            upstream = cotangent_ref[where, :].astype(jnp.float32)
            branch = wide[after_half(index), :] + b_down_ref[...]
            gate = item_rows(mod_ref, GATE_C, code)
            after = after_b[where, :]
            out = after + gate * branch
            wide[after_half(index), :] = out

            @pl.when(index >= blocks // 2)
            def _():
                wide[pl.ds(pl.multiple_of(index * block - half, block), block), :] = out

            sums_ref[2] += item_sums(mask, upstream * branch)
            grad_b_ref[0:1, :] += column_sum(gate * upstream)
            normed, inverse = normed_of(after)
            grad = back_sum[where, :]
            sums_ref[0] += item_sums(mask, grad)
            sums_ref[1] += item_sums(mask, grad * normed)
            total = upstream + normed_back(
                grad, item_rows(mod_ref, SCALE_C, code), normed, inverse
            )
            grad_after_ref[where, :] = total
            grad_b_ref[1:2, :] += column_sum(total)
            low = total.astype(low_type)
            low_branch[where, :] = low
            grad_cross_ref[where, :] = right_dot(low, w_out_cross_ref[...]).astype(low_type)
            return 0

        def flushes(index):
            rows_done, moved = span(index), after_half(index)
            pairs = [
                (grad_after_ref.at[rows_done], grad_after_out.at[rows_done]),
                (grad_cross_ref.at[rows_done], grad_cross_out.at[rows_done]),
                (wide.at[moved], wide_out.at[moved]),
            ]
            return [
                pltpu.make_async_copy(source, target, flush_sem.at[index, which])
                for which, (source, target) in enumerate(pairs)
            ]

        def flush_front(index):
            front = pl.ds(pl.multiple_of(index * block - half, block), block)
            return pltpu.make_async_copy(
                wide.at[front], wide_out.at[front], flush_sem.at[index, 3]
            )

        def block_done(index, carry):
            body(index, carry)
            for copy in flushes(index):
                copy.start()

            @pl.when(index >= blocks // 2)
            def _():
                flush_front(index).start()

            return 0

        lax.fori_loop(0, 1, block_done, 0)
        if core:
            settle(step)
        lax.fori_loop(1, blocks, block_done, 0)
        grad_w_out_cross_ref[...] = left_dot(cross_out_ref[...], low_branch[...]).astype(low_type)
        fill_table(table_ref, sums_ref)
        table_ref[:, table_ref.shape[1] - condition_ref.shape[1] :] = condition_ref[...]
        if core:
            finish(step - 1)
            finish(step)
        for index in range(blocks):
            for copy in flushes(index):
                copy.wait()
        for index in range(blocks // 2, blocks):
            flush_front(index).wait()


def text_back_kernel(
    big_ref,
    start_ref,
    grad_k_ref,
    grad_v_ref,
    text_ref,
    w_kv_ref,
    wide_ref,
    own_ref,
    sent_ref,
    grad_w_ref,
    frames_out_ref,
    all_k,
    all_v,
    all_text,
):
    step = pl.program_id(0)
    rows = frames_out_ref.shape[0]
    half = pl.num_programs(0) * rows // 2
    frames_out_ref[...] = rows_from(wide_ref, half - start_ref[0], step * rows, rows)
    block, width = grad_k_ref.shape
    span = own_ref.shape[1]
    where = pl.ds(pl.multiple_of(step * block, block), block)
    keys, values = grad_k_ref[...], grad_v_ref[...]
    all_k[where, :] = keys
    all_v[where, :] = values
    all_text[where, :] = text_ref[...]
    total = right_dot(keys, w_kv_ref[:, :width]) + right_dot(values, w_kv_ref[:, width:])
    own_ref[0] = total[:span]
    sent_ref[0] = total[span:].astype(low_type)

    @pl.when(step == pl.num_programs(0) - 1)
    def _():
        text_t = all_text[...].T
        grad_w_ref[0] = rows_dot(text_t, all_k[...]).astype(low_type)
        grad_w_ref[1] = rows_dot(text_t, all_v[...]).astype(low_type)


def back_middle_kernel(
    low_q_ref,
    normed_b_ref,
    after_a_ref,
    grad_after_b_ref,
    branch_ref,
    attended_ref,
    code_ref,
    code_row_ref,
    mod_ref,
    w_q_ref,
    w_out_ref,
    bias_mlp_ref,
    grad_after_ref,
    grad_attended_ref,
    grad_w_q_ref,
    grad_w_out_ref,
    grad_b_ref,
    sums_ref,
    table_ref,
    all_q,
    all_normed,
    all_attended,
    all_branch,
):
    step = pl.program_id(0)
    block = low_q_ref.shape[0]

    @pl.when(step == 0)
    def _():
        sums_ref[...] = jnp.zeros(sums_ref.shape, jnp.float32)
        grad_b_ref[...] = jnp.zeros(grad_b_ref.shape, jnp.float32)

    where = pl.ds(pl.multiple_of(step * block, block), block)
    code = code_ref[...]
    mask = item_mask(code_row_ref[...])
    low_q = low_q_ref[...]
    all_q[where, :] = low_q
    all_normed[where, :] = normed_b_ref[...]
    all_attended[where, :] = attended_ref[...]
    grad = right_dot(low_q, w_q_ref[...])
    normed, inverse = normed_of(after_a_ref[...])
    sums_ref[1] += item_sums(mask, grad)
    sums_ref[2] += item_sums(mask, grad * normed)
    total = grad_after_b_ref[...] + normed_back(
        grad, item_rows(mod_ref, SCALE_B, code), normed, inverse
    )
    grad_after_ref[...] = total
    sums_ref[0] += item_sums(mask, total * branch_ref[...])
    grad_branch = item_rows(mod_ref, GATE_A, code) * total
    grad_b_ref[0:1, :] += column_sum(grad_branch)
    low = grad_branch.astype(low_type)
    all_branch[where, :] = low
    grad_attended_ref[...] = right_dot(low, w_out_ref[...]).astype(low_type)

    @pl.when(step == pl.num_programs(0) - 1)
    def _():
        grad_w_q_ref[...] = left_dot(all_normed[...], all_q[...]).astype(low_type)
        weight = left_dot(all_attended[...], all_branch[...]).astype(low_type)
        fill_table(table_ref, sums_ref)
        grad_b_ref[1:, :] = bias_mlp_ref[:-1, :]
        if len(grad_w_out_ref.shape) == 2:
            grad_w_out_ref[...] = weight
        else:
            shares, rows = grad_w_out_ref.shape[0], grad_w_out_ref.shape[1] - 16
            grad_w_out_ref[:, :rows, :] = weight.reshape(shares, rows, weight.shape[1])
            grad_w_out_ref[:, rows:, :] = jnp.broadcast_to(
                jnp.concatenate([grad_b_ref[...]] * 2, axis=0).astype(low_type)[None],
                (shares, 16, weight.shape[1]),
            )


def leave_kernel(
    grad_q_ref,
    grad_k_ref,
    grad_v_ref,
    frames_ref,
    grad_after_ref,
    code_ref,
    code_row_ref,
    mod_ref,
    w_qkv_ref,
    sums_b_ref,
    sums_c_ref,
    embedding_ref,
    w_mod_ref,
    wide_out,
    table_ref,
    time_ref,
    sums_ref,
    low_sums,
    total,
    wide,
    flush_sem,
):
    step = pl.program_id(0)
    block, width = grad_q_ref.shape
    parts = low_sums.shape[0]
    blocks = pl.num_programs(0) - parts
    half = blocks * block // 2
    used = 3 * half

    @pl.when(step == 0)
    def _():
        sums_ref[...] = jnp.zeros(sums_ref.shape, jnp.float32)
        total[...] = jnp.zeros_like(total)

    @pl.when(step < blocks)
    def _():
        code = code_ref[...]
        mask = item_mask(code_row_ref[...])
        grad = jnp.zeros((block, width), jnp.float32)
        for index, ref in enumerate((grad_q_ref, grad_k_ref, grad_v_ref)):
            grad = grad + right_dot(ref[...], w_qkv_ref[:, index * width : (index + 1) * width])
        normed, inverse = normed_of(frames_ref[...].astype(jnp.float32))
        sums_ref[0] += item_sums(mask, grad)
        sums_ref[1] += item_sums(mask, grad * normed)
        out = grad_after_ref[...] + normed_back(
            grad, item_rows(mod_ref, SCALE_A, code), normed, inverse
        )
        wide[pl.ds(pl.multiple_of(half + step * block, block), block), :] = out

        @pl.when(step >= blocks // 2)
        def _():
            wide[pl.ds(pl.multiple_of(step * block - half, block), block), :] = out

    @pl.when(step == blocks - 1)
    def _():
        pltpu.make_async_copy(wide.at[:used], wide_out.at[:used], flush_sem.at[0]).start()
        fill_table(table_ref, sums_ref)
        at = 0
        for ref in (sums_ref, sums_b_ref, sums_c_ref):
            low_sums[at : at + ref.shape[0]] = ref[...].astype(low_type)
            at += ref.shape[0]

    @pl.when(step >= blocks)
    def _():
        total[...] += right_dot(low_sums[jnp.maximum(step - blocks, 0)], w_mod_ref[...])

    @pl.when(step == pl.num_programs(0) - 1)
    def _():
        embedding = embedding_ref[...]
        gate = 1.0 / (1.0 + jnp.exp(-embedding))
        time_ref[...] = total[...] * (gate + embedding * gate * (1.0 - gate))
        pltpu.make_async_copy(wide.at[:used], wide_out.at[:used], flush_sem.at[0]).wait()


def self_back_kernel(
    q_ref,
    k_ref,
    v_ref,
    grad_ref,
    log_ref,
    code_column_ref,
    code_row_ref,
    normed_ref,
    grad_q_ref,
    grad_k_ref,
    grad_v_ref,
    out_even_ref,
    out_odd_ref,
    bias_ref,
    normed_t,
    *core,
    key_split,
    met,
):
    step = pl.program_id(0)

    @pl.when(step == 0)
    def _():
        normed_t[...] = normed_ref[...].T

    attend_back_kernel(
        q_ref,
        k_ref,
        v_ref,
        grad_ref,
        log_ref,
        code_column_ref,
        code_row_ref,
        grad_q_ref,
        grad_k_ref,
        grad_v_ref,
        bias_ref,
        key_split=key_split,
    )
    pieces = jnp.concatenate([grad_q_ref[...], grad_k_ref[...], grad_v_ref[...]], axis=1)
    weight = rows_dot(normed_t[...], pieces).astype(low_type)
    if not core:
        out_even_ref[0] = weight
        return
    part, part_in, send, receive = core

    def core_copy(index):
        mine, peer = place(0)
        return remote(
            part.at[lax.rem(index, 2), :, :, 1 - mine],
            part_in.at[index],
            send.at[index],
            receive.at[index],
            peer,
        )

    def settle(index):
        core_copy(index).wait()
        total = part[lax.rem(index, 2), :, :, place(0)[0]] + part_in[index]

        @pl.when(lax.rem(index, 2) == 0)
        def _():
            out_even_ref[:, :, index // 2] = total

        @pl.when(lax.rem(index, 2) == 1)
        def _():
            for side in range(2):
                out_odd_ref[:, :, side, index // 2] = total[:, :, side]

    part[lax.rem(step, 2)] = weight.reshape(part.shape[1:])

    @pl.when(step == 0)
    def _():
        meet(met)

    core_copy(step).start()

    @pl.when(step > 0)
    def _():
        settle(step - 1)

    @pl.when(step == pl.num_programs(0) - 1)
    def _():
        settle(step)


def finish_kernel(
    start_ref,
    side_ref,
    spot_ref,
    big_ref,
    wide_ref,
    own_ref,
    partner_ref,
    table_a_ref,
    table_b_ref,
    table_c_ref,
    up_ref,
    even_ref,
    odd_ref,
    kv_ref,
    out_ref,
    time_ref,
    frames_grad_ref,
    text_grad_ref,
    grad_w_mod_ref,
    grad_b_mod_ref,
    sum_up_ref,
    sum_qkv_ref,
    sum_kv_ref,
    sum_out_ref,
    b_out_ref,
    b_out_cross_ref,
    b_up_ref,
    b_down_ref,
    time_out_ref,
    item_total_ref,
):
    tables = (table_a_ref, table_b_ref, table_c_ref)
    step = pl.program_id(0)
    rows = frames_grad_ref.shape[0]
    half = pl.num_programs(0) * rows // 2
    frames_grad_ref[...] = rows_from(wide_ref, half - start_ref[0], step * rows, rows)
    mine = step // (pl.num_programs(0) // 2) == side_ref[0]

    @pl.when(mine)
    def _():
        text_grad_ref[...] = own_ref[...]

    @pl.when(jnp.logical_not(mine))
    def _():
        text_grad_ref[...] = partner_ref[...].astype(jnp.float32)

    @pl.when(step == 0)
    def _():
        share, columns = grad_w_mod_ref.shape
        width = columns // 8
        entry = lax.broadcasted_iota(jnp.int32, (width, share), 0)
        wanted = lax.broadcasted_iota(jnp.int32, (width, share), 1) + spot_ref[0] * share
        chosen = jnp.where(entry == wanted, 1.0, 0.0).astype(low_type)
        own = rows_dot(tables[2][:, tables[2].shape[1] - width :], chosen)
        item = lax.broadcasted_iota(jnp.int32, own.shape, 0)
        shape = (8, tables[2].shape[0])
        row_half = lax.rem(lax.broadcasted_iota(jnp.int32, shape, 1) // 4, 2)
        picked = jnp.where(row_half == lax.broadcasted_iota(jnp.int32, shape, 0), 1.0, 0.0).astype(
            low_type
        )
        kept = [
            jnp.where(lax.rem(item // 4, 2) == part, own, 0.0).astype(low_type) for part in range(2)
        ]
        at = 0
        for table_ref, parts in zip(tables, (2, 3, 3)):
            cut = parts * width // 2
            table = table_ref[:, :cut]
            totals = rows_dot(picked, table)
            for part in range(2):
                grad_w_mod_ref[:, at : at + cut] = left_dot(kept[part], table)
                item_total_ref[:, at : at + cut] = totals[part : part + 1]
                at += cut
        chunk = up_ref.shape[3]
        for index in range(up_ref.shape[1]):
            for side in range(2):
                rows_here = slice(side * up_ref.shape[2], (side + 1) * up_ref.shape[2])
                sum_up_ref[rows_here, index * chunk : (index + 1) * chunk] = up_ref[side, index]
        piece = even_ref.shape[2] // 3
        for index in range(2 * even_ref.shape[0]):
            for kind in range(3):
                span = slice(kind * width + index * piece, kind * width + (index + 1) * piece)
                cut = slice(kind * piece, (kind + 1) * piece)
                if index % 2 == 0:
                    sum_qkv_ref[:, span] = even_ref[index // 2, :, cut]
                    continue
                for side in range(2):
                    rows_here = slice(side * odd_ref.shape[2], (side + 1) * odd_ref.shape[2])
                    sum_qkv_ref[rows_here, span] = odd_ref[side, index // 2, :, cut]
        size = grad_b_mod_ref.shape[0]
        totals = jnp.broadcast_to(item_total_ref[...], (8, columns))
        turn = lax.rem(columns - spot_ref[0] * size, columns)
        grad_b_mod_ref[...] = pltpu.roll(totals, turn, 1)[0, :size]
        sum_out_ref[...] = out_ref[:share, :]
        spread_bias = out_ref[share : share + 8, :]
        turned = pltpu.roll(spread_bias, lax.rem(width - spot_ref[0] * share, width), 1)
        at = spot_ref[0] * 4 * share
        offset = lax.rem(at, width)
        wanted = at // width
        up_rows = pltpu.roll(spread_bias, lax.rem(width - offset, width), 1)
        row = lax.broadcasted_iota(jnp.int32, up_rows.shape, 0)
        up = jnp.sum(jnp.where(row == wanted + 3, up_rows, 0.0), axis=0, keepdims=True)
        b_out_ref[...] = turned[0, :share]
        b_out_cross_ref[...] = turned[2, :share]
        b_down_ref[...] = turned[1, :share]
        b_up_ref[...] = up[0, : 4 * share]
        for item in range(ITEMS):
            time_out_ref[item : item + 1, :] = time_ref[
                pl.ds(lax.rem(item - big_ref[0] + ITEMS, ITEMS), 1), :
            ]
        for part in range(2):
            for side in range(2):
                rows_here = slice(side * kv_ref.shape[2], (side + 1) * kv_ref.shape[2])
                sum_kv_ref[rows_here, part * width : (part + 1) * width] = kv_ref[side, part]


def row_blocks(array, block=ROW_BLOCK):
    return pl.BlockSpec((block,) + tuple(array.shape[1:]), lambda step, *_: (step, 0))


def column_blocks(array, block=ROW_BLOCK):
    return pl.BlockSpec((array.shape[0], block), lambda step, *_: (0, step))


def shape_of(shape, kind):
    return jax.ShapeDtypeStruct(shape, kind)


MESH = pl.DeviceIdType.MESH


def place(label):
    spot = lax.axis_index("frames")
    side = lax.axis_index("text")
    if label == "text":
        return side, (spot, 1 - side)
    mine = lax.rem(spot // (1 << label), 2)
    return mine, (spot + (1 << label) * (1 - 2 * mine), side)


def greet(labels):
    for label in labels:
        pl.semaphore_signal(
            pltpu.get_barrier_semaphore(),
            inc=1,
            device_id=place(label)[1],
            device_id_type=MESH,
        )


def meet(labels):
    pl.semaphore_wait(pltpu.get_barrier_semaphore(), len(labels))


class Reduction:
    def __init__(self, labels, hops, source, out, buffers, send, receive, base):
        self.labels, self.hops, self.current, self.out = list(labels), hops, source, out
        self.buffers, self.send, self.receive, self.base = buffers, send, receive, base

    def copy(self, hop):
        kind, label = self.hops[hop]
        mine, peer = place(label)
        source = self.current
        if kind == "split":
            source = source.at[(slice(None),) * self.labels.index(label) + (1 - mine,)]
        return pltpu.make_async_remote_copy(
            src_ref=source,
            dst_ref=self.buffers[hop],
            send_sem=self.send.at[self.base + hop],
            recv_sem=self.receive.at[self.base + hop],
            device_id=peer,
            device_id_type=MESH,
        )

    def start(self, hop):
        if hop < len(self.hops):
            self.copy(hop).start()

    def finish(self, hop):
        if hop >= len(self.hops):
            return
        self.copy(hop).wait()
        kind, label = self.hops[hop]
        mine = place(label)[0]
        buffer, current = self.buffers[hop], self.current
        if kind == "split":
            dim = self.labels.index(label)
            rest = len(self.labels) - 1

            target = self.out if hop == len(self.hops) - 1 else buffer

            def body(index, _):
                spot = tuple(lax.rem(index // (1 << (rest - 1 - d)), 2) for d in range(rest))
                target[spot] = current[spot[:dim] + (mine,) + spot[dim:]] + buffer[spot]
                return 0

            if rest:
                lax.fori_loop(0, 1 << rest, body, 0)
            else:
                target[...] = current[mine] + buffer[...]
            self.labels.pop(dim)
            self.current = buffer
        elif kind == "sum":
            buffer[...] = current[...] + buffer[...]
            self.current = buffer
            if hop == len(self.hops) - 1:
                self.out[...] = buffer[...]
        elif kind == "swap":
            self.out[...] = buffer[...]
        elif kind == "full":
            self.out[...] = current[...].astype(jnp.float32) + buffer[...].astype(jnp.float32)
        else:
            self.out[mine] = current[...].astype(jnp.float32)
            self.out[1 - mine] = buffer[...].astype(jnp.float32)


class Gathering:
    def __init__(self, hops, source, out, buffer, send, receive, base):
        self.hops, self.source, self.out, self.buffer = hops, source, out, buffer
        self.send, self.receive, self.base = send, receive, base

    def block(self, hop):
        return tuple(place(label)[0] for label in self.hops[hop:][::-1])

    def copy(self, hop):
        where = self.block(hop)
        return pltpu.make_async_remote_copy(
            src_ref=self.buffer.at[where],
            dst_ref=self.buffer.at[where],
            send_sem=self.send.at[self.base + hop],
            recv_sem=self.receive.at[self.base + hop],
            device_id=place(self.hops[hop])[1],
            device_id_type=MESH,
        )

    def start(self, hop):
        if hop == 0:
            self.buffer[self.block(0)] = self.source[...]
        if hop < len(self.hops):
            self.copy(hop).start()

    def finish(self, hop):
        if hop < len(self.hops):
            self.copy(hop).wait()
        if hop == len(self.hops) - 1:
            self.out[...] = self.buffer[...]


def greeted(plans):
    labels = set()
    for names, hops in plans:
        labels |= set(hops) if names is None else {label for _, label in hops}
    return sorted(labels, key=str)


def exchange_parts(arrays, plans):
    outs, scratch, total = [], [], 0
    for array, (labels, hops) in zip(arrays, plans):
        total += len(hops)
        if labels is None:
            shape = (2,) * len(hops) + array.shape
            scratch.append(pltpu.VMEM(shape, array.dtype))
            outs.append(jax.ShapeDtypeStruct(shape, array.dtype))
            continue
        names, shape = list(labels), list(array.shape)
        for kind, label in hops:
            if kind == "split":
                dim = names.index(label)
                names.pop(dim)
                shape.pop(dim)
            scratch.append(pltpu.VMEM(tuple(shape), array.dtype))
        kind = hops[-1][0]
        lead = (2,) if kind == "gather" else ()
        wide = array.dtype if kind in ("split", "swap", "sum") else jnp.float32
        outs.append(jax.ShapeDtypeStruct(lead + tuple(shape), wide))
    semaphores = pltpu.SemaphoreType.DMA((total,))
    return outs, scratch + [semaphores, semaphores]


def make_flows(plans, sources, outs, rest):
    send, receive = rest[-2:]
    flows, base, used = [], 0, 0
    for (labels, hops), source, out in zip(plans, sources, outs):
        if labels is None:
            flows.append(Gathering(hops, source, out, rest[used], send, receive, base))
            used += 1
        else:
            buffers = rest[used : used + len(hops)]
            flows.append(Reduction(labels, hops, source, out, buffers, send, receive, base))
            used += len(hops)
        base += len(hops)
    return flows


def with_exchange(kernel, counts, arrays, plans, ends, begins, others):
    labels = sorted(set(greeted(plans)) | set(others), key=str)

    def body(*refs):
        groups, at = [], 0
        for count in counts:
            groups.append(refs[at : at + count])
            at += count
        scalars, inputs, given, outputs, targets, scratch, rest = groups
        given = list(given)
        sources = [outputs[a] if isinstance(a, int) else given.pop(0) for a in arrays]
        flows = make_flows(plans, sources, targets, rest)
        step = pl.program_id(0)

        @pl.when(step == 0)
        def _():
            greet(labels)

        kernel(*scalars, *inputs, *outputs, *scratch)

        @pl.when(step == 0)
        def _():
            if not others:
                meet(labels)

        times = set(begins) | {end for flow_ends in ends for end in flow_ends}
        for now in sorted(times):

            @pl.when(step == now)
            def _(now=now):
                for flow, begin in zip(flows, begins):
                    if begin == now:
                        flow.start(0)
                for hop in range(max(len(flow_ends) for flow_ends in ends)):
                    for flow, flow_ends in zip(flows, ends):
                        if hop < len(flow_ends) and flow_ends[hop] == now:
                            flow.finish(hop)
                            flow.start(hop + 1)

    return body


def whole(array):
    return pl.BlockSpec(
        array.shape, lambda step, *_: (0,) * len(array.shape), pipeline_mode=pl.Buffered(1)
    )


def run(
    kernel,
    name,
    grid,
    scalars,
    operands,
    specs,
    outs,
    out_specs,
    scratch,
    flops,
    exchange=None,
    transcendentals=0,
    collective=None,
    others=(),
):
    operands, specs, outs = list(operands), list(specs), list(outs)
    out_specs, scratch = list(out_specs), list(scratch)
    traffic = sum(a.size * a.dtype.itemsize for a in operands + outs)
    effects = {}
    if exchange is not None:
        arrays, plans, ends, collective = exchange[:4]
        begins = exchange[4] if len(exchange) > 4 else (0,) * len(arrays)
        shapes = [outs[a] if isinstance(a, int) else a for a in arrays]
        more_outs, more_scratch = exchange_parts(shapes, plans)
        given = [a for a in arrays if not isinstance(a, int)]
        counts = (
            len(scalars),
            len(operands),
            len(given),
            len(outs),
            len(more_outs),
            len(scratch),
            len(more_scratch),
        )
        kernel = with_exchange(kernel, counts, arrays, plans, ends, begins, others)
        operands += given
        specs += [whole(array) for array in given]
        outs += more_outs
        out_specs += [whole(array) for array in more_outs]
        scratch += more_scratch
    if collective is not None:
        effects = dict(collective_id=collective, has_side_effects=True)
    return pl.pallas_call(
        kernel,
        out_shape=outs,
        grid_spec=pltpu.PrefetchScalarGridSpec(
            num_scalar_prefetch=len(scalars),
            grid=(grid,),
            in_specs=specs,
            out_specs=out_specs,
            scratch_shapes=scratch,
        ),
        compiler_params=pltpu.CompilerParams(vmem_limit_bytes=GRANTS[name] << 20, **effects),
        cost_estimate=pl.CostEstimate(
            flops=flops, transcendentals=transcendentals, bytes_accessed=traffic
        ),
        name=name,
    )(*scalars, *operands)


GRANTS = dict(
    prepare=24,
    text_forward=24,
    enter=34,
    self_forward=20,
    middle=24,
    cross_forward=20,
    mlp=60,
    reduce_core=60,
    cross_backward=60,
    text_back=60,
    back_middle=60,
    self_backward=60,
    leave=60,
    finish=60,
)


def idle_kernel():
    pass


def swapped(value):
    return lax.ppermute(value, "text", [(0, 1), (1, 0)])


def on_device(
    frames_in,
    frame_item,
    text_in,
    text_len,
    time_embed,
    cotangent,
    w_mod,
    b_mod,
    w_qkv,
    w_out,
    b_out,
    w_q_cross,
    w_kv_cross,
    w_out_cross,
    b_out_cross,
    w_up,
    b_up,
    w_down,
    b_down,
):
    text_side = lax.axis_index("text")
    partner_side = 1 - text_side
    row_count, width = frames_in.shape
    half = row_count // 2
    hidden_width = w_up.shape[1]
    item_count = time_embed.shape[0]
    token_span = text_in.shape[1]
    token_rows = item_count * 2 * token_span
    share_count = lax.axis_size("frames")
    bits = share_count.bit_length() - 1
    spot = lax.axis_index("frames")
    partner_text = lax.dynamic_slice_in_dim(text_in, partner_side * item_count, item_count, 0)
    fetched_text = swapped(partner_text)
    pairs = width // LANES
    blocks = row_count // ROW_BLOCK
    matmul_flops = 2 * row_count * width * width

    scalar = jax.ShapeDtypeStruct((1,), jnp.int32)
    scalar_spec = pl.BlockSpec(memory_space=pltpu.SMEM)
    column = jax.ShapeDtypeStruct((row_count, 1), jnp.int32)
    token_column = jax.ShapeDtypeStruct((token_rows, 1), jnp.int32)
    row = jax.ShapeDtypeStruct((1, row_count), jnp.int32)
    both = (2 * item_count, width)
    mod_shape = jax.ShapeDtypeStruct((8, 2 * item_count, width), jnp.float32)
    outs = [
        mod_shape,
        scalar,
        scalar,
        column,
        row,
        token_column,
        jax.ShapeDtypeStruct(both, low_type),
        jax.ShapeDtypeStruct(both, jnp.float32),
    ]
    b_mod_row = b_mod.reshape(1, -1)
    mod, start_scalar, big_scalar, code_column, code_row, token_code, condition, embedding_rows = run(
        prepare_kernel,
        "prepare",
        8,
        (text_len,),
        (frame_item, time_embed, w_mod, b_mod_row),
        [
            whole(frame_item),
            whole(time_embed),
            column_blocks(w_mod, width),
            column_blocks(b_mod_row, width),
        ],
        outs,
        [pl.BlockSpec((1,) + mod_shape.shape[1:], lambda step, *_: (step, 0, 0))]
        + [scalar_spec] * 2
        + [whole(shape) for shape in outs[3:]],
        [pltpu.VMEM((item_count, width), jnp.float32)],
        0,
    )
    self_codes = (code_column, code_row)
    cross_codes = (token_code, code_row)

    def as_row(vector):
        return vector.astype(jnp.float32)[None, :]

    low_rows = shape_of((row_count, width), low_type)
    full_rows = shape_of((row_count, width), jnp.float32)
    square = shape_of((width, width), low_type)
    low_scratch = pltpu.VMEM((row_count, width), low_type)
    full_scratch = pltpu.VMEM((row_count, width), jnp.float32)
    wide_scratch = pltpu.VMEM((row_count + half + 8, width), jnp.float32)

    operands = (frames_in, cotangent, code_column, mod, w_qkv)
    packed_shape = shape_of((row_count, 3 * width), low_type)
    packed, normed_a, frames, upstream = run(
        enter_kernel,
        "enter",
        blocks,
        (start_scalar,),
        operands,
        [whole(frames_in), whole(cotangent), row_blocks(code_column), whole(mod), whole(w_qkv)],
        [packed_shape, low_rows, low_rows, low_rows],
        [row_blocks(packed_shape), row_blocks(low_rows), row_blocks(low_rows), row_blocks(low_rows)],
        [wide_scratch, wide_scratch],
        3 * matmul_flops,
    )
    packed_columns = (pairs, (0, pairs, 2 * pairs, 0))
    attended, self_log = attention_call(
        attend_kernel,
        "self_forward",
        (packed, packed, packed),
        packed_columns,
        self_codes,
        None,
        (row_count, "log"),
        half,
        row_count,
    )
    operands = (attended, frames, code_column, mod, w_out, as_row(b_out), w_q_cross)
    after_a, branch_a, normed_b, cross_q = run(
        middle_kernel,
        "middle",
        blocks,
        (),
        operands,
        [row_blocks(attended), row_blocks(frames), row_blocks(code_column)]
        + [whole(array) for array in operands[3:]],
        [full_rows, full_rows, low_rows, low_rows],
        [row_blocks(full_rows)] * 2 + [row_blocks(low_rows)] * 2,
        [],
        2 * matmul_flops,
    )
    text_rows = shape_of((token_rows, text_in.shape[2]), low_type)
    kv_rows = shape_of((token_rows, 2 * width), low_type)
    token_block = 2 * token_span
    side_scalar = text_side.reshape(1)
    text, text_kv = run(
        text_forward_kernel,
        "text_forward",
        item_count,
        (big_scalar, side_scalar),
        (text_in, fetched_text, w_kv_cross),
        [
            pl.BlockSpec(
                (1,) + text_in.shape[1:],
                lambda step, big_ref, side_ref: (
                    side_ref[0] * item_count + lax.rem(step + big_ref[0], item_count),
                    0,
                    0,
                ),
            ),
            pl.BlockSpec(
                (1,) + text_in.shape[1:],
                lambda step, big_ref, side_ref: (lax.rem(step + big_ref[0], item_count), 0, 0),
            ),
            whole(w_kv_cross),
        ],
        [text_rows, kv_rows],
        [row_blocks(text_rows, token_block), row_blocks(kv_rows, token_block)],
        [],
        2 * 2 * token_rows * width * width,
    )
    cross_columns = (pairs, (0, 0, pairs, 0))
    cross_out, cross_log = attention_call(
        attend_kernel,
        "cross_forward",
        (cross_q, text_kv, text_kv),
        cross_columns,
        cross_codes,
        None,
        (row_count, "log"),
        2 * token_span,
        token_rows,
    )
    frame_labels = tuple(range(bits))[::-1]
    frame_dims = (2,) * bits
    rest_labels, rest_dims = frame_labels[:-1], frame_dims[:-1]
    low_bits = [("split", bit) for bit in range(1, bits)]

    def shares(array):
        rows, columns = array.shape[-2:]
        return array.reshape(array.shape[:-2] + frame_dims + (rows // share_count, columns))

    def text_shares(array):
        rows, columns = array.shape[-2:]
        cut = (2, rows // share_count // 2, columns)
        return array.reshape(array.shape[:-2] + frame_dims + cut)

    def spread(count, low, top):
        return tuple(low + (top - low) * (hop + 1) // count for hop in range(count))

    chunks = 4
    chunk = hidden_width // chunks
    down_share, up_share = hidden_width // share_count, width // share_count
    chunk_pairs, pair_count = chunk // down_share // 2, share_count // 2
    in_core = down_share % 16 == 0 and up_share % 16 == 0
    operands = (
        cross_out,
        after_a,
        upstream,
        code_column,
        code_row,
        mod,
        w_out_cross,
        as_row(b_out_cross),
        as_row(b_down),
        w_up,
        as_row(b_up),
        w_down,
        condition,
    )
    bias_shape = shape_of((8, width), jnp.float32)
    sums_shape = shape_of((3, 8, width), jnp.float32)
    core_scratch = []
    if in_core:
        down_shape = shape_of((chunks, chunk_pairs // 2, down_share, width), low_type)
        up_shape = shape_of((chunks, pair_count, up_share // 2, chunk), low_type)
        weight_specs = [whole(down_shape), whole(up_shape)]
        core_scratch = [
            pltpu.VMEM((2, chunk_pairs // 2, 2, 2, down_share, width), low_type),
            pltpu.VMEM((2, pair_count, 2, 2, up_share // 2, chunk), low_type),
            pltpu.VMEM((chunks, chunk_pairs // 2, 2, down_share, width), low_type),
            pltpu.VMEM((chunks, pair_count, 2, up_share // 2, chunk), low_type),
            pltpu.VMEM(down_shape.shape, low_type),
            pltpu.VMEM(up_shape.shape, low_type),
            pltpu.SemaphoreType.DMA((chunks, 4)),
            pltpu.SemaphoreType.DMA((chunks, 4)),
        ]
    else:
        down_shape = shape_of((chunks, chunk, width), low_type)
        up_shape = shape_of((chunks, width, chunk), low_type)
        weight_specs = [
            pl.BlockSpec((1,) + shape.shape[1:], lambda step, *_: (step, 0, 0))
            for shape in (down_shape, up_shape)
        ]
    wide_shape = shape_of((row_count + half + 8, width), jnp.float32)
    outs = [wide_shape, full_rows, low_rows, down_shape, up_shape, square]
    table_c_shape = shape_of((2 * item_count, 3 * width // 2 + width), low_type)
    table_b_shape = shape_of((2 * item_count, 3 * width // 2), low_type)
    table_a_shape = shape_of((2 * item_count, width), low_type)
    outs += [bias_shape, sums_shape, table_c_shape]
    (
        wide_out,
        grad_after_b,
        grad_cross,
        part_down,
        part_up,
        grad_w_out_cross,
        grad_b_mlp,
        sums_c,
        table_c,
    ) = run(
        mlp_kernel,
        "mlp",
        chunks,
        (),
        operands,
        [whole(array) for array in operands[:9]]
        + [
            column_blocks(w_up, chunk),
            column_blocks(operands[10], chunk),
            row_blocks(w_down, chunk),
            whole(operands[12]),
        ],
        outs,
        [pl.BlockSpec(memory_space=pl.ANY)] * 3
        + weight_specs
        + [
            whole(square),
            whole(bias_shape),
            whole(sums_shape),
            whole(table_c_shape),
        ],
        [
            low_scratch,
            pltpu.VMEM((width, row_count), low_type),
            low_scratch,
            full_scratch,
            pltpu.VMEM((row_count, chunk), low_type),
            pltpu.VMEM((row_count, chunk), low_type),
            wide_scratch,
            full_scratch,
            low_scratch,
            pltpu.SemaphoreType.DMA((blocks, 4)),
        ]
        + core_scratch,
        26 * matmul_flops,
        collective=0 if in_core else None,
    )
    chunk_labels = ("chunk", "block")
    if in_core:
        part_down = part_down.reshape(rest_dims[:-1] + (2, down_share // 2, width))
        part_up = part_up.reshape((2, 2) + rest_dims + (up_share // 2, chunk))
    else:
        part_down, part_up = run(
            idle_kernel,
            "reduce_core",
            1,
            (),
            (),
            [],
            [],
            [],
            [],
            0,
            (
                [
                    text_shares(part_down.reshape(hidden_width, width)),
                    text_shares(part_up.reshape(2, 2, width, chunk)),
                ],
                [
                    (frame_labels + ("text",), [("split", 0), ("split", 1)]),
                    (
                        chunk_labels + frame_labels + ("text",),
                        [("split", 0), ("split", "text")],
                    ),
                ],
                [(0, 0), (0, 0)],
                6,
            ),
        )

    gather_hops = tuple(range(1, bits))[::-1] + ("text", 0)
    all_labels = tuple(range(bits)) + ("text",)
    (
        low_cross_q,
        grad_text_k,
        grad_text_v,
        table_c,
        part_down,
        part_up,
    ) = attention_call(
        attend_back_kernel,
        "cross_backward",
        (cross_q, text_kv, text_kv, grad_cross),
        cross_columns,
        cross_codes,
        cross_log,
        (row_count, token_rows, token_rows),
        2 * token_span,
        token_rows,
        (
            [table_c, part_down, part_up],
            [
                (None, gather_hops[:-2]),
                (rest_labels[:-1] + ("text",), [("split", "text")]),
                (chunk_labels + rest_labels, low_bits[:1]),
            ],
            [
                spread(bits - 1, -1, pairs - 1),
                (pairs - 3,),
                (pairs - 3,),
            ],
            1,
        ),
    )
    half_text = (item_count, token_span, text.shape[1])
    own_shape, sent_shape = shape_of(half_text, jnp.float32), shape_of(half_text, low_type)
    kv_shape = shape_of((2, text.shape[1], width), low_type)
    operands = (grad_text_k, grad_text_v, text, w_kv_cross, wide_out)
    item_spec = pl.BlockSpec(
        (1,) + half_text[1:], lambda step, big_ref, _: (lax.rem(step + big_ref[0], item_count), 0, 0)
    )
    own_text_grad, sent_text_grad, grad_w_kv, frames_out = run(
        text_back_kernel,
        "text_back",
        item_count,
        (big_scalar, start_scalar),
        operands,
        [row_blocks(array, token_block) for array in operands[:3]]
        + [whole(w_kv_cross), whole(wide_out)],
        [own_shape, sent_shape, kv_shape, full_rows],
        [item_spec, item_spec, whole(kv_shape), row_blocks(full_rows, row_count // item_count)],
        [pltpu.VMEM((token_rows, width), low_type)] * 2
        + [pltpu.VMEM((token_rows, text.shape[1]), low_type)],
        4 * 2 * token_rows * width * width,
    )
    operands = (
        low_cross_q,
        normed_b,
        after_a,
        grad_after_b,
        branch_a,
        attended,
        code_column,
        code_row,
        mod,
        w_q_cross,
        w_out,
        grad_b_mlp,
    )
    out_rows = up_share + 16
    out_shape = shape_of((share_count, out_rows, width), low_type) if in_core else square
    (
        grad_after_a,
        grad_attended,
        grad_w_q_cross,
        grad_w_out,
        grad_b_middle,
        sums_b,
        table_b,
        table_c,
        part_down,
        part_up,
        part_kv,
    ) = run(
        back_middle_kernel,
        "back_middle",
        blocks,
        (),
        operands,
        [row_blocks(array) for array in operands[:7]]
        + [column_blocks(code_row)]
        + [whole(array) for array in operands[8:]],
        [full_rows, low_rows, square, out_shape, bias_shape, sums_shape, table_b_shape],
        [row_blocks(full_rows), row_blocks(low_rows), whole(square), whole(out_shape)]
        + [whole(bias_shape), whole(sums_shape), whole(table_b_shape)],
        [low_scratch] * 4,
        4 * matmul_flops,
        (
            [table_c, part_down, part_up, text_shares(grad_w_kv)],
            [
                (None, gather_hops[-2:]),
                (rest_labels[:-1], low_bits[1:2]),
                (chunk_labels + rest_labels[:-1], low_bits[1:2]),
                (("pair",) + frame_labels + ("text",), [("split", 0), ("split", 1)]),
            ],
            [
                (blocks - 2, blocks - 1),
                (blocks - 1,),
                (blocks - 1,),
                (0, blocks - 1),
            ],
            2,
        ),
    )
    piece = 3 * LANES
    even_pairs = pairs - pairs // 2
    if not in_core:
        grad_w_out = jnp.concatenate(
            [
                grad_w_out.reshape(share_count, up_share, width),
                jnp.broadcast_to(
                    jnp.concatenate([grad_b_middle] * 2, axis=0).astype(low_type)[None],
                    (share_count, 16, width),
                ),
            ],
            axis=1,
        )
    part_out = grad_w_out.reshape(frame_dims + (2, out_rows // 2, width))
    if in_core:
        lead = pair_count // 2
        even_shape = shape_of((lead, 2, even_pairs, 2, up_share // 2, piece), low_type)
        odd_shape = shape_of((lead, 2, 2, pairs // 2, up_share // 2, piece), low_type)
        core_scratch = [
            pltpu.VMEM((2, lead, 2, 2, 2, up_share // 2, piece), low_type),
            pltpu.VMEM((pairs, lead, 2, 2, up_share // 2, piece), low_type),
            pltpu.SemaphoreType.DMA((pairs,)),
            pltpu.SemaphoreType.DMA((pairs,)),
        ]
        weight_specs = [whole(even_shape), whole(odd_shape)]
    else:
        even_shape = shape_of((pairs, width, piece), low_type)
        odd_shape = shape_of((8, LANES), low_type)
        core_scratch = []
        weight_specs = [
            pl.BlockSpec((1, width, piece), lambda step, *_: (step, 0, 0)),
            whole(odd_shape),
        ]
    pair_block = pl.BlockSpec((row_count, LANES), lambda step: (0, step))
    (
        grad_q,
        grad_k,
        grad_v,
        part_even,
        part_odd,
        table_b,
        sum_w_down,
        sum_w_up,
        part_kv,
        part_q_cross,
        part_out_cross,
        part_out,
    ) = run(
        functools.partial(self_back_kernel, key_split=half, met=all_labels),
        "self_backward",
        pairs,
        (),
        (packed, packed, packed, grad_attended, self_log, code_column, code_row, normed_a),
        [
            pl.BlockSpec((row_count, LANES), lambda step, offset=offset: (0, offset + step))
            for offset in packed_columns[1]
        ]
        + [pl.BlockSpec((1, 8, row_count), lambda step: (step, 0, 0))]
        + [whole(array) for array in (code_column, code_row, normed_a)],
        [low_rows, low_rows, low_rows, even_shape, odd_shape],
        [pair_block] * 3 + weight_specs,
        [pltpu.VMEM((half, half), jnp.float32), pltpu.VMEM((width, row_count), low_type)]
        + core_scratch,
        8 * matmul_flops,
        (
            [
                table_b,
                part_down,
                part_up,
                part_kv,
                text_shares(grad_w_q_cross),
                text_shares(grad_w_out_cross),
                part_out,
            ],
            [
                (None, gather_hops),
                (rest_labels[:-2], low_bits[2:] + [("gather", "text")]),
                (chunk_labels + rest_labels[:-2], low_bits[2:] + [("gather", "text")]),
                (("pair",) + rest_labels[:-1] + ("text",), [("split", "text")]),
                (frame_labels + ("text",), [("split", 0), ("split", "text"), ("split", 1)]),
                (frame_labels + ("text",), [("split", 0), ("split", 1), ("split", "text")]),
                (frame_labels + ("text",), [("split", 0), ("split", 1)]),
            ],
            [
                spread(bits + 1, 0, pairs - 1),
                spread(bits - 2, 0, pairs - 2),
                spread(bits - 2, 0, pairs - 2),
                (pairs - 2,),
                (1, pairs - 3, pairs - 1),
                (1, pairs - 3, pairs - 1),
                (1, pairs - 2),
            ],
            3,
        ),
        others=all_labels if in_core else (),
    )
    even_labels, odd_labels = rest_labels, rest_labels + ("text",)
    if in_core:
        part_even = part_even.reshape(rest_dims + (even_pairs, up_share, piece))
        part_odd = part_odd.reshape(rest_dims + (2, pairs // 2, up_share // 2, piece))
    else:
        by_pair = part_even.reshape((pairs,) + frame_dims + (up_share, piece))
        part_even = jnp.moveaxis(by_pair[0::2], 0, bits)
        part_odd = by_pair[1::2].reshape(
            (pairs // 2,) + frame_dims + (2, up_share // 2, piece)
        )
        part_even, part_odd = run(
            idle_kernel,
            "reduce_core",
            1,
            (),
            (),
            [],
            [],
            [],
            [],
            0,
            (
                [part_even, jnp.moveaxis(part_odd, 0, bits + 1)],
                [
                    (frame_labels, [("split", 0)]),
                    (frame_labels + ("text",), [("split", 0)]),
                ],
                [(0,), (0,)],
                7,
            ),
        )
    operands = (
        grad_q,
        grad_k,
        grad_v,
        frames,
        grad_after_a,
        code_column,
        code_row,
        mod,
        w_qkv,
        sums_b,
        sums_c,
        embedding_rows,
        w_mod,
    )
    mod_columns = 8 * width
    time_rows = shape_of((8, width), jnp.float32)
    last_block = blocks - 1
    steps = blocks + 8
    late = steps - 1

    def early(array):
        return pl.BlockSpec(
            (ROW_BLOCK, array.shape[1]), lambda step: (jnp.minimum(step, last_block), 0)
        )

    (
        wide_grad,
        _,
        time_grad,
        table_a,
        sum_even,
        sum_odd,
        sum_kv,
        sum_q_cross,
        sum_out_cross,
        sum_out,
        partner_text_grad,
    ) = run(
        leave_kernel,
        "leave",
        steps,
        (),
        operands,
        [early(array) for array in operands[:6]]
        + [pl.BlockSpec((1, ROW_BLOCK), lambda step: (0, jnp.minimum(step, last_block)))]
        + [whole(array) for array in operands[7:12]]
        + [pl.BlockSpec((width, width), lambda step: (0, jnp.maximum(step - blocks, 0)))],
        [wide_shape, table_a_shape, time_rows],
        [pl.BlockSpec(memory_space=pl.ANY), whole(table_a_shape), whole(time_rows)],
        [
            pltpu.VMEM((2, 8, width), jnp.float32),
            pltpu.VMEM((8, 8, width), low_type),
            pltpu.VMEM((8, width), jnp.float32),
            wide_scratch,
            pltpu.SemaphoreType.DMA((1,)),
        ],
        4 * matmul_flops,
        (
            [1, part_even, part_odd, part_kv, part_q_cross, part_out_cross, part_out, sent_text_grad],
            [
                (None, gather_hops),
                (even_labels, low_bits + [("full", "text")]),
                (odd_labels, [("split", "text")] + low_bits + [("gather", "text")]),
                (("pair",) + rest_labels[:-1], low_bits[1:] + [("gather", "text")]),
                (rest_labels[:-1], low_bits[1:] + [("gather", "text")]),
                (rest_labels[:-1], low_bits[1:] + [("gather", "text")]),
                (
                    rest_labels[:-1] + ("text",),
                    [("split", "text")] + low_bits[1:] + [("gather", "text")],
                ),
                ((), [("swap", "text")]),
            ],
            [
                spread(bits + 1, blocks + 2, late),
                (blocks + 1,) + spread(bits - 1, blocks + 4, late),
                (blocks + 1,) + spread(bits, blocks + 4, late),
                spread(bits - 1, last_block - 2, late),
                spread(bits - 1, last_block - 2, late),
                spread(bits - 1, last_block - 2, late),
                spread(bits, last_block, late),
                (late,),
            ],
            4,
            (last_block,) + (0,) * 6 + (blocks + 1,),
        ),
    )
    text_pair = item_count // 2
    text_shape = shape_of((2 * item_count,) + half_text[1:], jnp.float32)

    def text_spec(turn):
        return pl.BlockSpec(
            (text_pair,) + half_text[1:],
            (lambda step, *_: (lax.rem(step, 2), 0, 0)) if turn else (lambda step, *_: (step, 0, 0)),
        )

    operands = (
        wide_grad,
        own_text_grad,
        partner_text_grad,
        table_a.reshape(-1, width),
        table_b.reshape(-1, table_b.shape[-1]),
        table_c.reshape(-1, table_c.shape[-1]),
        sum_w_up.reshape(2, chunks, up_share // 2, chunk),
        sum_even,
        sum_odd,
        sum_kv,
        sum_out.reshape(out_rows, width),
        time_grad,
    )
    mod_shape = shape_of((up_share, mod_columns), jnp.float32)
    b_mod_shape = shape_of((mod_columns // share_count,), jnp.float32)
    sum_up_shape = shape_of((up_share, hidden_width), jnp.float32)
    sum_qkv_shape = shape_of((up_share, 3 * width), jnp.float32)
    sum_kv_shape = shape_of((up_share, 2 * width), jnp.float32)
    sum_out_shape = shape_of((up_share, width), jnp.float32)
    biases_shape = [
        shape_of((size,), jnp.float32) for size in (up_share, up_share, down_share, up_share)
    ]
    time_shape = shape_of((item_count, width), jnp.float32)
    more = [mod_shape, b_mod_shape, sum_up_shape, sum_qkv_shape, sum_kv_shape]
    more += [sum_out_shape] + biases_shape + [time_shape]
    (
        frames_grad,
        text_grad,
        grad_w_mod,
        grad_b_mod,
        sum_w_up,
        sum_qkv,
        sum_kv,
        sum_out,
        *bias_cuts,
        time_grad,
    ) = run(
        finish_kernel,
        "finish",
        4,
        (start_scalar, side_scalar, spot.reshape(1), big_scalar),
        operands,
        [whole(wide_grad), text_spec(True), text_spec(True)] + [whole(a) for a in operands[3:]],
        [full_rows, text_shape] + more,
        [row_blocks(full_rows, row_count // 4), text_spec(False)] + [whole(a) for a in more],
        [pltpu.VMEM((1, mod_columns), jnp.float32)],
        0,
    )
    return (
        frames_out,
        frames_grad,
        text_grad,
        time_grad,
        grad_w_mod,
        grad_b_mod,
        sum_qkv,
        sum_out,
        bias_cuts[0],
        sum_q_cross.reshape(up_share, width),
        sum_kv,
        sum_out_cross.reshape(up_share, width),
        bias_cuts[1],
        sum_w_up,
        bias_cuts[2],
        sum_w_down.reshape(down_share, width),
        bias_cuts[3],
    )


def solution(mesh):
    in_specs = (
        P(("frames", "text"), None),
        P("frames", None),
        P("frames", "text", None),
        P("frames"),
        P(("frames", "text"), None),
        P(("frames", "text"), None),
    ) + (P(),) * 13
    out_specs = (
        P(("frames", "text"), None),
        P(("frames", "text"), None),
        P("frames", "text", None),
        P(("frames", "text"), None),
        P("frames", None),
        P("frames"),
        P("frames", None),
        P("frames", None),
        P("frames"),
        P("frames", None),
        P("frames", None),
        P("frames", None),
        P("frames"),
        P("frames", None),
        P("frames"),
        P("frames", None),
        P("frames"),
    )
    return jax.shard_map(
        on_device, mesh=mesh, in_specs=in_specs, out_specs=out_specs, check_vma=False
    )
```

```python
import functools

import jax
import jax.numpy as jnp
from jax import lax
from jax.experimental import pallas as pl
from jax.experimental.pallas import tpu as pltpu
from jax.sharding import PartitionSpec as P

HEAD_DIM = 64
LANES = 128
VMEM_LIMIT = 60 << 20

epsilon = 1e-06
masked_add = -1000000000.0
highest = lax.Precision.HIGHEST
low_type = jnp.bfloat16


def rows_dot(left_side, right_side):
    return jnp.dot(left_side, right_side, preferred_element_type=jnp.float32)


def left_dot(left_side, right_side):
    return lax.dot_general(
        left_side, right_side, (((0,), (0,)), ((), ())), preferred_element_type=jnp.float32
    )


def right_dot(left_side, right_side):
    return lax.dot_general(
        left_side, right_side, (((1,), (1,)), ((), ())), preferred_element_type=jnp.float32
    )


def layer_norm(values):
    center = values - jnp.mean(values, axis=-1, keepdims=True)
    spread = jnp.mean(center * center, axis=-1, keepdims=True)
    return center * lax.rsqrt(spread + epsilon)


def modulate(values, shift_by, scale_by):
    return layer_norm(values) * (1.0 + scale_by) + shift_by


def gelu_tanh(inputs):
    return (
        0.5
        * inputs
        * (1.0 + jnp.tanh(0.7978845608028654 * (inputs + 0.044715 * inputs * inputs * inputs)))
    )


def head_lanes(value, head, scale=None):
    lane = lax.broadcasted_iota(jnp.int32, value.shape, 1)
    scaled = value if scale is None else value * jnp.asarray(scale, value.dtype)
    return jnp.where(lane // HEAD_DIM == head, scaled, jnp.zeros_like(scaled))


def fill_bias(code_column_ref, code_row_ref, bias_refs, key_split):
    half = code_row_ref.shape[1] // 2
    spans = ((0, key_split), (key_split, code_column_ref.shape[0]))
    for part, bias_ref in enumerate(bias_refs):
        if bias_ref is None:
            continue
        low, top = spans[part]
        bias_ref[...] = jnp.where(
            code_column_ref[low:top, :] == code_row_ref[:, part * half : (part + 1) * half],
            0.0,
            masked_add,
        )


def attend_kernel(
    q_ref, k_ref, v_ref, code_column_ref, code_row_ref, out_ref, log_ref, *bias_refs, key_split
):
    half = q_ref.shape[0] // 2
    scale = HEAD_DIM ** (-0.5)
    if len(bias_refs) == 1:
        bias_refs = (None,) + bias_refs

    @pl.when(pl.program_id(0) == 0)
    def _():
        fill_bias(code_column_ref, code_row_ref, bias_refs, key_split)

    value_t = v_ref[...].T
    key_spans = (slice(0, key_split), slice(key_split, k_ref.shape[0]))
    units = [(part, head) for part in range(2) for head in range(2)]

    def scores_of(part, head):
        queries = q_ref[part * half : (part + 1) * half, :]
        scores = right_dot(k_ref[key_spans[part], :], head_lanes(queries, head, scale))
        return scores if bias_refs[part] is None else scores + bias_refs[part][...]

    ahead = scores_of(*units[0])
    outs = []
    for index, (part, head) in enumerate(units):
        scores = ahead
        if index + 1 < len(units):
            ahead = scores_of(*units[index + 1])
        rows = slice(part * half, (part + 1) * half)
        peak = jnp.max(scores, axis=0, keepdims=True)
        exponent = jnp.exp(scores - peak)
        total = jnp.sum(exponent, axis=0, keepdims=True)
        log_ref[0, head : head + 1, rows] = peak + jnp.log(total)
        lanes = slice(HEAD_DIM * head, HEAD_DIM * (head + 1))
        outs.append(
            rows_dot(value_t[lanes, key_spans[part]], exponent.astype(low_type)) / total
        )
        if head == 1:
            out_ref[rows, :] = jnp.concatenate(outs, axis=0).T.astype(low_type)
            outs = []


def attend_back_kernel(
    q_ref,
    k_ref,
    v_ref,
    grad_ref,
    log_ref,
    code_column_ref,
    code_row_ref,
    grad_q_ref,
    grad_k_ref,
    grad_v_ref,
    *bias_refs,
    key_split,
):
    half = q_ref.shape[0] // 2
    scale = HEAD_DIM ** (-0.5)
    if len(bias_refs) == 1:
        bias_refs = (None,) + bias_refs

    @pl.when(pl.program_id(0) == 0)
    def _():
        fill_bias(code_column_ref, code_row_ref, bias_refs, key_split)

    key_t = k_ref[...].T
    key_spans = (slice(0, key_split), slice(key_split, k_ref.shape[0]))
    units = [(part, head) for part in range(2) for head in range(2)]

    def products_of(part, head):
        rows = slice(part * half, (part + 1) * half)
        query_head = head_lanes(q_ref[rows, :], head, scale)
        grad_head = head_lanes(grad_ref[rows, :], head)
        scores = right_dot(k_ref[key_spans[part], :], query_head)
        if bias_refs[part] is not None:
            scores = scores + bias_refs[part][...]
        grad_prob = right_dot(v_ref[key_spans[part], :], grad_head)
        return scores, grad_prob, query_head, grad_head

    ahead = products_of(*units[0])
    grad_q, grad_k, grad_v = [], [], []
    for index, (part, head) in enumerate(units):
        scores, grad_prob, query_head, grad_head = ahead
        if index + 1 < len(units):
            ahead = products_of(*units[index + 1])
        rows = slice(part * half, (part + 1) * half)
        prob = jnp.exp(scores - log_ref[0, head : head + 1, rows])
        weighted = prob * grad_prob
        delta = jnp.sum(weighted, axis=0, keepdims=True)
        grad_scores = (weighted - prob * delta).astype(low_type)
        grad_k.append(rows_dot(grad_scores, query_head))
        grad_v.append(rows_dot(prob.astype(low_type), grad_head))
        lanes = slice(HEAD_DIM * head, HEAD_DIM * (head + 1))
        grad_q.append(rows_dot(key_t[lanes, key_spans[part]], grad_scores) * scale)
        if head == 1:
            grad_q_ref[rows, :] = jnp.concatenate(grad_q, axis=0).T.astype(low_type)
            grad_k_ref[key_spans[part], :] = (grad_k[0] + grad_k[1]).astype(low_type)
            grad_v_ref[key_spans[part], :] = (grad_v[0] + grad_v[1]).astype(low_type)
            grad_q, grad_k, grad_v = [], [], []


def attention_call(
    kernel, name, operands, columns, codes, log_total, outs, key_split, key_rows, exchange=None
):
    rows = codes[1].shape[1]
    half = rows // 2
    pairs, offsets = columns
    specs = [
        pl.BlockSpec((array.shape[0], LANES), lambda step, offset=offset: (0, offset + step))
        for array, offset in zip(operands, offsets)
    ]
    extra = []
    log_spec = pl.BlockSpec((1, 8, rows), lambda step: (step, 0, 0))
    if log_total is not None:
        specs.append(log_spec)
        extra.append(log_total)
    specs += [whole(code) for code in codes]
    out_shape, out_specs = [], []
    for count in outs:
        if count == "log":
            out_shape.append(jax.ShapeDtypeStruct((pairs, 8, rows), jnp.float32))
            out_specs.append(log_spec)
        else:
            out_shape.append(jax.ShapeDtypeStruct((count, pairs * LANES), low_type))
            out_specs.append(pl.BlockSpec((count, LANES), lambda step: (0, step)))
    scratch = [pltpu.VMEM((key_rows - key_split, half), jnp.float32)]
    if key_split != half:
        scratch = [pltpu.VMEM((key_split, half), jnp.float32)] + scratch
    products = 2 if log_total is None else 5
    cells = half * key_rows
    return run(
        functools.partial(kernel, key_split=key_split),
        name,
        pairs,
        (),
        list(operands) + extra + list(codes),
        specs,
        out_shape,
        out_specs,
        scratch,
        products * pairs * 2 * cells * 256 * 2,
        exchange,
        pairs * 2 * cells,
    )


ITEMS = 4

ROW_BLOCK = 256
SHIFT_A, SCALE_A, GATE_A, SHIFT_B, SCALE_B, SHIFT_C, SCALE_C, GATE_C = range(8)


def item_rows(mod_ref, part, code):
    out = mod_ref[part, 0:1, :]
    for item in range(1, ITEMS):
        out = jnp.where(code == item, mod_ref[part, item : item + 1, :], out)
    return out


def item_mask(code_row):
    ids = lax.broadcasted_iota(jnp.int32, (8, code_row.shape[1]), 0)
    return jnp.where(ids == code_row, 1.0, 0.0).astype(low_type)


def item_sums(mask, values):
    high = values.astype(low_type)
    rest = (values - high.astype(jnp.float32)).astype(low_type)
    return rows_dot(mask, high) + rows_dot(mask, rest)


def column_sum(values):
    return jnp.sum(values, axis=0, keepdims=True)


def normed_of(values):
    center = values - jnp.mean(values, axis=-1, keepdims=True)
    spread = jnp.mean(center * center, axis=-1, keepdims=True)
    inverse = lax.rsqrt(spread + epsilon)
    return center * inverse, inverse


def normed_back(grad, scale_by, normed, inverse):
    inner = grad * (1.0 + scale_by)
    return inverse * (
        inner
        - jnp.mean(inner, axis=-1, keepdims=True)
        - normed * jnp.mean(inner * normed, axis=-1, keepdims=True)
    )


def rolled_rows(source_ref, wide_ref):
    rows = source_ref.shape[0]
    wide_ref[:rows, :] = source_ref[...].astype(jnp.float32)
    wide_ref[rows : rows + rows // 2, :] = source_ref[: rows // 2, :].astype(jnp.float32)


def rows_from(wide_ref, first, offset, count):
    rest = lax.rem(first, 8)
    where = pl.ds(pl.multiple_of(first - rest + offset, 8), count + 8)
    rows = wide_ref[where, :].reshape(count // 8 + 1, 8, wide_ref.shape[1])
    turned = pltpu.roll(rows, lax.rem(8 - rest, 8), 1)
    near = lax.broadcasted_iota(jnp.int32, (1, 8, wide_ref.shape[1]), 1) < 8 - rest
    return jnp.where(near, turned[:-1], turned[1:]).reshape(count, wide_ref.shape[1])


def prepare_kernel(
    length_ref,
    item_ref,
    embed_ref,
    w_mod_ref,
    b_mod_ref,
    mod_ref,
    start_ref,
    big_ref,
    code_column_ref,
    code_row_ref,
    token_code_ref,
    condition_ref,
    embedding_ref,
    plain,
):
    side = lax.axis_index("text")

    @pl.when(pl.program_id(0) == 0)
    def _():
        rows = item_ref.shape[1]
        segment = item_ref[pl.ds(side, 1), :]
        counts = [
            jnp.sum(jnp.where(segment == item, 1.0, 0.0)).astype(jnp.int32)
            for item in range(ITEMS)
        ]
        big = sum(item * (count == rows // 2).astype(jnp.int32) for item, count in enumerate(counts))
        start = sum(
            count * (item < big).astype(jnp.int32) for item, count in enumerate(counts)
        )
        start_ref[0] = start
        big_ref[0] = big
        local = lax.rem(segment - big + ITEMS, ITEMS).astype(jnp.float32)
        local = pltpu.roll(
            jnp.broadcast_to(local, (8, rows)), lax.rem(rows - start, rows), 1
        )
        code_row_ref[...] = local[0:1].astype(jnp.int32)
        code_column_ref[...] = local.T[:, 0:1].astype(jnp.int32)
        tokens = token_code_ref.shape[0] // ITEMS
        spot = lax.broadcasted_iota(jnp.int32, (tokens, 128), 0)
        span = tokens // 2
        position = jnp.where(
            spot < span, side * span + spot, (1 - side) * span + spot - span
        )
        plain[...] = embed_ref[...].astype(jnp.float32)
        for item in range(ITEMS):
            origin = lax.rem(big + item, ITEMS)
            valid = position < length_ref[side * ITEMS + origin]
            code = jnp.where(valid, item, -1)
            token_code_ref[item * tokens : (item + 1) * tokens, :] = code[:, 0:1]
            row = plain[pl.ds(origin, 1), :]
            low = row / (1.0 + jnp.exp(-row))
            for copy in (item, item + ITEMS):
                embedding_ref[copy : copy + 1, :] = row
                mod_ref[0, copy : copy + 1, :] = low
        condition_ref[...] = mod_ref[0].astype(low_type)

    mod_ref[0] = rows_dot(condition_ref[...], w_mod_ref[...]) + b_mod_ref[...].astype(jnp.float32)


def text_forward_kernel(big_ref, side_ref, own_ref, fetched_ref, w_kv_ref, text_ref, kv_ref):
    span = own_ref.shape[1]
    for part, ref in enumerate((own_ref, fetched_ref)):
        rows = slice(part * span, (part + 1) * span)
        text = ref[0]
        text_ref[rows, :] = text
        kv_ref[rows, :] = rows_dot(text, w_kv_ref[...]).astype(low_type)


def enter_kernel(
    start_ref,
    frames_ref,
    cotangent_ref,
    code_ref,
    mod_ref,
    w_qkv_ref,
    packed_ref,
    normed_ref,
    frames_out_ref,
    cotangent_out_ref,
    wide_frames,
    wide_cotangent,
):
    step = pl.program_id(0)
    block = packed_ref.shape[0]

    @pl.when(step == 0)
    def _():
        rolled_rows(frames_ref, wide_frames)
        rolled_rows(cotangent_ref, wide_cotangent)

    frames = rows_from(wide_frames, start_ref[0], step * block, block)
    frames_out_ref[...] = frames.astype(low_type)
    cotangent_out_ref[...] = rows_from(wide_cotangent, start_ref[0], step * block, block).astype(
        low_type
    )
    code = code_ref[...]
    normed, _ = normed_of(frames)
    modulated = normed * (1.0 + item_rows(mod_ref, SCALE_A, code)) + item_rows(
        mod_ref, SHIFT_A, code
    )
    low = modulated.astype(low_type)
    normed_ref[...] = low
    packed_ref[...] = rows_dot(low, w_qkv_ref[...]).astype(low_type)


def middle_kernel(
    attended_ref,
    frames_ref,
    code_ref,
    mod_ref,
    w_out_ref,
    b_out_ref,
    w_q_ref,
    after_ref,
    branch_ref,
    normed_ref,
    cross_q_ref,
):
    code = code_ref[...]
    branch = rows_dot(attended_ref[...], w_out_ref[...]) + b_out_ref[...]
    branch_ref[...] = branch
    after = frames_ref[...].astype(jnp.float32) + item_rows(mod_ref, GATE_A, code) * branch
    after_ref[...] = after
    normed, _ = normed_of(after)
    low = (
        normed * (1.0 + item_rows(mod_ref, SCALE_B, code)) + item_rows(mod_ref, SHIFT_B, code)
    ).astype(low_type)
    normed_ref[...] = low
    cross_q_ref[...] = rows_dot(low, w_q_ref[...]).astype(low_type)


GELU_FACTOR = 0.7978845608028654
GELU_CUBE = 0.044715


def gelu_both(inputs):
    square = inputs * inputs
    bend = jnp.tanh(inputs * (GELU_FACTOR + (GELU_FACTOR * GELU_CUBE) * square))
    half_up = 0.5 + 0.5 * bend
    slope = half_up + (0.5 * inputs) * (1.0 - bend * bend) * (
        GELU_FACTOR + (3.0 * GELU_FACTOR * GELU_CUBE) * square
    )
    return inputs * half_up, slope


def remote(source, target, send, receive, peer):
    return pltpu.make_async_remote_copy(
        src_ref=source,
        dst_ref=target,
        send_sem=send,
        recv_sem=receive,
        device_id=peer,
        device_id_type=MESH,
    )


def fill_table(table_ref, sums_ref):
    parts, _, width = sums_ref.shape
    items = table_ref.shape[0] // 2
    flat = jnp.concatenate([sums_ref[part, :items, :] for part in range(parts)], axis=1)
    middle = parts * width // 2
    both = jnp.concatenate([flat[:, :middle], flat[:, middle:]], axis=0)
    table_ref[:, :middle] = both.astype(low_type)


def mlp_kernel(
    cross_out_ref,
    after_a_ref,
    cotangent_ref,
    code_ref,
    code_row_ref,
    mod_ref,
    w_out_cross_ref,
    b_out_cross_ref,
    b_down_ref,
    w_up_ref,
    b_up_ref,
    w_down_ref,
    condition_ref,
    wide_out,
    grad_after_out,
    grad_cross_out,
    grad_w_down_ref,
    grad_w_up_ref,
    grad_w_out_cross_ref,
    grad_b_ref,
    sums_ref,
    table_ref,
    normed_c,
    normed_c_t,
    low_branch,
    back_sum,
    active,
    low_hidden,
    wide,
    grad_after_ref,
    grad_cross_ref,
    flush_sem,
    *core,
):
    after_b = grad_after_ref
    step = pl.program_id(0)
    steps = pl.num_programs(0)
    rows = cross_out_ref.shape[0]
    half = rows // 2
    block = ROW_BLOCK
    blocks = rows // block

    def span(index):
        return pl.ds(pl.multiple_of(index * block, block), block)

    def after_half(index):
        return pl.ds(pl.multiple_of(half + index * block, block), block)

    def core_copies(index):
        down, up, down_in, up_in, down_next, up_next, send, receive = core
        mine, peer = place(0)
        slot = lax.rem(index, 2)
        ends = ((down.at[slot, :, :, 1 - mine], down_in), (up.at[slot, :, 1 - mine], up_in))
        return [
            remote(out, into.at[index], send.at[index, which], receive.at[index, which], peer)
            for which, (out, into) in enumerate(ends)
        ]

    def next_copies(index):
        down, up, down_in, up_in, down_next, up_next, send, receive = core
        bit, across = place(1)
        side, beside = place("text")
        return [
            remote(
                down_in.at[index, :, 1 - bit],
                down_next.at[index],
                send.at[index, 2],
                receive.at[index, 2],
                across,
            ),
            remote(
                up_in.at[index, :, 1 - side],
                up_next.at[index],
                send.at[index, 3],
                receive.at[index, 3],
                beside,
            ),
        ]

    def settle(index):
        down, up, down_in, up_in = core[:4]
        mine = place(0)[0]
        slot = lax.rem(index, 2)
        for copy in core_copies(index):
            copy.wait()
        down_in[index] = down[slot, :, :, mine] + down_in[index]
        up_in[index] = up[slot, :, mine] + up_in[index]
        for copy in next_copies(index):
            copy.start()

    def finish(index):
        down_in, up_in, down_next, up_next = core[2:6]
        for copy in next_copies(index):
            copy.wait()
        grad_w_down_ref[index] = down_in[index, :, place(1)[0]] + down_next[index]
        grad_w_up_ref[index] = up_in[index, :, place("text")[0]] + up_next[index]

    @pl.when(step == 0)
    def _():
        if core:
            greet([0, 1, "text"])
            meet([0, 1, "text"])

        def body(index, _):
            where = span(index)
            code = code_ref[where, :]
            branch = rows_dot(cross_out_ref[where, :], w_out_cross_ref[...]) + b_out_cross_ref[...]
            after = after_a_ref[where, :] + branch
            after_b[where, :] = after
            normed, _ = normed_of(after)
            normed_c[where, :] = (
                normed * (1.0 + item_rows(mod_ref, SCALE_C, code))
                + item_rows(mod_ref, SHIFT_C, code)
            ).astype(low_type)
            low_branch[where, :] = (
                item_rows(mod_ref, GATE_C, code) * cotangent_ref[where, :].astype(jnp.float32)
            ).astype(low_type)
            wide[after_half(index), :] = jnp.zeros((block, wide.shape[1]), jnp.float32)
            back_sum[where, :] = jnp.zeros((block, back_sum.shape[1]), jnp.float32)
            return 0

        lax.fori_loop(0, blocks, body, 0)
        normed_c_t[...] = normed_c[...].T

    def products_of(index):
        where = pl.ds(index * block, block)
        hidden = rows_dot(normed_c[where, :], w_up_ref[...]) + b_up_ref[...]
        return hidden, right_dot(low_branch[where, :], w_down_ref[...])

    bias_total = jnp.zeros((1, w_up_ref.shape[1]), jnp.float32)
    ahead = products_of(0)
    for index in range(blocks):
        where = pl.ds(index * block, block)
        hidden, grad_active = ahead
        if index + 1 < blocks:
            ahead = products_of(index + 1)
        value, slope = gelu_both(hidden)
        low_value = value.astype(low_type)
        active[where, :] = low_value
        grad_hidden = slope * grad_active
        bias_total = bias_total + column_sum(grad_hidden)
        low = grad_hidden.astype(low_type)
        low_hidden[where, :] = low
        wide[after_half(index), :] += rows_dot(low_value, w_down_ref[...])
        back_sum[where, :] += right_dot(low, w_up_ref[...])

    @pl.when(step == 0)
    def _():
        grad_b_ref[...] = jnp.zeros(grad_b_ref.shape, jnp.float32)

    grad_b_ref[pl.ds(2 + step, 1), :] = bias_total
    down_part = left_dot(active[...], low_branch[...]).astype(low_type)
    up_part = rows_dot(normed_c_t[...], low_hidden[...]).astype(low_type)
    if core:
        slot = lax.rem(step, 2)
        core[0][slot] = down_part.reshape(core[0].shape[1:])
        core[1][slot] = up_part.reshape(core[1].shape[1:])
        for copy in core_copies(step):
            copy.start()

        @pl.when(step > 0)
        def _():
            settle(step - 1)

        @pl.when(step > 1)
        def _():
            finish(step - 2)
    else:
        grad_w_down_ref[0] = down_part
        grad_w_up_ref[0] = up_part

    @pl.when(step == steps - 1)
    def _():
        sums_ref[...] = jnp.zeros(sums_ref.shape, jnp.float32)

        def body(index, _):
            where = span(index)
            code = code_ref[where, :]
            mask = item_mask(code_row_ref[:, where])
            upstream = cotangent_ref[where, :].astype(jnp.float32)
            branch = wide[after_half(index), :] + b_down_ref[...]
            gate = item_rows(mod_ref, GATE_C, code)
            after = after_b[where, :]
            out = after + gate * branch
            wide[after_half(index), :] = out

            @pl.when(index >= blocks // 2)
            def _():
                wide[pl.ds(pl.multiple_of(index * block - half, block), block), :] = out

            sums_ref[2] += item_sums(mask, upstream * branch)
            grad_b_ref[0:1, :] += column_sum(gate * upstream)
            normed, inverse = normed_of(after)
            grad = back_sum[where, :]
            sums_ref[0] += item_sums(mask, grad)
            sums_ref[1] += item_sums(mask, grad * normed)
            total = upstream + normed_back(
                grad, item_rows(mod_ref, SCALE_C, code), normed, inverse
            )
            grad_after_ref[where, :] = total
            grad_b_ref[1:2, :] += column_sum(total)
            low = total.astype(low_type)
            low_branch[where, :] = low
            grad_cross_ref[where, :] = right_dot(low, w_out_cross_ref[...]).astype(low_type)
            return 0

        def flushes(index):
            rows_done, moved = span(index), after_half(index)
            pairs = [
                (grad_after_ref.at[rows_done], grad_after_out.at[rows_done]),
                (grad_cross_ref.at[rows_done], grad_cross_out.at[rows_done]),
                (wide.at[moved], wide_out.at[moved]),
            ]
            return [
                pltpu.make_async_copy(source, target, flush_sem.at[index, which])
                for which, (source, target) in enumerate(pairs)
            ]

        def flush_front(index):
            front = pl.ds(pl.multiple_of(index * block - half, block), block)
            return pltpu.make_async_copy(
                wide.at[front], wide_out.at[front], flush_sem.at[index, 3]
            )

        def block_done(index, carry):
            body(index, carry)
            for copy in flushes(index):
                copy.start()

            @pl.when(index >= blocks // 2)
            def _():
                flush_front(index).start()

            return 0

        lax.fori_loop(0, 1, block_done, 0)
        if core:
            settle(step)
        lax.fori_loop(1, blocks, block_done, 0)
        grad_w_out_cross_ref[...] = left_dot(cross_out_ref[...], low_branch[...]).astype(low_type)
        fill_table(table_ref, sums_ref)
        table_ref[:, table_ref.shape[1] - condition_ref.shape[1] :] = condition_ref[...]
        if core:
            finish(step - 1)
            finish(step)
        for index in range(blocks):
            for copy in flushes(index):
                copy.wait()
        for index in range(blocks // 2, blocks):
            flush_front(index).wait()


def text_back_kernel(
    big_ref,
    start_ref,
    grad_k_ref,
    grad_v_ref,
    text_ref,
    w_kv_ref,
    wide_ref,
    own_ref,
    sent_ref,
    grad_w_ref,
    frames_out_ref,
    all_k,
    all_v,
    all_text,
):
    step = pl.program_id(0)
    rows = frames_out_ref.shape[0]
    half = pl.num_programs(0) * rows // 2
    frames_out_ref[...] = rows_from(wide_ref, half - start_ref[0], step * rows, rows)
    block, width = grad_k_ref.shape
    span = own_ref.shape[1]
    where = pl.ds(pl.multiple_of(step * block, block), block)
    keys, values = grad_k_ref[...], grad_v_ref[...]
    all_k[where, :] = keys
    all_v[where, :] = values
    all_text[where, :] = text_ref[...]
    total = right_dot(keys, w_kv_ref[:, :width]) + right_dot(values, w_kv_ref[:, width:])
    own_ref[0] = total[:span]
    sent_ref[0] = total[span:].astype(low_type)

    @pl.when(step == pl.num_programs(0) - 1)
    def _():
        text_t = all_text[...].T
        grad_w_ref[0] = rows_dot(text_t, all_k[...]).astype(low_type)
        grad_w_ref[1] = rows_dot(text_t, all_v[...]).astype(low_type)


def back_middle_kernel(
    low_q_ref,
    normed_b_ref,
    after_a_ref,
    grad_after_b_ref,
    branch_ref,
    attended_ref,
    code_ref,
    code_row_ref,
    mod_ref,
    w_q_ref,
    w_out_ref,
    bias_mlp_ref,
    grad_after_ref,
    grad_attended_ref,
    grad_w_q_ref,
    grad_w_out_ref,
    grad_b_ref,
    sums_ref,
    table_ref,
    all_q,
    all_normed,
    all_attended,
    all_branch,
):
    step = pl.program_id(0)
    block = low_q_ref.shape[0]

    @pl.when(step == 0)
    def _():
        sums_ref[...] = jnp.zeros(sums_ref.shape, jnp.float32)
        grad_b_ref[...] = jnp.zeros(grad_b_ref.shape, jnp.float32)

    where = pl.ds(pl.multiple_of(step * block, block), block)
    code = code_ref[...]
    mask = item_mask(code_row_ref[...])
    low_q = low_q_ref[...]
    all_q[where, :] = low_q
    all_normed[where, :] = normed_b_ref[...]
    all_attended[where, :] = attended_ref[...]
    grad = right_dot(low_q, w_q_ref[...])
    normed, inverse = normed_of(after_a_ref[...])
    sums_ref[1] += item_sums(mask, grad)
    sums_ref[2] += item_sums(mask, grad * normed)
    total = grad_after_b_ref[...] + normed_back(
        grad, item_rows(mod_ref, SCALE_B, code), normed, inverse
    )
    grad_after_ref[...] = total
    sums_ref[0] += item_sums(mask, total * branch_ref[...])
    grad_branch = item_rows(mod_ref, GATE_A, code) * total
    grad_b_ref[0:1, :] += column_sum(grad_branch)
    low = grad_branch.astype(low_type)
    all_branch[where, :] = low
    grad_attended_ref[...] = right_dot(low, w_out_ref[...]).astype(low_type)

    @pl.when(step == pl.num_programs(0) - 1)
    def _():
        grad_w_q_ref[...] = left_dot(all_normed[...], all_q[...]).astype(low_type)
        weight = left_dot(all_attended[...], all_branch[...]).astype(low_type)
        fill_table(table_ref, sums_ref)
        grad_b_ref[1:, :] = bias_mlp_ref[:-1, :]
        if len(grad_w_out_ref.shape) == 2:
            grad_w_out_ref[...] = weight
        else:
            shares, rows = grad_w_out_ref.shape[0], grad_w_out_ref.shape[1] - 16
            grad_w_out_ref[:, :rows, :] = weight.reshape(shares, rows, weight.shape[1])
            grad_w_out_ref[:, rows:, :] = jnp.broadcast_to(
                jnp.concatenate([grad_b_ref[...]] * 2, axis=0).astype(low_type)[None],
                (shares, 16, weight.shape[1]),
            )


def leave_kernel(
    grad_q_ref,
    grad_k_ref,
    grad_v_ref,
    frames_ref,
    grad_after_ref,
    code_ref,
    code_row_ref,
    mod_ref,
    w_qkv_ref,
    sums_b_ref,
    sums_c_ref,
    embedding_ref,
    w_mod_ref,
    wide_out,
    table_ref,
    time_ref,
    sums_ref,
    low_sums,
    total,
    wide,
    flush_sem,
):
    step = pl.program_id(0)
    block, width = grad_q_ref.shape
    parts = low_sums.shape[0]
    blocks = pl.num_programs(0) - parts
    half = blocks * block // 2
    used = 3 * half

    @pl.when(step == 0)
    def _():
        sums_ref[...] = jnp.zeros(sums_ref.shape, jnp.float32)
        total[...] = jnp.zeros_like(total)

    @pl.when(step < blocks)
    def _():
        code = code_ref[...]
        mask = item_mask(code_row_ref[...])
        grad = jnp.zeros((block, width), jnp.float32)
        for index, ref in enumerate((grad_q_ref, grad_k_ref, grad_v_ref)):
            grad = grad + right_dot(ref[...], w_qkv_ref[:, index * width : (index + 1) * width])
        normed, inverse = normed_of(frames_ref[...].astype(jnp.float32))
        sums_ref[0] += item_sums(mask, grad)
        sums_ref[1] += item_sums(mask, grad * normed)
        out = grad_after_ref[...] + normed_back(
            grad, item_rows(mod_ref, SCALE_A, code), normed, inverse
        )
        wide[pl.ds(pl.multiple_of(half + step * block, block), block), :] = out

        @pl.when(step >= blocks // 2)
        def _():
            wide[pl.ds(pl.multiple_of(step * block - half, block), block), :] = out

    @pl.when(step == blocks - 1)
    def _():
        pltpu.make_async_copy(wide.at[:used], wide_out.at[:used], flush_sem.at[0]).start()
        fill_table(table_ref, sums_ref)
        at = 0
        for ref in (sums_ref, sums_b_ref, sums_c_ref):
            low_sums[at : at + ref.shape[0]] = ref[...].astype(low_type)
            at += ref.shape[0]

    @pl.when(step >= blocks)
    def _():
        total[...] += right_dot(low_sums[jnp.maximum(step - blocks, 0)], w_mod_ref[...])

    @pl.when(step == pl.num_programs(0) - 1)
    def _():
        embedding = embedding_ref[...]
        gate = 1.0 / (1.0 + jnp.exp(-embedding))
        time_ref[...] = total[...] * (gate + embedding * gate * (1.0 - gate))
        pltpu.make_async_copy(wide.at[:used], wide_out.at[:used], flush_sem.at[0]).wait()


def self_back_kernel(
    q_ref,
    k_ref,
    v_ref,
    grad_ref,
    log_ref,
    code_column_ref,
    code_row_ref,
    normed_ref,
    grad_q_ref,
    grad_k_ref,
    grad_v_ref,
    out_even_ref,
    out_odd_ref,
    bias_ref,
    normed_t,
    *core,
    key_split,
    met,
):
    step = pl.program_id(0)

    @pl.when(step == 0)
    def _():
        normed_t[...] = normed_ref[...].T

    attend_back_kernel(
        q_ref,
        k_ref,
        v_ref,
        grad_ref,
        log_ref,
        code_column_ref,
        code_row_ref,
        grad_q_ref,
        grad_k_ref,
        grad_v_ref,
        bias_ref,
        key_split=key_split,
    )
    pieces = jnp.concatenate([grad_q_ref[...], grad_k_ref[...], grad_v_ref[...]], axis=1)
    weight = rows_dot(normed_t[...], pieces).astype(low_type)
    if not core:
        out_even_ref[0] = weight
        return
    part, part_in, send, receive = core

    def core_copy(index):
        mine, peer = place(0)
        return remote(
            part.at[lax.rem(index, 2), :, :, 1 - mine],
            part_in.at[index],
            send.at[index],
            receive.at[index],
            peer,
        )

    def settle(index):
        core_copy(index).wait()
        total = part[lax.rem(index, 2), :, :, place(0)[0]] + part_in[index]

        @pl.when(lax.rem(index, 2) == 0)
        def _():
            out_even_ref[:, :, index // 2] = total

        @pl.when(lax.rem(index, 2) == 1)
        def _():
            for side in range(2):
                out_odd_ref[:, :, side, index // 2] = total[:, :, side]

    part[lax.rem(step, 2)] = weight.reshape(part.shape[1:])

    @pl.when(step == 0)
    def _():
        meet(met)

    core_copy(step).start()

    @pl.when(step > 0)
    def _():
        settle(step - 1)

    @pl.when(step == pl.num_programs(0) - 1)
    def _():
        settle(step)


def finish_kernel(
    start_ref,
    side_ref,
    spot_ref,
    big_ref,
    wide_ref,
    own_ref,
    partner_ref,
    table_a_ref,
    table_b_ref,
    table_c_ref,
    up_ref,
    even_ref,
    odd_ref,
    kv_ref,
    out_ref,
    time_ref,
    frames_grad_ref,
    text_grad_ref,
    grad_w_mod_ref,
    grad_b_mod_ref,
    sum_up_ref,
    sum_qkv_ref,
    sum_kv_ref,
    sum_out_ref,
    b_out_ref,
    b_out_cross_ref,
    b_up_ref,
    b_down_ref,
    time_out_ref,
    item_total_ref,
):
    tables = (table_a_ref, table_b_ref, table_c_ref)
    step = pl.program_id(0)
    rows = frames_grad_ref.shape[0]
    half = pl.num_programs(0) * rows // 2
    frames_grad_ref[...] = rows_from(wide_ref, half - start_ref[0], step * rows, rows)
    mine = step // (pl.num_programs(0) // 2) == side_ref[0]

    @pl.when(mine)
    def _():
        text_grad_ref[...] = own_ref[...]

    @pl.when(jnp.logical_not(mine))
    def _():
        text_grad_ref[...] = partner_ref[...].astype(jnp.float32)

    @pl.when(step == 0)
    def _():
        share, columns = grad_w_mod_ref.shape
        width = columns // 8
        entry = lax.broadcasted_iota(jnp.int32, (width, share), 0)
        wanted = lax.broadcasted_iota(jnp.int32, (width, share), 1) + spot_ref[0] * share
        chosen = jnp.where(entry == wanted, 1.0, 0.0).astype(low_type)
        own = rows_dot(tables[2][:, tables[2].shape[1] - width :], chosen)
        item = lax.broadcasted_iota(jnp.int32, own.shape, 0)
        shape = (8, tables[2].shape[0])
        row_half = lax.rem(lax.broadcasted_iota(jnp.int32, shape, 1) // 4, 2)
        picked = jnp.where(row_half == lax.broadcasted_iota(jnp.int32, shape, 0), 1.0, 0.0).astype(
            low_type
        )
        kept = [
            jnp.where(lax.rem(item // 4, 2) == part, own, 0.0).astype(low_type) for part in range(2)
        ]
        at = 0
        for table_ref, parts in zip(tables, (2, 3, 3)):
            cut = parts * width // 2
            table = table_ref[:, :cut]
            totals = rows_dot(picked, table)
            for part in range(2):
                grad_w_mod_ref[:, at : at + cut] = left_dot(kept[part], table)
                item_total_ref[:, at : at + cut] = totals[part : part + 1]
                at += cut
        chunk = up_ref.shape[3]
        for index in range(up_ref.shape[1]):
            for side in range(2):
                rows_here = slice(side * up_ref.shape[2], (side + 1) * up_ref.shape[2])
                sum_up_ref[rows_here, index * chunk : (index + 1) * chunk] = up_ref[side, index]
        piece = even_ref.shape[2] // 3
        for index in range(2 * even_ref.shape[0]):
            for kind in range(3):
                span = slice(kind * width + index * piece, kind * width + (index + 1) * piece)
                cut = slice(kind * piece, (kind + 1) * piece)
                if index % 2 == 0:
                    sum_qkv_ref[:, span] = even_ref[index // 2, :, cut]
                    continue
                for side in range(2):
                    rows_here = slice(side * odd_ref.shape[2], (side + 1) * odd_ref.shape[2])
                    sum_qkv_ref[rows_here, span] = odd_ref[side, index // 2, :, cut]
        size = grad_b_mod_ref.shape[0]
        totals = jnp.broadcast_to(item_total_ref[...], (8, columns))
        turn = lax.rem(columns - spot_ref[0] * size, columns)
        grad_b_mod_ref[...] = pltpu.roll(totals, turn, 1)[0, :size]
        sum_out_ref[...] = out_ref[:share, :]
        spread_bias = out_ref[share : share + 8, :]
        turned = pltpu.roll(spread_bias, lax.rem(width - spot_ref[0] * share, width), 1)
        at = spot_ref[0] * 4 * share
        offset = lax.rem(at, width)
        wanted = at // width
        up_rows = pltpu.roll(spread_bias, lax.rem(width - offset, width), 1)
        row = lax.broadcasted_iota(jnp.int32, up_rows.shape, 0)
        up = jnp.sum(jnp.where(row == wanted + 3, up_rows, 0.0), axis=0, keepdims=True)
        b_out_ref[...] = turned[0, :share]
        b_out_cross_ref[...] = turned[2, :share]
        b_down_ref[...] = turned[1, :share]
        b_up_ref[...] = up[0, : 4 * share]
        for item in range(ITEMS):
            time_out_ref[item : item + 1, :] = time_ref[
                pl.ds(lax.rem(item - big_ref[0] + ITEMS, ITEMS), 1), :
            ]
        for part in range(2):
            for side in range(2):
                rows_here = slice(side * kv_ref.shape[2], (side + 1) * kv_ref.shape[2])
                sum_kv_ref[rows_here, part * width : (part + 1) * width] = kv_ref[side, part]


def row_blocks(array, block=ROW_BLOCK):
    return pl.BlockSpec((block,) + tuple(array.shape[1:]), lambda step, *_: (step, 0))


def column_blocks(array, block=ROW_BLOCK):
    return pl.BlockSpec((array.shape[0], block), lambda step, *_: (0, step))


def shape_of(shape, kind):
    return jax.ShapeDtypeStruct(shape, kind)


MESH = pl.DeviceIdType.MESH


def place(label):
    spot = lax.axis_index("frames")
    side = lax.axis_index("text")
    if label == "text":
        return side, (spot, 1 - side)
    mine = lax.rem(spot // (1 << label), 2)
    return mine, (spot + (1 << label) * (1 - 2 * mine), side)


def greet(labels):
    for label in labels:
        pl.semaphore_signal(
            pltpu.get_barrier_semaphore(),
            inc=1,
            device_id=place(label)[1],
            device_id_type=MESH,
        )


def meet(labels):
    pl.semaphore_wait(pltpu.get_barrier_semaphore(), len(labels))


class Reduction:
    def __init__(self, labels, hops, source, out, buffers, send, receive, base):
        self.labels, self.hops, self.current, self.out = list(labels), hops, source, out
        self.buffers, self.send, self.receive, self.base = buffers, send, receive, base

    def copy(self, hop):
        kind, label = self.hops[hop]
        mine, peer = place(label)
        source = self.current
        if kind == "split":
            source = source.at[(slice(None),) * self.labels.index(label) + (1 - mine,)]
        return pltpu.make_async_remote_copy(
            src_ref=source,
            dst_ref=self.buffers[hop],
            send_sem=self.send.at[self.base + hop],
            recv_sem=self.receive.at[self.base + hop],
            device_id=peer,
            device_id_type=MESH,
        )

    def start(self, hop):
        if hop < len(self.hops):
            self.copy(hop).start()

    def finish(self, hop):
        if hop >= len(self.hops):
            return
        self.copy(hop).wait()
        kind, label = self.hops[hop]
        mine = place(label)[0]
        buffer, current = self.buffers[hop], self.current
        if kind == "split":
            dim = self.labels.index(label)
            rest = len(self.labels) - 1

            target = self.out if hop == len(self.hops) - 1 else buffer

            def body(index, _):
                spot = tuple(lax.rem(index // (1 << (rest - 1 - d)), 2) for d in range(rest))
                target[spot] = current[spot[:dim] + (mine,) + spot[dim:]] + buffer[spot]
                return 0

            if rest:
                lax.fori_loop(0, 1 << rest, body, 0)
            else:
                target[...] = current[mine] + buffer[...]
            self.labels.pop(dim)
            self.current = buffer
        elif kind == "sum":
            buffer[...] = current[...] + buffer[...]
            self.current = buffer
            if hop == len(self.hops) - 1:
                self.out[...] = buffer[...]
        elif kind == "swap":
            self.out[...] = buffer[...]
        elif kind == "full":
            self.out[...] = current[...].astype(jnp.float32) + buffer[...].astype(jnp.float32)
        else:
            self.out[mine] = current[...].astype(jnp.float32)
            self.out[1 - mine] = buffer[...].astype(jnp.float32)


class Gathering:
    def __init__(self, hops, source, out, buffer, send, receive, base):
        self.hops, self.source, self.out, self.buffer = hops, source, out, buffer
        self.send, self.receive, self.base = send, receive, base

    def block(self, hop):
        return tuple(place(label)[0] for label in self.hops[hop:][::-1])

    def copy(self, hop):
        where = self.block(hop)
        return pltpu.make_async_remote_copy(
            src_ref=self.buffer.at[where],
            dst_ref=self.buffer.at[where],
            send_sem=self.send.at[self.base + hop],
            recv_sem=self.receive.at[self.base + hop],
            device_id=place(self.hops[hop])[1],
            device_id_type=MESH,
        )

    def start(self, hop):
        if hop == 0:
            self.buffer[self.block(0)] = self.source[...]
        if hop < len(self.hops):
            self.copy(hop).start()

    def finish(self, hop):
        if hop < len(self.hops):
            self.copy(hop).wait()
        if hop == len(self.hops) - 1:
            self.out[...] = self.buffer[...]


def greeted(plans):
    labels = set()
    for names, hops in plans:
        labels |= set(hops) if names is None else {label for _, label in hops}
    return sorted(labels, key=str)


def exchange_parts(arrays, plans):
    outs, scratch, total = [], [], 0
    for array, (labels, hops) in zip(arrays, plans):
        total += len(hops)
        if labels is None:
            shape = (2,) * len(hops) + array.shape
            scratch.append(pltpu.VMEM(shape, array.dtype))
            outs.append(jax.ShapeDtypeStruct(shape, array.dtype))
            continue
        names, shape = list(labels), list(array.shape)
        for kind, label in hops:
            if kind == "split":
                dim = names.index(label)
                names.pop(dim)
                shape.pop(dim)
            scratch.append(pltpu.VMEM(tuple(shape), array.dtype))
        kind = hops[-1][0]
        lead = (2,) if kind == "gather" else ()
        wide = array.dtype if kind in ("split", "swap", "sum") else jnp.float32
        outs.append(jax.ShapeDtypeStruct(lead + tuple(shape), wide))
    semaphores = pltpu.SemaphoreType.DMA((total,))
    return outs, scratch + [semaphores, semaphores]


def make_flows(plans, sources, outs, rest):
    send, receive = rest[-2:]
    flows, base, used = [], 0, 0
    for (labels, hops), source, out in zip(plans, sources, outs):
        if labels is None:
            flows.append(Gathering(hops, source, out, rest[used], send, receive, base))
            used += 1
        else:
            buffers = rest[used : used + len(hops)]
            flows.append(Reduction(labels, hops, source, out, buffers, send, receive, base))
            used += len(hops)
        base += len(hops)
    return flows


def with_exchange(kernel, counts, arrays, plans, ends, begins, others):
    labels = sorted(set(greeted(plans)) | set(others), key=str)

    def body(*refs):
        groups, at = [], 0
        for count in counts:
            groups.append(refs[at : at + count])
            at += count
        scalars, inputs, far, outputs, targets, scratch, rest, near, load_sem = groups
        loads = [
            pltpu.make_async_copy(source, target, load_sem[0].at[index])
            for index, (source, target) in enumerate(zip(far, near))
        ]
        given = list(near)
        sources = [outputs[a] if isinstance(a, int) else given.pop(0) for a in arrays]
        flows = make_flows(plans, sources, targets, rest)
        step = pl.program_id(0)

        @pl.when(step == 0)
        def _():
            greet(labels)
            for load in loads:
                load.start()

        kernel(*scalars, *inputs, *outputs, *scratch)

        @pl.when(step == 0)
        def _():
            if not others:
                meet(labels)
            for load in loads:
                load.wait()

        times = set(begins) | {end for flow_ends in ends for end in flow_ends}
        for now in sorted(times):

            @pl.when(step == now)
            def _(now=now):
                for flow, begin in zip(flows, begins):
                    if begin == now:
                        flow.start(0)
                for hop in range(max(len(flow_ends) for flow_ends in ends)):
                    for flow, flow_ends in zip(flows, ends):
                        if hop < len(flow_ends) and flow_ends[hop] == now:
                            flow.finish(hop)
                            flow.start(hop + 1)

    return body


def whole(array):
    return pl.BlockSpec(
        array.shape, lambda step, *_: (0,) * len(array.shape), pipeline_mode=pl.Buffered(1)
    )


def run(
    kernel,
    name,
    grid,
    scalars,
    operands,
    specs,
    outs,
    out_specs,
    scratch,
    flops,
    exchange=None,
    transcendentals=0,
    collective=None,
    others=(),
):
    operands, specs, outs = list(operands), list(specs), list(outs)
    out_specs, scratch = list(out_specs), list(scratch)
    traffic = sum(a.size * a.dtype.itemsize for a in operands + outs)
    effects = {}
    if exchange is not None:
        arrays, plans, ends, collective = exchange[:4]
        begins = exchange[4] if len(exchange) > 4 else (0,) * len(arrays)
        shapes = [outs[a] if isinstance(a, int) else a for a in arrays]
        more_outs, more_scratch = exchange_parts(shapes, plans)
        given = [a for a in arrays if not isinstance(a, int)]
        counts = (
            len(scalars),
            len(operands),
            len(given),
            len(outs),
            len(more_outs),
            len(scratch),
            len(more_scratch),
            len(given),
            1,
        )
        kernel = with_exchange(kernel, counts, arrays, plans, ends, begins, others)
        operands += given
        specs += [pl.BlockSpec(memory_space=pl.ANY)] * len(given)
        more_scratch += [pltpu.VMEM(array.shape, array.dtype) for array in given]
        more_scratch.append(pltpu.SemaphoreType.DMA((max(len(given), 1),)))
        outs += more_outs
        out_specs += [whole(array) for array in more_outs]
        scratch += more_scratch
    if collective is not None:
        effects = dict(collective_id=collective, has_side_effects=True)
    return pl.pallas_call(
        kernel,
        out_shape=outs,
        grid_spec=pltpu.PrefetchScalarGridSpec(
            num_scalar_prefetch=len(scalars),
            grid=(grid,),
            in_specs=specs,
            out_specs=out_specs,
            scratch_shapes=scratch,
        ),
        compiler_params=pltpu.CompilerParams(vmem_limit_bytes=GRANTS[name] << 20, **effects),
        cost_estimate=pl.CostEstimate(
            flops=flops, transcendentals=transcendentals, bytes_accessed=traffic
        ),
        name=name,
    )(*scalars, *operands)


GRANTS = dict(
    prepare=24,
    text_forward=24,
    enter=34,
    self_forward=20,
    middle=24,
    cross_forward=20,
    mlp=60,
    reduce_core=60,
    cross_backward=60,
    text_back=60,
    back_middle=60,
    self_backward=60,
    leave=60,
    finish=60,
)


def idle_kernel():
    pass


def swapped(value):
    return lax.ppermute(value, "text", [(0, 1), (1, 0)])


def on_device(
    frames_in,
    frame_item,
    text_in,
    text_len,
    time_embed,
    cotangent,
    w_mod,
    b_mod,
    w_qkv,
    w_out,
    b_out,
    w_q_cross,
    w_kv_cross,
    w_out_cross,
    b_out_cross,
    w_up,
    b_up,
    w_down,
    b_down,
):
    text_side = lax.axis_index("text")
    partner_side = 1 - text_side
    row_count, width = frames_in.shape
    half = row_count // 2
    hidden_width = w_up.shape[1]
    item_count = time_embed.shape[0]
    token_span = text_in.shape[1]
    token_rows = item_count * 2 * token_span
    share_count = lax.axis_size("frames")
    bits = share_count.bit_length() - 1
    spot = lax.axis_index("frames")
    partner_text = lax.dynamic_slice_in_dim(text_in, partner_side * item_count, item_count, 0)
    fetched_text = swapped(partner_text)
    pairs = width // LANES
    blocks = row_count // ROW_BLOCK
    matmul_flops = 2 * row_count * width * width

    scalar = jax.ShapeDtypeStruct((1,), jnp.int32)
    scalar_spec = pl.BlockSpec(memory_space=pltpu.SMEM)
    column = jax.ShapeDtypeStruct((row_count, 1), jnp.int32)
    token_column = jax.ShapeDtypeStruct((token_rows, 1), jnp.int32)
    row = jax.ShapeDtypeStruct((1, row_count), jnp.int32)
    both = (2 * item_count, width)
    mod_shape = jax.ShapeDtypeStruct((8, 2 * item_count, width), jnp.float32)
    outs = [
        mod_shape,
        scalar,
        scalar,
        column,
        row,
        token_column,
        jax.ShapeDtypeStruct(both, low_type),
        jax.ShapeDtypeStruct(both, jnp.float32),
    ]
    b_mod_row = b_mod.reshape(1, -1)
    mod, start_scalar, big_scalar, code_column, code_row, token_code, condition, embedding_rows = run(
        prepare_kernel,
        "prepare",
        8,
        (text_len,),
        (frame_item, time_embed, w_mod, b_mod_row),
        [
            whole(frame_item),
            whole(time_embed),
            column_blocks(w_mod, width),
            column_blocks(b_mod_row, width),
        ],
        outs,
        [pl.BlockSpec((1,) + mod_shape.shape[1:], lambda step, *_: (step, 0, 0))]
        + [scalar_spec] * 2
        + [whole(shape) for shape in outs[3:]],
        [pltpu.VMEM((item_count, width), jnp.float32)],
        0,
    )
    self_codes = (code_column, code_row)
    cross_codes = (token_code, code_row)

    def as_row(vector):
        return vector.astype(jnp.float32)[None, :]

    low_rows = shape_of((row_count, width), low_type)
    full_rows = shape_of((row_count, width), jnp.float32)
    square = shape_of((width, width), low_type)
    low_scratch = pltpu.VMEM((row_count, width), low_type)
    full_scratch = pltpu.VMEM((row_count, width), jnp.float32)
    wide_scratch = pltpu.VMEM((row_count + half + 8, width), jnp.float32)

    operands = (frames_in, cotangent, code_column, mod, w_qkv)
    packed_shape = shape_of((row_count, 3 * width), low_type)
    packed, normed_a, frames, upstream = run(
        enter_kernel,
        "enter",
        blocks,
        (start_scalar,),
        operands,
        [whole(frames_in), whole(cotangent), row_blocks(code_column), whole(mod), whole(w_qkv)],
        [packed_shape, low_rows, low_rows, low_rows],
        [row_blocks(packed_shape), row_blocks(low_rows), row_blocks(low_rows), row_blocks(low_rows)],
        [wide_scratch, wide_scratch],
        3 * matmul_flops,
    )
    packed_columns = (pairs, (0, pairs, 2 * pairs, 0))
    attended, self_log = attention_call(
        attend_kernel,
        "self_forward",
        (packed, packed, packed),
        packed_columns,
        self_codes,
        None,
        (row_count, "log"),
        half,
        row_count,
    )
    operands = (attended, frames, code_column, mod, w_out, as_row(b_out), w_q_cross)
    after_a, branch_a, normed_b, cross_q = run(
        middle_kernel,
        "middle",
        blocks,
        (),
        operands,
        [row_blocks(attended), row_blocks(frames), row_blocks(code_column)]
        + [whole(array) for array in operands[3:]],
        [full_rows, full_rows, low_rows, low_rows],
        [row_blocks(full_rows)] * 2 + [row_blocks(low_rows)] * 2,
        [],
        2 * matmul_flops,
    )
    text_rows = shape_of((token_rows, text_in.shape[2]), low_type)
    kv_rows = shape_of((token_rows, 2 * width), low_type)
    token_block = 2 * token_span
    side_scalar = text_side.reshape(1)
    text, text_kv = run(
        text_forward_kernel,
        "text_forward",
        item_count,
        (big_scalar, side_scalar),
        (text_in, fetched_text, w_kv_cross),
        [
            pl.BlockSpec(
                (1,) + text_in.shape[1:],
                lambda step, big_ref, side_ref: (
                    side_ref[0] * item_count + lax.rem(step + big_ref[0], item_count),
                    0,
                    0,
                ),
            ),
            pl.BlockSpec(
                (1,) + text_in.shape[1:],
                lambda step, big_ref, side_ref: (lax.rem(step + big_ref[0], item_count), 0, 0),
            ),
            whole(w_kv_cross),
        ],
        [text_rows, kv_rows],
        [row_blocks(text_rows, token_block), row_blocks(kv_rows, token_block)],
        [],
        2 * 2 * token_rows * width * width,
    )
    cross_columns = (pairs, (0, 0, pairs, 0))
    cross_out, cross_log = attention_call(
        attend_kernel,
        "cross_forward",
        (cross_q, text_kv, text_kv),
        cross_columns,
        cross_codes,
        None,
        (row_count, "log"),
        2 * token_span,
        token_rows,
    )
    frame_labels = tuple(range(bits))[::-1]
    frame_dims = (2,) * bits
    rest_labels, rest_dims = frame_labels[:-1], frame_dims[:-1]
    low_bits = [("split", bit) for bit in range(1, bits)]

    def shares(array):
        rows, columns = array.shape[-2:]
        return array.reshape(array.shape[:-2] + frame_dims + (rows // share_count, columns))

    def text_shares(array):
        rows, columns = array.shape[-2:]
        cut = (2, rows // share_count // 2, columns)
        return array.reshape(array.shape[:-2] + frame_dims + cut)

    def spread(count, low, top):
        return tuple(low + (top - low) * (hop + 1) // count for hop in range(count))

    chunks = 4
    chunk = hidden_width // chunks
    down_share, up_share = hidden_width // share_count, width // share_count
    chunk_pairs, pair_count = chunk // down_share // 2, share_count // 2
    in_core = down_share % 16 == 0 and up_share % 16 == 0
    operands = (
        cross_out,
        after_a,
        upstream,
        code_column,
        code_row,
        mod,
        w_out_cross,
        as_row(b_out_cross),
        as_row(b_down),
        w_up,
        as_row(b_up),
        w_down,
        condition,
    )
    bias_shape = shape_of((8, width), jnp.float32)
    sums_shape = shape_of((3, 8, width), jnp.float32)
    core_scratch = []
    if in_core:
        down_shape = shape_of((chunks, chunk_pairs // 2, down_share, width), low_type)
        up_shape = shape_of((chunks, pair_count, up_share // 2, chunk), low_type)
        weight_specs = [whole(down_shape), whole(up_shape)]
        core_scratch = [
            pltpu.VMEM((2, chunk_pairs // 2, 2, 2, down_share, width), low_type),
            pltpu.VMEM((2, pair_count, 2, 2, up_share // 2, chunk), low_type),
            pltpu.VMEM((chunks, chunk_pairs // 2, 2, down_share, width), low_type),
            pltpu.VMEM((chunks, pair_count, 2, up_share // 2, chunk), low_type),
            pltpu.VMEM(down_shape.shape, low_type),
            pltpu.VMEM(up_shape.shape, low_type),
            pltpu.SemaphoreType.DMA((chunks, 4)),
            pltpu.SemaphoreType.DMA((chunks, 4)),
        ]
    else:
        down_shape = shape_of((chunks, chunk, width), low_type)
        up_shape = shape_of((chunks, width, chunk), low_type)
        weight_specs = [
            pl.BlockSpec((1,) + shape.shape[1:], lambda step, *_: (step, 0, 0))
            for shape in (down_shape, up_shape)
        ]
    wide_shape = shape_of((row_count + half + 8, width), jnp.float32)
    outs = [wide_shape, full_rows, low_rows, down_shape, up_shape, square]
    table_c_shape = shape_of((2 * item_count, 3 * width // 2 + width), low_type)
    table_b_shape = shape_of((2 * item_count, 3 * width // 2), low_type)
    table_a_shape = shape_of((2 * item_count, width), low_type)
    outs += [bias_shape, sums_shape, table_c_shape]
    (
        wide_out,
        grad_after_b,
        grad_cross,
        part_down,
        part_up,
        grad_w_out_cross,
        grad_b_mlp,
        sums_c,
        table_c,
    ) = run(
        mlp_kernel,
        "mlp",
        chunks,
        (),
        operands,
        [whole(array) for array in operands[:9]]
        + [
            column_blocks(w_up, chunk),
            column_blocks(operands[10], chunk),
            row_blocks(w_down, chunk),
            whole(operands[12]),
        ],
        outs,
        [pl.BlockSpec(memory_space=pl.ANY)] * 3
        + weight_specs
        + [
            whole(square),
            whole(bias_shape),
            whole(sums_shape),
            whole(table_c_shape),
        ],
        [
            low_scratch,
            pltpu.VMEM((width, row_count), low_type),
            low_scratch,
            full_scratch,
            pltpu.VMEM((row_count, chunk), low_type),
            pltpu.VMEM((row_count, chunk), low_type),
            wide_scratch,
            full_scratch,
            low_scratch,
            pltpu.SemaphoreType.DMA((blocks, 4)),
        ]
        + core_scratch,
        26 * matmul_flops,
        collective=0 if in_core else None,
    )
    chunk_labels = ("chunk", "block")
    if in_core:
        part_down = part_down.reshape(rest_dims[:-1] + (2, down_share // 2, width))
        part_up = part_up.reshape((2, 2) + rest_dims + (up_share // 2, chunk))
    else:
        part_down, part_up = run(
            idle_kernel,
            "reduce_core",
            1,
            (),
            (),
            [],
            [],
            [],
            [],
            0,
            (
                [
                    text_shares(part_down.reshape(hidden_width, width)),
                    text_shares(part_up.reshape(2, 2, width, chunk)),
                ],
                [
                    (frame_labels + ("text",), [("split", 0), ("split", 1)]),
                    (
                        chunk_labels + frame_labels + ("text",),
                        [("split", 0), ("split", "text")],
                    ),
                ],
                [(0, 0), (0, 0)],
                6,
            ),
        )

    gather_hops = tuple(range(1, bits))[::-1] + ("text", 0)
    all_labels = tuple(range(bits)) + ("text",)
    (
        low_cross_q,
        grad_text_k,
        grad_text_v,
        table_c,
        part_down,
        part_up,
    ) = attention_call(
        attend_back_kernel,
        "cross_backward",
        (cross_q, text_kv, text_kv, grad_cross),
        cross_columns,
        cross_codes,
        cross_log,
        (row_count, token_rows, token_rows),
        2 * token_span,
        token_rows,
        (
            [table_c, part_down, part_up],
            [
                (None, gather_hops[:-2]),
                (rest_labels[:-1] + ("text",), [("split", "text")]),
                (chunk_labels + rest_labels, low_bits[:1]),
            ],
            [
                spread(bits - 1, -1, pairs - 1),
                (pairs - 3,),
                (pairs - 3,),
            ],
            1,
        ),
    )
    half_text = (item_count, token_span, text.shape[1])
    own_shape, sent_shape = shape_of(half_text, jnp.float32), shape_of(half_text, low_type)
    kv_shape = shape_of((2, text.shape[1], width), low_type)
    operands = (grad_text_k, grad_text_v, text, w_kv_cross, wide_out)
    item_spec = pl.BlockSpec(
        (1,) + half_text[1:], lambda step, big_ref, _: (lax.rem(step + big_ref[0], item_count), 0, 0)
    )
    own_text_grad, sent_text_grad, grad_w_kv, frames_out = run(
        text_back_kernel,
        "text_back",
        item_count,
        (big_scalar, start_scalar),
        operands,
        [row_blocks(array, token_block) for array in operands[:3]]
        + [whole(w_kv_cross), whole(wide_out)],
        [own_shape, sent_shape, kv_shape, full_rows],
        [item_spec, item_spec, whole(kv_shape), row_blocks(full_rows, row_count // item_count)],
        [pltpu.VMEM((token_rows, width), low_type)] * 2
        + [pltpu.VMEM((token_rows, text.shape[1]), low_type)],
        4 * 2 * token_rows * width * width,
    )
    operands = (
        low_cross_q,
        normed_b,
        after_a,
        grad_after_b,
        branch_a,
        attended,
        code_column,
        code_row,
        mod,
        w_q_cross,
        w_out,
        grad_b_mlp,
    )
    out_rows = up_share + 16
    out_shape = shape_of((share_count, out_rows, width), low_type) if in_core else square
    (
        grad_after_a,
        grad_attended,
        grad_w_q_cross,
        grad_w_out,
        grad_b_middle,
        sums_b,
        table_b,
        table_c,
        part_down,
        part_up,
        part_kv,
    ) = run(
        back_middle_kernel,
        "back_middle",
        blocks,
        (),
        operands,
        [row_blocks(array) for array in operands[:7]]
        + [column_blocks(code_row)]
        + [whole(array) for array in operands[8:]],
        [full_rows, low_rows, square, out_shape, bias_shape, sums_shape, table_b_shape],
        [row_blocks(full_rows), row_blocks(low_rows), whole(square), whole(out_shape)]
        + [whole(bias_shape), whole(sums_shape), whole(table_b_shape)],
        [low_scratch] * 4,
        4 * matmul_flops,
        (
            [table_c, part_down, part_up, text_shares(grad_w_kv)],
            [
                (None, gather_hops[-2:]),
                (rest_labels[:-1], low_bits[1:2]),
                (chunk_labels + rest_labels[:-1], low_bits[1:2]),
                (("pair",) + frame_labels + ("text",), [("split", 0), ("split", 1)]),
            ],
            [
                (blocks - 2, blocks - 1),
                (blocks - 1,),
                (blocks - 1,),
                (0, blocks - 1),
            ],
            2,
        ),
    )
    piece = 3 * LANES
    even_pairs = pairs - pairs // 2
    if not in_core:
        grad_w_out = jnp.concatenate(
            [
                grad_w_out.reshape(share_count, up_share, width),
                jnp.broadcast_to(
                    jnp.concatenate([grad_b_middle] * 2, axis=0).astype(low_type)[None],
                    (share_count, 16, width),
                ),
            ],
            axis=1,
        )
    part_out = grad_w_out.reshape(frame_dims + (2, out_rows // 2, width))
    if in_core:
        lead = pair_count // 2
        even_shape = shape_of((lead, 2, even_pairs, 2, up_share // 2, piece), low_type)
        odd_shape = shape_of((lead, 2, 2, pairs // 2, up_share // 2, piece), low_type)
        core_scratch = [
            pltpu.VMEM((2, lead, 2, 2, 2, up_share // 2, piece), low_type),
            pltpu.VMEM((pairs, lead, 2, 2, up_share // 2, piece), low_type),
            pltpu.SemaphoreType.DMA((pairs,)),
            pltpu.SemaphoreType.DMA((pairs,)),
        ]
        weight_specs = [whole(even_shape), whole(odd_shape)]
    else:
        even_shape = shape_of((pairs, width, piece), low_type)
        odd_shape = shape_of((8, LANES), low_type)
        core_scratch = []
        weight_specs = [
            pl.BlockSpec((1, width, piece), lambda step, *_: (step, 0, 0)),
            whole(odd_shape),
        ]
    pair_block = pl.BlockSpec((row_count, LANES), lambda step: (0, step))
    (
        grad_q,
        grad_k,
        grad_v,
        part_even,
        part_odd,
        table_b,
        sum_w_down,
        sum_w_up,
        part_kv,
        part_q_cross,
        part_out_cross,
        part_out,
    ) = run(
        functools.partial(self_back_kernel, key_split=half, met=all_labels),
        "self_backward",
        pairs,
        (),
        (packed, packed, packed, grad_attended, self_log, code_column, code_row, normed_a),
        [
            pl.BlockSpec((row_count, LANES), lambda step, offset=offset: (0, offset + step))
            for offset in packed_columns[1]
        ]
        + [pl.BlockSpec((1, 8, row_count), lambda step: (step, 0, 0))]
        + [whole(array) for array in (code_column, code_row, normed_a)],
        [low_rows, low_rows, low_rows, even_shape, odd_shape],
        [pair_block] * 3 + weight_specs,
        [pltpu.VMEM((half, half), jnp.float32), pltpu.VMEM((width, row_count), low_type)]
        + core_scratch,
        8 * matmul_flops,
        (
            [
                table_b,
                part_down,
                part_up,
                part_kv,
                text_shares(grad_w_q_cross),
                text_shares(grad_w_out_cross),
                part_out,
            ],
            [
                (None, gather_hops),
                (rest_labels[:-2], low_bits[2:] + [("gather", "text")]),
                (chunk_labels + rest_labels[:-2], low_bits[2:] + [("gather", "text")]),
                (("pair",) + rest_labels[:-1] + ("text",), [("split", "text")]),
                (frame_labels + ("text",), [("split", 0), ("split", "text"), ("split", 1)]),
                (frame_labels + ("text",), [("split", 0), ("split", 1), ("split", "text")]),
                (frame_labels + ("text",), [("split", 0), ("split", 1)]),
            ],
            [
                spread(bits + 1, 0, pairs - 1),
                spread(bits - 2, 0, pairs - 2),
                spread(bits - 2, 0, pairs - 2),
                (pairs - 2,),
                (1, pairs - 3, pairs - 1),
                (1, pairs - 3, pairs - 1),
                (1, pairs - 2),
            ],
            3,
        ),
        others=all_labels if in_core else (),
    )
    even_labels, odd_labels = rest_labels, rest_labels + ("text",)
    if in_core:
        part_even = part_even.reshape(rest_dims + (even_pairs, up_share, piece))
        part_odd = part_odd.reshape(rest_dims + (2, pairs // 2, up_share // 2, piece))
    else:
        by_pair = part_even.reshape((pairs,) + frame_dims + (up_share, piece))
        part_even = jnp.moveaxis(by_pair[0::2], 0, bits)
        part_odd = by_pair[1::2].reshape(
            (pairs // 2,) + frame_dims + (2, up_share // 2, piece)
        )
        part_even, part_odd = run(
            idle_kernel,
            "reduce_core",
            1,
            (),
            (),
            [],
            [],
            [],
            [],
            0,
            (
                [part_even, jnp.moveaxis(part_odd, 0, bits + 1)],
                [
                    (frame_labels, [("split", 0)]),
                    (frame_labels + ("text",), [("split", 0)]),
                ],
                [(0,), (0,)],
                7,
            ),
        )
    operands = (
        grad_q,
        grad_k,
        grad_v,
        frames,
        grad_after_a,
        code_column,
        code_row,
        mod,
        w_qkv,
        sums_b,
        sums_c,
        embedding_rows,
        w_mod,
    )
    mod_columns = 8 * width
    time_rows = shape_of((8, width), jnp.float32)
    last_block = blocks - 1
    steps = blocks + 8
    late = steps - 1

    def early(array):
        return pl.BlockSpec(
            (ROW_BLOCK, array.shape[1]), lambda step: (jnp.minimum(step, last_block), 0)
        )

    (
        wide_grad,
        _,
        time_grad,
        table_a,
        sum_even,
        sum_odd,
        sum_kv,
        sum_q_cross,
        sum_out_cross,
        sum_out,
        partner_text_grad,
    ) = run(
        leave_kernel,
        "leave",
        steps,
        (),
        operands,
        [early(array) for array in operands[:6]]
        + [pl.BlockSpec((1, ROW_BLOCK), lambda step: (0, jnp.minimum(step, last_block)))]
        + [whole(array) for array in operands[7:12]]
        + [pl.BlockSpec((width, width), lambda step: (0, jnp.maximum(step - blocks, 0)))],
        [wide_shape, table_a_shape, time_rows],
        [pl.BlockSpec(memory_space=pl.ANY), whole(table_a_shape), whole(time_rows)],
        [
            pltpu.VMEM((2, 8, width), jnp.float32),
            pltpu.VMEM((8, 8, width), low_type),
            pltpu.VMEM((8, width), jnp.float32),
            wide_scratch,
            pltpu.SemaphoreType.DMA((1,)),
        ],
        4 * matmul_flops,
        (
            [1, part_even, part_odd, part_kv, part_q_cross, part_out_cross, part_out, sent_text_grad],
            [
                (None, gather_hops),
                (even_labels, low_bits + [("full", "text")]),
                (odd_labels, [("split", "text")] + low_bits + [("gather", "text")]),
                (("pair",) + rest_labels[:-1], low_bits[1:] + [("gather", "text")]),
                (rest_labels[:-1], low_bits[1:] + [("gather", "text")]),
                (rest_labels[:-1], low_bits[1:] + [("gather", "text")]),
                (
                    rest_labels[:-1] + ("text",),
                    [("split", "text")] + low_bits[1:] + [("gather", "text")],
                ),
                ((), [("swap", "text")]),
            ],
            [
                spread(bits + 1, blocks + 2, late),
                (blocks + 1,) + spread(bits - 1, blocks + 4, late),
                (blocks + 1,) + spread(bits, blocks + 4, late),
                spread(bits - 1, last_block - 2, late),
                spread(bits - 1, last_block - 2, late),
                spread(bits - 1, last_block - 2, late),
                spread(bits, last_block, late),
                (late,),
            ],
            4,
            (last_block,) + (0,) * 6 + (blocks + 1,),
        ),
    )
    text_pair = item_count // 2
    text_shape = shape_of((2 * item_count,) + half_text[1:], jnp.float32)

    def text_spec(turn):
        return pl.BlockSpec(
            (text_pair,) + half_text[1:],
            (lambda step, *_: (lax.rem(step, 2), 0, 0)) if turn else (lambda step, *_: (step, 0, 0)),
        )

    operands = (
        wide_grad,
        own_text_grad,
        partner_text_grad,
        table_a.reshape(-1, width),
        table_b.reshape(-1, table_b.shape[-1]),
        table_c.reshape(-1, table_c.shape[-1]),
        sum_w_up.reshape(2, chunks, up_share // 2, chunk),
        sum_even,
        sum_odd,
        sum_kv,
        sum_out.reshape(out_rows, width),
        time_grad,
    )
    mod_shape = shape_of((up_share, mod_columns), jnp.float32)
    b_mod_shape = shape_of((mod_columns // share_count,), jnp.float32)
    sum_up_shape = shape_of((up_share, hidden_width), jnp.float32)
    sum_qkv_shape = shape_of((up_share, 3 * width), jnp.float32)
    sum_kv_shape = shape_of((up_share, 2 * width), jnp.float32)
    sum_out_shape = shape_of((up_share, width), jnp.float32)
    biases_shape = [
        shape_of((size,), jnp.float32) for size in (up_share, up_share, down_share, up_share)
    ]
    time_shape = shape_of((item_count, width), jnp.float32)
    more = [mod_shape, b_mod_shape, sum_up_shape, sum_qkv_shape, sum_kv_shape]
    more += [sum_out_shape] + biases_shape + [time_shape]
    (
        frames_grad,
        text_grad,
        grad_w_mod,
        grad_b_mod,
        sum_w_up,
        sum_qkv,
        sum_kv,
        sum_out,
        *bias_cuts,
        time_grad,
    ) = run(
        finish_kernel,
        "finish",
        4,
        (start_scalar, side_scalar, spot.reshape(1), big_scalar),
        operands,
        [whole(wide_grad), text_spec(True), text_spec(True)] + [whole(a) for a in operands[3:]],
        [full_rows, text_shape] + more,
        [row_blocks(full_rows, row_count // 4), text_spec(False)] + [whole(a) for a in more],
        [pltpu.VMEM((1, mod_columns), jnp.float32)],
        0,
    )
    return (
        frames_out,
        frames_grad,
        text_grad,
        time_grad,
        grad_w_mod,
        grad_b_mod,
        sum_qkv,
        sum_out,
        bias_cuts[0],
        sum_q_cross.reshape(up_share, width),
        sum_kv,
        sum_out_cross.reshape(up_share, width),
        bias_cuts[1],
        sum_w_up,
        bias_cuts[2],
        sum_w_down.reshape(down_share, width),
        bias_cuts[3],
    )


def solution(mesh):
    in_specs = (
        P(("frames", "text"), None),
        P("frames", None),
        P("frames", "text", None),
        P("frames"),
        P(("frames", "text"), None),
        P(("frames", "text"), None),
    ) + (P(),) * 13
    out_specs = (
        P(("frames", "text"), None),
        P(("frames", "text"), None),
        P("frames", "text", None),
        P(("frames", "text"), None),
        P("frames", None),
        P("frames"),
        P("frames", None),
        P("frames", None),
        P("frames"),
        P("frames", None),
        P("frames", None),
        P("frames", None),
        P("frames"),
        P("frames", None),
        P("frames"),
        P("frames", None),
        P("frames"),
    )
    return jax.shard_map(
        on_device, mesh=mesh, in_specs=in_specs, out_specs=out_specs, check_vma=False
    )
```
